32 devices in a mesh: gx: 4 (over z), gy: 4 (over x, core), gz: 2 (over y).
Axes of the slice: x: 2, y: 2, z: 4, core: 2. Of those that a mesh axis runs over, the one named last changes fastest.
Arguments:
- pop_flow: float32 [19, 8, 64, 512], P(None, 'gz', 'gx', 'gy'), may hold values from 0.01 to 0.5, as said below
- pop_therm: float32 [7, 8, 64, 512], P(None, 'gz', 'gx', 'gy'), may hold values from 0.04 to 0.6, as said below
- flags: int32 [8, 64, 512], P('gz', 'gx', 'gy'), may hold values from 0 to 3, as said below
- nozzle_id: int32 [64, 512], P('gx', 'gy'), may hold values from 0 to 63
- jet_velocity: float32 [3, 64], replicated, may hold values from -0.2 to 0.2
- cot_flow: float32 [19, 8, 64, 512], P(None, 'gz', 'gx', 'gy'), may hold values from -6 to 6
- cot_therm: float32 [7, 8, 64, 512], P(None, 'gz', 'gx', 'gy'), may hold values from -6 to 6
- cot_plate: float32 [20, 64, 512], P('gz', 'gx', 'gy'), may hold values from -6 to 6
Outputs:
- grad_flow: float32 [19, 8, 64, 512], P(None, 'gz', 'gx', 'gy')
- grad_therm: float32 [7, 8, 64, 512], P(None, 'gz', 'gx', 'gy')
- grad_plate: float32 [20, 64, 512], P('gz', 'gx', 'gy')
The draws below stay inside these ranges and needn't reach their ends.
Inputs may be any that keep to these rules, and one draw needn't show every extreme that they name: `flags`: cells of the top layer are nozzle inlets (2) or walls (1); the other cells on the four side faces are outlets (3); all other cells are fluid (0) or wall (1), with no walls on the layer z = 0. `pop_flow`: every population is positive. `pop_therm`: every population is positive.
All inputs are finite; a program needn't handle non-finite values.
Results may differ from the reference program's by a relative error of at most 0.0003.
Values sent between devices are 32-bit elements; how exact they have to be, the bound alone decides.
No kernel may reach another device: no remote copies, remote signals or barrier semaphores. Data moves between devices by JAX's collectives and lax.ppermute only.
A program may use at most 64 MiB of HBM per device.

```python
import math
import jax
import jax.numpy as jnp
from jax import lax

NOZ = 64
NX = 64
NY = 512
NZ = 8
PLATE = 20


WEIGHTS_FLOW = (1.0 / 3.0,) + (1.0 / 18.0,) * 6 + (1.0 / 36.0,) * 12


WEIGHTS_HEAT = (0.25,) + (0.125,) * 6


def draw_pop_flow(key, part):
    weights = jnp.array(WEIGHTS_FLOW, jnp.float32)
    factor = jax.random.uniform(key, (19, NZ, NX, NY), jnp.float32, 0.6, 1.4)
    return weights[:, None, None, None] * factor


def draw_pop_therm(key, part):
    first, second = jax.random.split(key)
    weights = jnp.array(WEIGHTS_HEAT, jnp.float32)
    temper = jnp.exp(jax.random.uniform(first, (1, NZ, NX, NY), jnp.float32, math.log(0.5), math.log(2.0)))
    factor = jax.random.uniform(second, (7, NZ, NX, NY), jnp.float32, 0.8, 1.2)
    return weights[:, None, None, None] * temper * factor


def draw_flags(key, part):
    first, second = jax.random.split(key)
    shape = (NZ, NX, NY)
    height = lax.broadcasted_iota(jnp.int32, shape, 0)
    across = lax.broadcasted_iota(jnp.int32, shape, 1)
    along = lax.broadcasted_iota(jnp.int32, shape, 2)
    holes = jax.random.randint(first, shape, 0, 4)
    blocks = jax.random.randint(second, shape, 0, 32)
    top = height == NZ - 1
    side = (across == 0) | (across == NX - 1) | (along == 0) | (along == NY - 1)
    inner = jnp.where((blocks == 0) & (height > 0), 1, 0)
    return jnp.where(top, jnp.where(holes == 0, 2, 1), jnp.where(side, 3, inner)).astype(jnp.int32)


def plant(result, rng, least, high):
    index_at = [jax.random.randint(jax.random.fold_in(rng, axis), (), 0, length) for axis, length in enumerate(result.shape)]
    main_axis = result.shape.index(max(result.shape))
    neighbour = index_at[:main_axis] + [(index_at[main_axis] + 1) % result.shape[main_axis]] + index_at[main_axis + 1:]
    return result.at[tuple(index_at)].set(least).at[tuple(neighbour)].set(high)


def level_of(own_key, extent, cuts, least, top_value):
    def one(axis_at, shards_of):
        steps = jax.random.uniform(jax.random.fold_in(jax.random.fold_in(own_key, 6), axis_at), (shards_of,), jnp.float32, least / len(cuts), top_value / len(cuts))
        return jnp.repeat(jnp.exp(steps), extent[axis_at] // shards_of).reshape((-1,) + (1,) * (len(extent) - axis_at - 1))

    factor_of = one(*cuts[0])
    for cut in cuts[1:]:
        factor_of = factor_of * one(*cut)
    return factor_of


def gaussian(stream_key, shape, scale, bound, cuts=(), kind=jnp.bfloat16):
    drawn = jax.random.normal(stream_key, shape, jnp.float32) * scale
    if len(cuts) > 0:
        drawn = level_of(stream_key, shape, cuts, -0.22, 0.18) * drawn
    return jnp.clip(drawn, min=-bound, max=bound).astype(kind)


def setup_inputs(seed: int = 0) -> dict:
    key_list = jax.random.split(jax.random.key(seed), 9)
    pop_flow = draw_pop_flow(jax.random.fold_in(key_list[8], 71), 0)
    pop_therm = draw_pop_therm(jax.random.fold_in(key_list[8], 71), 0)
    flags = draw_flags(jax.random.fold_in(key_list[8], 71), 0)
    nozzle_id = plant(jax.random.randint(key_list[3], (NX, NY), 0, NOZ), jax.random.fold_in(key_list[3], 1), 0, NOZ - 1).astype(jnp.int32)
    jet_velocity = jnp.clip(jax.random.uniform(key_list[4], (3, NOZ), jnp.float32, -0.2, 0.2), -0.2, 0.2)
    cot_flow = gaussian(key_list[5], (19, NZ, NX, NY), 1.0, 6.0, ((1, 2), (2, 4), (3, 4)), jnp.float32)
    cot_therm = gaussian(key_list[6], (7, NZ, NX, NY), 1.0, 6.0, ((1, 2), (2, 4), (3, 4)), jnp.float32)
    cot_plate = gaussian(key_list[7], (PLATE, NX, NY), 1.0, 6.0, ((0, 2), (1, 4), (2, 4)), jnp.float32)
    return {"pop_flow": pop_flow, "pop_therm": pop_therm, "flags": flags, "nozzle_id": nozzle_id, "jet_velocity": jet_velocity, "cot_flow": cot_flow, "cot_therm": cot_therm, "cot_plate": cot_plate}


VELOCITY = ((0, 0, 0), (1, 0, 0), (-1, 0, 0), (0, 1, 0), (0, -1, 0), (0, 0, 1), (0, 0, -1), (1, 1, 0), (-1, -1, 0), (1, -1, 0), (-1, 1, 0), (1, 0, 1), (-1, 0, -1), (1, 0, -1), (-1, 0, 1), (0, 1, 1), (0, -1, -1), (0, 1, -1), (0, -1, 1))
OPPOSITE = tuple((VELOCITY.index((-a, -b, -c)) for a, b, c in VELOCITY))
WEIGHTS_FLOW = (1.0 / 3.0,) + (1.0 / 18.0,) * 6 + (1.0 / 36.0,) * 12
WEIGHTS_HEAT = (0.25,) + (0.125,) * 6
tau_flow = 0.8
tau_heat = 0.9
diffusion = 0.12
coupling = 0.3
jet_heat = 0.4

def moment(pops, component):
    total = jnp.zeros_like(pops[0])
    for q in range(pops.shape[0]):
        sign = VELOCITY[q][component]
        if sign != 0:
            total = total + sign * pops[q]
    return total

def flow_equilibrium(density, vel_x, vel_y, vel_z):
    speed_sq = vel_x * vel_x + vel_y * vel_y + vel_z * vel_z
    terms = []
    for weight, (cx, cy, cz) in zip(WEIGHTS_FLOW, VELOCITY):
        along = cx * vel_x + cy * vel_y + cz * vel_z
        terms.append(weight * density * (1.0 + 3.0 * along + 4.5 * along * along - 1.5 * speed_sq))
    return jnp.stack(terms)

def heat_equilibrium(temper, vel_x, vel_y, vel_z):
    terms = []
    for weight, (cx, cy, cz) in zip(WEIGHTS_HEAT, VELOCITY[:7]):
        along = cx * vel_x + cy * vel_y + cz * vel_z
        terms.append(weight * temper * (1.0 + 4.0 * along))
    return jnp.stack(terms)

def collide(flow, heat, flags, jet):
    density = lax.optimization_barrier(jnp.sum(flow, axis=0))
    vel_x = moment(flow, 0) / density
    vel_y = moment(flow, 1) / density
    vel_z = moment(flow, 2) / density
    temper = lax.optimization_barrier(jnp.sum(heat, axis=0))
    relaxed_flow = flow - (flow - flow_equilibrium(density, vel_x, vel_y, vel_z)) / tau_flow
    relaxed_heat = heat - (heat - heat_equilibrium(temper, vel_x, vel_y, vel_z)) / tau_heat
    bounced_flow = jnp.stack([flow[o] for o in OPPOSITE])
    bounced_heat = jnp.stack([heat[o] for o in OPPOSITE[:7]])
    inlet_flow = flow_equilibrium(density, jet[0], jet[1], jet[2])
    inlet_heat = heat_equilibrium(jet_heat * jnp.ones_like(temper), jet[0], jet[1], jet[2])
    wall = (flags == 1)[None]
    inlet = (flags == 2)[None]
    out_flow = jnp.where(wall, bounced_flow, jnp.where(inlet, inlet_flow, relaxed_flow))
    out_heat = jnp.where(wall, bounced_heat, jnp.where(inlet, inlet_heat, relaxed_heat))
    return (out_flow, out_heat)

def lookup(nozzle_id, jet_velocity):
    labels = jnp.arange(jet_velocity.shape[1], dtype=jnp.int32)
    match = nozzle_id[None] == labels[:, None, None]
    return lax.optimization_barrier(jnp.sum(jnp.where(match[None], jet_velocity[:, :, None, None], 0.0), axis=1))

def pull_back(field, count):
    size_z, size_x, size_y = field.shape[1:]
    rows = []
    for q in range(count):
        cx, cy, cz = VELOCITY[q]
        padded = jnp.pad(field[q], 1)
        rows.append(padded[1 + cz:1 + cz + size_z, 1 + cx:1 + cx + size_x, 1 + cy:1 + cy + size_y])
    return jnp.stack(rows)

def reference(pop_flow, pop_therm, flags, nozzle_id, jet_velocity, cot_flow, cot_therm, cot_plate):
    jet = lookup(nozzle_id, jet_velocity)
    star_flow = pull_back(cot_flow, 19)
    for q in range(19):
        if VELOCITY[q][2] == -1:
            star_flow = star_flow.at[q, 0].add(cot_flow[OPPOSITE[q], 0])
    star_heat = pull_back(cot_therm, 7)
    star_heat = star_heat.at[6, 0].add(-cot_therm[5, 0])

    def layer(items):
        flow, heat, kinds, cflow, cheat = items
        _, back = jax.vjp(lambda f, h: collide(f, h, kinds, jet), flow, heat)
        return back((cflow, cheat))
    grad_flow, grad_heat = lax.map(layer, (jnp.transpose(pop_flow, (1, 0, 2, 3)), jnp.transpose(pop_therm, (1, 0, 2, 3)), flags, jnp.transpose(star_flow, (1, 0, 2, 3)), jnp.transpose(star_heat, (1, 0, 2, 3))))
    grad_flow = jnp.transpose(grad_flow, (1, 0, 2, 3))
    grad_heat = jnp.transpose(grad_heat, (1, 0, 2, 3))
    grad_heat = grad_heat.at[:, 0].add(coupling * cot_plate[0][None])
    padded = jnp.pad(cot_plate, 1)
    beside_all = padded[2:, 1:-1, 1:-1] + padded[:-2, 1:-1, 1:-1]
    beside_all = beside_all + padded[1:-1, 2:, 1:-1] + padded[1:-1, :-2, 1:-1]
    beside_all = beside_all + padded[1:-1, 1:-1, 2:] + padded[1:-1, 1:-1, :-2]
    grad_plate = cot_plate + diffusion * (beside_all - 6.0 * cot_plate)
    grad_plate = grad_plate.at[0].add(-coupling * cot_plate[0] + 0.25 * cot_therm[5, 0])
    return (grad_flow, grad_heat, grad_plate)
```

```python
import functools

import jax
import jax.numpy as jnp
from jax import lax
from jax.experimental import pallas as pl
from jax.experimental.pallas import tpu as pltpu
from jax.sharding import PartitionSpec as P

VELOCITY = (
    (0, 0, 0),
    (1, 0, 0),
    (-1, 0, 0),
    (0, 1, 0),
    (0, -1, 0),
    (0, 0, 1),
    (0, 0, -1),
    (1, 1, 0),
    (-1, -1, 0),
    (1, -1, 0),
    (-1, 1, 0),
    (1, 0, 1),
    (-1, 0, -1),
    (1, 0, -1),
    (-1, 0, 1),
    (0, 1, 1),
    (0, -1, -1),
    (0, 1, -1),
    (0, -1, 1),
)
OPPOSITE = tuple((VELOCITY.index((-a, -b, -c)) for a, b, c in VELOCITY))
WEIGHTS_FLOW = (1.0 / 3.0,) + (1.0 / 18.0,) * 6 + (1.0 / 36.0,) * 12
WEIGHTS_HEAT = (0.25,) + (0.125,) * 6
FLOW = 19
HEAT = 7
DIRECTIONS = VELOCITY + VELOCITY[:HEAT]
tau_flow = 0.8
tau_heat = 0.9
diffusion = 0.12
coupling = 0.3

AXES = ("gx", "gy", "gz")
COMPONENT = {"gx": 0, "gy": 1, "gz": 2}
VMEM_LIMIT = 8 << 20


def moving(component, sign):
    return [k for k, c in enumerate(DIRECTIONS) if c[component] == sign]


XP, XM = moving(0, 1), moving(0, -1)
YP, YM = moving(1, 1), moving(1, -1)
ZP, ZM = moving(2, 1), moving(2, -1)
XZP = [k for k in ZP if DIRECTIONS[k][0] != 0]
XZM = [k for k in ZM if DIRECTIONS[k][0] != 0]


def rounds(size):
    return 1 if size == 2 else 2


def swap(value, axis, turn):
    sizes = [lax.axis_size(name) for name in AXES]
    at = AXES.index(axis)
    pairs = []
    for a in range(sizes[0]):
        for b in range(sizes[1]):
            for c in range(sizes[2]):
                here = [a, b, c]
                there = [a, b, c]
                i = here[at]
                j = i ^ 1 if turn == 0 else (i + 1 if i % 2 else i - 1)
                if 0 <= j < sizes[at]:
                    there[at] = j
                elif axis == "gy":
                    there[at] = sizes[at] - 1 - i
                else:
                    there[1] = b ^ 1
                flat = lambda p: (p[0] * sizes[1] + p[1]) * sizes[2] + p[2]
                pairs.append((flat(here), flat(there)))
    return lax.ppermute(value, AXES, pairs)


def place(axis):
    i = lax.axis_index(axis)
    return lax.rem(i, 2) == 0, i < lax.axis_size(axis) - 1, i > 0


def outgoing(axis, turn, to_higher, to_lower):
    even, _, _ = place(axis)
    return jnp.where(even, to_higher, to_lower) if turn == 0 else jnp.where(even, to_lower, to_higher)


def incoming(axis, turns):
    even, higher, lower = place(axis)
    first, last = turns[0], turns[-1]
    zero = jnp.zeros_like(first)
    above = jnp.where(higher, jnp.where(even, first, last), zero)
    below = jnp.where(lower, jnp.where(even, last, first), zero)
    return above, below


def slab(cot_flow, cot_heat, k, z):
    return cot_flow[k, z] if k < FLOW else cot_heat[k - FLOW, z]


def row_of(cot_flow, cot_heat, k, z, x):
    return cot_flow[k, z, x : x + 1, :] if k < FLOW else cot_heat[k - FLOW, z, x : x + 1, :]


def padded(rows):
    return -(-rows // 8) * 8


def pack_faces(nzt, nxt, cot_flow, cot_heat, cot_plate, *outs):
    depth, width = cot_flow.shape[1], cot_flow.shape[2]
    layers = cot_plate.shape[0]
    for turn in range(nzt):
        out = outs[turn]
        for n, (hi, lo) in enumerate(zip(ZM, ZP)):
            out[n * width : (n + 1) * width, :] = outgoing(
                "gz", turn, slab(cot_flow, cot_heat, hi, depth - 1), slab(cot_flow, cot_heat, lo, 0)
            )
        n = len(ZM)
        out[n * width : (n + 1) * width, :] = outgoing("gz", turn, cot_plate[layers - 1], cot_plate[0])
    for turn in range(nxt):
        out = outs[nzt + turn]
        for n, (hi, lo) in enumerate(zip(XM, XP)):
            for z in range(depth):
                r = n * depth + z
                out[r : r + 1, :] = outgoing(
                    "gx",
                    turn,
                    row_of(cot_flow, cot_heat, hi, z, width - 1),
                    row_of(cot_flow, cot_heat, lo, z, 0),
                )
        for l in range(layers):
            r = len(XM) * depth + l
            out[r : r + 1, :] = outgoing(
                "gx", turn, cot_plate[l, width - 1 : width, :], cot_plate[l, 0:1, :]
            )


class Halo:
    def __init__(self, cot_flow, cot_heat, z_in, x_in, xz_in):
        self.flow, self.heat = cot_flow, cot_heat
        self.depth, self.width = cot_flow.shape[1], cot_flow.shape[2]
        self.z_in, self.x_in, self.xz_in = z_in, x_in, xz_in

    def face(self, k, n=None):
        up = n is not None and n > 0 or (n is None and DIRECTIONS[k][2] == 1)
        at = (ZP if up else ZM).index(k) if n is None else len(ZP)
        rows = slice(at * self.width, (at + 1) * self.width)
        above, below = incoming("gz", [r[rows, :] for r in self.z_in])
        return above if up else below

    def row(self, k, z):
        up = DIRECTIONS[k][0] == 1
        if 0 <= z < self.depth:
            at = (XP if up else XM).index(k) * self.depth + z
            above, below = incoming("gx", [r[at : at + 1, :] for r in self.x_in])
            return above if up else below
        from_above = z >= self.depth
        at = (XZP if from_above else XZM).index(k)
        above, below = incoming("gz", [r[at : at + 1, :] for r in self.xz_in])
        return above if from_above else below

    def shifted(self, k, z):
        cx, _, cz = DIRECTIONS[k]
        at = z + cz
        plane = slab(self.flow, self.heat, k, at) if 0 <= at < self.depth else self.face(k)
        if cx == 0:
            return plane
        return shift_rows(plane, cx, self.row(k, at))


def shift_rows(plane, sign, halo_row):
    width = plane.shape[0]
    x = lax.broadcasted_iota(jnp.int32, plane.shape, 0)
    if sign == 1:
        return jnp.where(x == width - 1, halo_row, pltpu.roll(plane, width - 1, 0))
    return jnp.where(x == 0, halo_row, pltpu.roll(plane, 1, 0))


def shift_lanes(plane, sign, halo, lane):
    length = plane.shape[1]
    y = lax.broadcasted_iota(jnp.int32, plane.shape, 1)
    edge = length - 1 if sign == 1 else 0
    turn = (edge - lane) % length
    column = pltpu.roll(halo, turn, 1) if turn else halo
    return jnp.where(y == edge, column, pltpu.roll(plane, length - 1 if sign == 1 else 1, 1))


def pack_edges(nzt, nxt, nyt, cot_flow, cot_heat, cot_plate, *refs):
    z_in, x_in = refs[:nzt], refs[nzt : nzt + nxt]
    outs = refs[nzt + nxt :]
    halo = Halo(cot_flow, cot_heat, z_in, x_in, None)
    depth, width = halo.depth, halo.width
    length = cot_flow.shape[3]
    layers = cot_plate.shape[0]
    y = lax.broadcasted_iota(jnp.int32, (width, length), 1)

    def put(packed, plane, source, lane):
        turn = (lane - source) % length
        return jnp.where(y == lane, pltpu.roll(plane, turn, 1) if turn else plane, packed)

    packs = []
    for side, source in ((YM, length - 1), (YP, 0)):
        packed = jnp.zeros((width, length), jnp.float32)
        for n, k in enumerate(side):
            for z in range(depth):
                packed = put(packed, halo.shifted(k, z), source, n * depth + z)
        for l in range(layers):
            packed = put(packed, cot_plate[l], source, len(side) * depth + l)
        packs.append(packed)
    for turn in range(nyt):
        outs[turn][...] = outgoing("gy", turn, packs[0], packs[1])
    for turn in range(nzt):
        out = outs[nyt + turn]
        out[...] = jnp.zeros_like(out)
        for n, (hi, lo) in enumerate(zip(XZM, XZP)):
            out[n : n + 1, :] = outgoing("gz", turn, halo.row(hi, depth - 1), halo.row(lo, 0))


def prepare(pop_flow, pop_heat, flags, nozzle, jet_velocity, ue_out, ratio_out):
    jets = [jnp.zeros(nozzle.shape, jnp.float32)] * 3
    which = nozzle[...]
    for n in range(jet_velocity.shape[1]):
        hit = which == n
        jets = [jnp.where(hit, jet_velocity[c, n], jets[c]) for c in range(3)]
    for z in range(pop_flow.shape[1]):
        inlet = flags[z] == 2
        pops = [pop_flow[q, z] for q in range(FLOW)]
        rho = sum(pops[1:], pops[0])
        inverse = 1.0 / rho
        for c in range(3):
            plus = [pops[q] for q in range(FLOW) if VELOCITY[q][c] == 1]
            minus = [pops[q] for q in range(FLOW) if VELOCITY[q][c] == -1]
            total = sum(plus[1:], plus[0]) - sum(minus[1:], minus[0])
            ue_out[c, z] = jnp.where(inlet, jets[c], total * inverse)
        heat = [pop_heat[q, z] for q in range(HEAT)]
        ratio_out[z] = sum(heat[1:], heat[0]) * inverse


def finish(nzt, nxt, nyt, flags, ue_in, ratio_in, cot_flow, cot_heat, cot_plate, *refs):
    z_in, refs = refs[:nzt], refs[nzt:]
    x_in, refs = refs[:nxt], refs[nxt:]
    y_in, refs = refs[:nyt], refs[nyt:]
    xz_in, (grad_flow, grad_heat, grad_plate) = refs[:nzt], refs[nzt:]
    halo = Halo(cot_flow, cot_heat, z_in, x_in, xz_in)
    depth, width = halo.depth, halo.width
    layers = cot_plate.shape[0]
    y_above, y_below = incoming("gy", [r[...] for r in y_in])
    base = lax.axis_index("gz") == 0

    for z in range(depth):
        star = []
        for k, (cx, cy, cz) in enumerate(DIRECTIONS):
            plane = halo.shifted(k, z)
            if cy == 1:
                plane = shift_lanes(plane, 1, y_above, YP.index(k) * depth + z)
            elif cy == -1:
                plane = shift_lanes(plane, -1, y_below, YM.index(k) * depth + z)
            if cz == -1 and z == 0:
                if k < FLOW:
                    bounced = cot_flow[OPPOSITE[k], 0]
                else:
                    bounced = -cot_heat[OPPOSITE[k - FLOW], 0]
                plane = jnp.where(base, bounced, plane)
            star.append(plane)
        kind = flags[z]
        wall, inlet = kind == 1, kind == 2
        ue = [ue_in[c, z] for c in range(3)]
        ratio = ratio_in[z]
        s, t = star[:FLOW], star[FLOW:]

        zero_moment = WEIGHTS_FLOW[0] * s[0]
        first = [None] * 3
        second = {}
        add = lambda a, b: b if a is None else a + b
        pair_sum = None
        for group, weight in ((range(1, 7), WEIGHTS_FLOW[1]), (range(7, 19), WEIGHTS_FLOW[7])):
            odd = [None] * 3
            even = {}
            total = None
            for q in group:
                o = OPPOSITE[q]
                if o < q:
                    continue
                c = VELOCITY[q]
                plus, minus = s[q] + s[o], s[q] - s[o]
                total = add(total, plus)
                for i in range(3):
                    if c[i]:
                        odd[i] = add(odd[i], minus if c[i] == 1 else -minus)
                    for j in range(i, 3):
                        if c[i] * c[j]:
                            even[i, j] = add(even.get((i, j)), plus if c[i] * c[j] == 1 else -plus)
            zero_moment = zero_moment + weight * total
            for i in range(3):
                first[i] = add(first[i], weight * odd[i])
            for key, value in even.items():
                second[key] = add(second.get(key), weight * value)
        heat_first = [WEIGHTS_HEAT[1] * (t[2 * c + 1] - t[2 * c + 2]) for c in range(3)]
        heat_zero = WEIGHTS_HEAT[0] * t[0] + WEIGHTS_HEAT[1] * (
            (t[1] + t[2]) + (t[3] + t[4]) + (t[5] + t[6])
        )

        bent = [
            sum(second[min(i, j), max(i, j)] * ue[j] for j in range(3)) for i in range(3)
        ]
        dot = lambda a, b: a[0] * b[0] + a[1] * b[1] + a[2] * b[2]
        speed = dot(ue, ue)
        gain = zero_moment * (1.0 - 1.5 * speed) + 3.0 * dot(first, ue) + 4.5 * dot(bent, ue)
        pull = [
            (3.0 / tau_flow) * (first[i] + 3.0 * bent[i] - ue[i] * zero_moment)
            + (4.0 / tau_heat) * ratio * heat_first[i]
            for i in range(3)
        ]
        common = jnp.where(inlet, gain, (1.0 / tau_flow) * gain - dot(ue, pull))
        pull = [jnp.where(inlet, 0.0, p) for p in pull]
        keep = jnp.where(inlet, 0.0, 1.0 - 1.0 / tau_flow)
        for q in range(FLOW):
            o = OPPOSITE[q]
            value = keep * s[q] + common
            for i in range(3):
                if VELOCITY[q][i] == 1:
                    value = value + pull[i]
                elif VELOCITY[q][i] == -1:
                    value = value - pull[i]
            grad_flow[q, z] = jnp.where(wall, s[o], value)
        heat_common = jnp.where(
            inlet, 0.0, (1.0 / tau_heat) * (heat_zero + 4.0 * dot(heat_first, ue))
        )
        heat_keep = jnp.where(inlet, 0.0, 1.0 - 1.0 / tau_heat)
        for q in range(HEAT):
            value = jnp.where(wall, t[OPPOSITE[q]], heat_keep * t[q] + heat_common)
            if z == 0:
                value = value + jnp.where(base, coupling * cot_plate[0], 0.0)
            grad_heat[q, z] = value

    x_above, x_below = incoming("gx", [r[...] for r in x_in])
    z_rows = slice(len(ZP) * width, (len(ZP) + 1) * width)
    z_above, z_below = incoming("gz", [r[z_rows, :] for r in z_in])
    for l in range(layers):
        own = cot_plate[l]
        up = cot_plate[l + 1] if l + 1 < layers else z_above
        down = cot_plate[l - 1] if l > 0 else z_below
        r = len(XP) * depth + l
        total = up + down
        total = total + shift_rows(own, 1, x_above[r : r + 1, :])
        total = total + shift_rows(own, -1, x_below[r : r + 1, :])
        total = total + shift_lanes(own, 1, y_above, len(YP) * depth + l)
        total = total + shift_lanes(own, -1, y_below, len(YM) * depth + l)
        value = own + diffusion * (total - 6.0 * own)
        if l == 0:
            value = value + jnp.where(base, 0.25 * cot_heat[5, 0] - coupling * own, 0.0)
        grad_plate[l] = value


def kernel_call(body, shapes, count, smem=(), name=None):
    specs = [
        pl.BlockSpec(memory_space=pltpu.SMEM if i in smem else pltpu.VMEM) for i in range(count)
    ]
    return pl.pallas_call(
        body,
        out_shape=[jax.ShapeDtypeStruct(s, jnp.float32) for s in shapes],
        in_specs=specs,
        out_specs=[pl.BlockSpec(memory_space=pltpu.VMEM)] * len(shapes),
        compiler_params=pltpu.CompilerParams(vmem_limit_bytes=VMEM_LIMIT),
        name=name,
    )


def local(pop_flow, pop_heat, flags, nozzle_id, jet_velocity, cot_flow, cot_heat, cot_plate):
    nxt, nyt, nzt = (rounds(lax.axis_size(a)) for a in AXES)
    _, depth, width, length = cot_flow.shape
    layers = cot_plate.shape[0]
    cots = (cot_flow, cot_heat, cot_plate)
    face = ((len(ZM) + 1) * width, length)
    side = (padded(len(XM) * depth + layers), length)
    sends = kernel_call(
        functools.partial(pack_faces, nzt, nxt), [face] * nzt + [side] * nxt, 3, name="faces"
    )(*cots)
    z_in = [swap(sends[t], "gz", t) for t in range(nzt)]
    x_in = [swap(sends[nzt + t], "gx", t) for t in range(nxt)]
    ue, ratio = kernel_call(
        prepare, [(3, depth, width, length), (depth, width, length)], 5, (4,), name="prepare"
    )(pop_flow, pop_heat, flags, nozzle_id, jet_velocity)
    sends = kernel_call(
        functools.partial(pack_edges, nzt, nxt, nyt),
        [(width, length)] * nyt + [(8, length)] * nzt,
        3 + nzt + nxt,
        name="edges",
    )(*cots, *z_in, *x_in)
    y_in = [swap(sends[t], "gy", t) for t in range(nyt)]
    xz_in = [swap(sends[nyt + t], "gz", t) for t in range(nzt)]
    return tuple(
        kernel_call(
            functools.partial(finish, nzt, nxt, nyt),
            [cot_flow.shape, cot_heat.shape, cot_plate.shape],
            6 + 2 * nzt + nxt + nyt,
            name="finish",
        )(flags, ue, ratio, *cots, *z_in, *x_in, *y_in, *xz_in)
    )


def solution(mesh):
    return jax.shard_map(
        local,
        mesh=mesh,
        in_specs=(
            P(None, "gz", "gx", "gy"),
            P(None, "gz", "gx", "gy"),
            P("gz", "gx", "gy"),
            P("gx", "gy"),
            P(),
            P(None, "gz", "gx", "gy"),
            P(None, "gz", "gx", "gy"),
            P("gz", "gx", "gy"),
        ),
        out_specs=(P(None, "gz", "gx", "gy"), P(None, "gz", "gx", "gy"), P("gz", "gx", "gy")),
        check_vma=False,
    )
```

```python
import functools

import jax
import jax.numpy as jnp
from jax import lax
from jax.experimental import pallas as pl
from jax.experimental.pallas import tpu as pltpu
from jax.sharding import PartitionSpec as P

VELOCITY = (
    (0, 0, 0),
    (1, 0, 0),
    (-1, 0, 0),
    (0, 1, 0),
    (0, -1, 0),
    (0, 0, 1),
    (0, 0, -1),
    (1, 1, 0),
    (-1, -1, 0),
    (1, -1, 0),
    (-1, 1, 0),
    (1, 0, 1),
    (-1, 0, -1),
    (1, 0, -1),
    (-1, 0, 1),
    (0, 1, 1),
    (0, -1, -1),
    (0, 1, -1),
    (0, -1, 1),
)
OPPOSITE = tuple((VELOCITY.index((-a, -b, -c)) for a, b, c in VELOCITY))
WEIGHTS_FLOW = (1.0 / 3.0,) + (1.0 / 18.0,) * 6 + (1.0 / 36.0,) * 12
WEIGHTS_HEAT = (0.25,) + (0.125,) * 6
FLOW = 19
HEAT = 7
DIRECTIONS = VELOCITY + VELOCITY[:HEAT]
tau_flow = 0.8
tau_heat = 0.9
diffusion = 0.12
coupling = 0.3

AXES = ("gx", "gy", "gz")
COMPONENT = {"gx": 0, "gy": 1, "gz": 2}
VMEM_LIMIT = 8 << 20
VMEM_FIRST = 8 << 20


def moving(component, sign):
    return [k for k, c in enumerate(DIRECTIONS) if c[component] == sign]


XP, XM = moving(0, 1), moving(0, -1)
YP, YM = moving(1, 1), moving(1, -1)
ZP, ZM = moving(2, 1), moving(2, -1)
XZP = [k for k in ZP if DIRECTIONS[k][0] != 0]
XZM = [k for k in ZM if DIRECTIONS[k][0] != 0]


def rounds(size):
    return 1 if size == 2 else 2


def swap(value, axis, turn):
    sizes = [lax.axis_size(name) for name in AXES]
    at = AXES.index(axis)
    pairs = []
    for a in range(sizes[0]):
        for b in range(sizes[1]):
            for c in range(sizes[2]):
                here = [a, b, c]
                there = [a, b, c]
                i = here[at]
                j = i ^ 1 if turn == 0 else (i + 1 if i % 2 else i - 1)
                if 0 <= j < sizes[at]:
                    there[at] = j
                elif axis == "gy":
                    there[at] = sizes[at] - 1 - i
                else:
                    there[1] = b ^ 1
                flat = lambda p: (p[0] * sizes[1] + p[1]) * sizes[2] + p[2]
                pairs.append((flat(here), flat(there)))
    return lax.ppermute(value, AXES, pairs)


def place(axis):
    i = lax.axis_index(axis)
    return lax.rem(i, 2) == 0, i < lax.axis_size(axis) - 1, i > 0


def outgoing(axis, turn, to_higher, to_lower):
    even, _, _ = place(axis)
    return jnp.where(even, to_higher, to_lower) if turn == 0 else jnp.where(even, to_lower, to_higher)


def incoming(axis, turns):
    even, higher, lower = place(axis)
    first, last = turns[0], turns[-1]
    zero = jnp.zeros_like(first)
    above = jnp.where(higher, jnp.where(even, first, last), zero)
    below = jnp.where(lower, jnp.where(even, last, first), zero)
    return above, below


def slab(cot_flow, cot_heat, k, z):
    return cot_flow[k, z] if k < FLOW else cot_heat[k - FLOW, z]


def padded(rows):
    return -(-rows // 8) * 8


def pack_first(nxt, nzt, cot_flow, cot_heat, cot_plate, *refs):
    x_outs, z_outs = refs[:nxt], refs[nxt : nxt + nzt]
    to_higher, to_lower, x_sems, plate_sems, z_sems = refs[nxt + nzt :]
    depth, width = cot_flow.shape[1], cot_flow.shape[2]
    layers = cot_plate.shape[0]
    copies = []

    def start(source, target, sem):
        copies.append(pltpu.make_async_copy(source, target, sem))
        copies[-1].start()

    for side, (rows, ks, x) in enumerate(((to_higher, XM, width - 1), (to_lower, XP, 0))):
        for n, k in enumerate(ks):
            ref = cot_flow.at[k] if k < FLOW else cot_heat.at[k - FLOW]
            start(ref.at[:, x, :], rows.at[n * depth : (n + 1) * depth, :], x_sems.at[side, n])
        n = len(ks) * depth
        start(cot_plate.at[:, x, :], rows.at[n : n + layers, :], plate_sems.at[side])
    even, _, _ = place("gz")
    for turn in range(nzt):
        up = even if turn == 0 else jnp.logical_not(even)
        z = jnp.where(up, depth - 1, 0)
        for n, (hi, lo) in enumerate(zip(ZM, ZP)):
            ref, skip = (cot_flow, 0) if hi < FLOW else (cot_heat, FLOW)
            k = jnp.where(up, hi - skip, lo - skip)
            start(ref.at[k, z], z_outs[turn].at[n * width : (n + 1) * width, :], z_sems.at[turn, n])
    for copy in copies:
        copy.wait()
    for turn in range(nxt):
        x_outs[turn][...] = outgoing("gx", turn, to_higher[...], to_lower[...])


def halo_row(x_in, k, z, depth):
    up = DIRECTIONS[k][0] == 1
    at = (XP if up else XM).index(k) * depth + z
    above, below = incoming("gx", [r[at : at + 1, :] for r in x_in])
    return above if up else below


class Halo:
    def __init__(self, cot_flow, cot_heat, x_in, z_in, rest_in=None):
        self.flow, self.heat = cot_flow, cot_heat
        self.depth, self.width = cot_flow.shape[1], cot_flow.shape[2]
        self.x_in, self.z_in, self.rest_in = x_in, z_in, rest_in

    def face(self, k):
        up = DIRECTIONS[k][2] == 1
        at = (ZP if up else ZM).index(k) * self.width
        above, below = incoming("gz", [r[at : at + self.width, :] for r in self.z_in])
        return above if up else below

    def row(self, k, z):
        if 0 <= z < self.depth:
            return halo_row(self.x_in, k, z, self.depth)
        from_above = z >= self.depth
        at = self.width + (XZP if from_above else XZM).index(k)
        above, below = incoming("gz", [r[at : at + 1, :] for r in self.rest_in])
        return above if from_above else below

    def shifted(self, k, z):
        cx, _, cz = DIRECTIONS[k]
        at = z + cz
        plane = slab(self.flow, self.heat, k, at) if 0 <= at < self.depth else self.face(k)
        if cx == 0:
            return plane
        return shift_rows(plane, cx, self.row(k, at))


def shift_rows(plane, sign, halo_row):
    width = plane.shape[0]
    x = lax.broadcasted_iota(jnp.int32, plane.shape, 0)
    if sign == 1:
        return jnp.where(x == width - 1, halo_row, pltpu.roll(plane, width - 1, 0))
    return jnp.where(x == 0, halo_row, pltpu.roll(plane, 1, 0))


def shift_lanes(plane, sign):
    length = plane.shape[1]
    y = lax.broadcasted_iota(jnp.int32, plane.shape, 1)
    if sign == 1:
        return jnp.where(y == length - 1, 0.0, pltpu.roll(plane, length - 1, 1))
    return jnp.where(y == 0, 0.0, pltpu.roll(plane, 1, 1))


def column_lane(n, z, depth):
    return 2 * (n * depth + z)


def plate_lane(l, depth):
    return column_lane(len(YM), 0, depth) + l


def turned(plane, by):
    by %= plane.shape[1]
    return pltpu.roll(plane, by, 1) if by else plane


def pack_rest(nxt, nzt, depth, cot_plate, *refs):
    x_in, outs = refs[:nxt], refs[-nzt:]
    layers, width = cot_plate.shape[:2]
    for turn in range(nzt):
        out = outs[turn]
        out[:width, :] = outgoing("gz", turn, cot_plate[layers - 1], cot_plate[0])
        out[width:, :] = jnp.zeros((out.shape[0] - width, out.shape[1]), jnp.float32)
        for n, (hi, lo) in enumerate(zip(XZM, XZP)):
            out[width + n : width + n + 1, :] = outgoing(
                "gz", turn, halo_row(x_in, hi, depth - 1, depth), halo_row(x_in, lo, 0, depth)
            )


def pack_columns(nxt, nyt, nzt, cot_flow, cot_heat, cot_plate, *refs):
    x_in, z_in = refs[:nxt], refs[nxt : nxt + nzt]
    outs = refs[-nyt:]
    halo = Halo(cot_flow, cot_heat, x_in, z_in)
    depth, width = halo.depth, halo.width
    length = cot_flow.shape[3]
    layers = cot_plate.shape[0]
    y = lax.broadcasted_iota(jnp.int32, (width, length), 1)

    def put(packed, plane, source, lane):
        return jnp.where(y == lane, turned(plane, lane - source), packed)

    packs = []
    for side, source in ((YM, length - 1), (YP, 0)):
        packed = jnp.zeros((width, length), jnp.float32)
        for n, k in enumerate(side):
            for z in range(depth):
                packed = put(packed, halo.shifted(k, z), source, column_lane(n, z, depth))
        for l in range(layers):
            packed = put(packed, cot_plate[l], source, plate_lane(l, depth))
        packs.append(packed)
    for turn in range(nyt):
        outs[turn][...] = outgoing("gy", turn, packs[0], packs[1])


def prepare(pop_flow, pop_heat, flags, nozzle, jet_velocity, *refs):
    ue_out, ratio_out, ends_out, kinds_out = refs[-4:]
    jets = [jnp.zeros(nozzle.shape, jnp.float32)] * 3
    which = nozzle[...]
    for n in range(jet_velocity.shape[1]):
        hit = which == n
        jets = [jnp.where(hit, jet_velocity[c, n], jets[c]) for c in range(3)]
    y = lax.broadcasted_iota(jnp.int32, nozzle.shape, 1)
    ends = [None] * 4
    kinds = None
    for z in range(pop_flow.shape[1]):
        kind = flags[z]
        inlet = kind == 2
        pops = [pop_flow[q, z] for q in range(FLOW)]
        rho = sum(pops[1:], pops[0])
        inverse = 1.0 / rho
        values = []
        for c in range(3):
            plus = [pops[q] for q in range(FLOW) if VELOCITY[q][c] == 1]
            minus = [pops[q] for q in range(FLOW) if VELOCITY[q][c] == -1]
            total = sum(plus[1:], plus[0]) - sum(minus[1:], minus[0])
            values.append(jnp.where(inlet, jets[c], total * inverse))
            ue_out[c, z] = values[c]
        heat = [pop_heat[q, z] for q in range(HEAT)]
        values.append(sum(heat[1:], heat[0]) * inverse)
        ratio_out[z] = values[3]
        if z == 0:
            ends, kinds = values, kind
        else:
            here = end_lanes(y, z)
            ends = [jnp.where(here, turned(v, 2 * z), e) for v, e in zip(values, ends)]
            kinds = jnp.where(here, turned(kind, 2 * z), kinds)
    for c in range(4):
        ends_out[c] = ends[c]
    kinds_out[...] = kinds


def end_lanes(y, z):
    return (y == 2 * z) | (y == (2 * z - 1) % y.shape[1])


def collide_back(s, t, ue, ratio, wall, inlet):
    add = lambda a, b: b if a is None else a + b
    zero_moment = WEIGHTS_FLOW[0] * s[0]
    first = [None] * 3
    second = {}
    for group, weight in ((range(1, 7), WEIGHTS_FLOW[1]), (range(7, 19), WEIGHTS_FLOW[7])):
        odd = [None] * 3
        even = {}
        total = None
        for q in group:
            o = OPPOSITE[q]
            if o < q:
                continue
            c = VELOCITY[q]
            plus, minus = s[q] + s[o], s[q] - s[o]
            total = add(total, plus)
            for i in range(3):
                if c[i]:
                    odd[i] = add(odd[i], minus if c[i] == 1 else -minus)
                for j in range(i, 3):
                    if c[i] * c[j]:
                        even[i, j] = add(even.get((i, j)), plus if c[i] * c[j] == 1 else -plus)
        zero_moment = zero_moment + weight * total
        for i in range(3):
            first[i] = add(first[i], weight * odd[i])
        for key, value in even.items():
            second[key] = add(second.get(key), weight * value)
    heat_first = [WEIGHTS_HEAT[1] * (t[2 * c + 1] - t[2 * c + 2]) for c in range(3)]
    heat_zero = WEIGHTS_HEAT[0] * t[0] + WEIGHTS_HEAT[1] * (
        (t[1] + t[2]) + (t[3] + t[4]) + (t[5] + t[6])
    )
    dot = lambda a, b: a[0] * b[0] + a[1] * b[1] + a[2] * b[2]
    bent = [sum(second[min(i, j), max(i, j)] * ue[j] for j in range(3)) for i in range(3)]
    gain = zero_moment * (1.0 - 1.5 * dot(ue, ue)) + 3.0 * dot(first, ue) + 4.5 * dot(bent, ue)
    pull = [
        (3.0 / tau_flow) * (first[i] + 3.0 * bent[i] - ue[i] * zero_moment)
        + (4.0 / tau_heat) * ratio * heat_first[i]
        for i in range(3)
    ]
    common = jnp.where(inlet, gain, (1.0 / tau_flow) * gain - dot(ue, pull))
    pull = [jnp.where(inlet, 0.0, p) for p in pull]
    keep = jnp.where(inlet, 0.0, 1.0 - 1.0 / tau_flow)
    flow = []
    for q in range(FLOW):
        value = keep * s[q] + common
        for i in range(3):
            if VELOCITY[q][i] == 1:
                value = value + pull[i]
            elif VELOCITY[q][i] == -1:
                value = value - pull[i]
        flow.append(jnp.where(wall, s[OPPOSITE[q]], value))
    heat_common = jnp.where(inlet, 0.0, (1.0 / tau_heat) * (heat_zero + 4.0 * dot(heat_first, ue)))
    heat_keep = jnp.where(inlet, 0.0, 1.0 - 1.0 / tau_heat)
    heat = [
        jnp.where(wall, t[OPPOSITE[q]], heat_keep * t[q] + heat_common) for q in range(HEAT)
    ]
    return flow, heat


def interior(nxt, nzt, flags, ue_in, ratio_in, cot_flow, cot_heat, cot_plate, *refs):
    x_in, z_in = refs[:nxt], refs[nxt : nxt + nzt]
    rest_in = refs[nxt + nzt : nxt + 2 * nzt]
    grad_flow, grad_heat, grad_plate = refs[-3:]
    halo = Halo(cot_flow, cot_heat, x_in, z_in, rest_in)
    depth, width = halo.depth, halo.width
    layers = cot_plate.shape[0]
    base = lax.axis_index("gz") == 0

    for z in range(depth):
        star = []
        for k, (_, cy, cz) in enumerate(DIRECTIONS):
            plane = halo.shifted(k, z)
            if cy:
                plane = shift_lanes(plane, cy)
            if cz == -1 and z == 0:
                if k < FLOW:
                    bounced = cot_flow[OPPOSITE[k], 0]
                else:
                    bounced = -cot_heat[OPPOSITE[k - FLOW], 0]
                plane = jnp.where(base, bounced, plane)
            star.append(plane)
        kind = flags[z]
        flow, heat = collide_back(
            star[:FLOW], star[FLOW:], [ue_in[c, z] for c in range(3)], ratio_in[z], kind == 1, kind == 2
        )
        for q in range(FLOW):
            grad_flow[q, z] = flow[q]
        for q in range(HEAT):
            value = heat[q]
            if z == 0:
                value = value + jnp.where(base, coupling * cot_plate[0], 0.0)
            grad_heat[q, z] = value

    x_above, x_below = incoming("gx", [r[...] for r in x_in])
    z_above, z_below = incoming("gz", [r[:width, :] for r in rest_in])
    for l in range(layers):
        own = cot_plate[l]
        up = cot_plate[l + 1] if l + 1 < layers else z_above
        down = cot_plate[l - 1] if l > 0 else z_below
        r = len(XP) * depth + l
        total = up + down
        total = total + shift_rows(own, 1, x_above[r : r + 1, :])
        total = total + shift_rows(own, -1, x_below[r : r + 1, :])
        total = total + shift_lanes(own, 1) + shift_lanes(own, -1)
        value = own + diffusion * (total - 6.0 * own)
        if l == 0:
            value = value + jnp.where(base, 0.25 * cot_heat[5, 0] - coupling * own, 0.0)
        grad_plate[l] = value


def finish(nyt, depth, ends, kinds, main_flow, main_heat, main_plate, *refs):
    y_in = refs[:nyt]
    out_flow, out_heat, out_plate, flow_buf, heat_buf, plate_buf, sems = refs[nyt:]
    above, below = incoming("gy", [r[...] for r in y_in])
    layers = main_plate.shape[0]
    length = above.shape[1]
    y = lax.broadcasted_iota(jnp.int32, above.shape, 1)
    zero = jnp.zeros_like(above)
    from_below, from_above = y == 0, y == length - 1
    for z in range(1, depth):
        from_below = from_below | (y == 2 * z)
        from_above = from_above | (y == 2 * z - 1)
    star = []
    for k, c in enumerate(DIRECTIONS):
        if c[1] == -1:
            lane = column_lane(YM.index(k), 0, depth)
            star.append(jnp.where(from_below, turned(below, -lane), zero))
        elif c[1] == 1:
            lane = column_lane(YP.index(k), 0, depth)
            star.append(jnp.where(from_above, turned(above, -lane - 1), zero))
        else:
            star.append(zero)
    kind = kinds[...]
    flow, heat = collide_back(
        star[:FLOW], star[FLOW:], [ends[c] for c in range(3)], ends[3], kind == 1, kind == 2
    )
    edge = (y == 0) | (y == length - 1)
    copies = []
    for values, main, buf, out, first in (
        (flow, main_flow, flow_buf, out_flow, 0),
        (heat, main_heat, heat_buf, out_heat, FLOW),
    ):
        for q, value in enumerate(values):
            for z in range(depth):
                buf[q, z] = main[q, z] + jnp.where(edge, turned(value, -2 * z), 0.0)
            copies.append(pltpu.make_async_copy(buf.at[q], out.at[q], sems.at[first + q]))
            copies[-1].start()
    for l in range(layers):
        lane = plate_lane(l, depth)
        beside = jnp.where(
            y == 0, turned(below, -lane), jnp.where(from_above, turned(above, length - 1 - lane), 0.0)
        )
        beside = jnp.where(edge, beside, 0.0)
        plate_buf[l] = main_plate[l] + diffusion * beside
    copies.append(pltpu.make_async_copy(plate_buf, out_plate, sems.at[FLOW + HEAT]))
    copies[-1].start()
    for copy in copies:
        copy.wait()


def kernel_call(body, outs, count, name, cost=0, smem=(), scratch=(), **params):
    return pl.pallas_call(
        body,
        out_shape=outs,
        in_specs=[
            pl.BlockSpec(memory_space=pltpu.SMEM if i in smem else pltpu.VMEM) for i in range(count)
        ],
        out_specs=[pl.BlockSpec(memory_space=pltpu.VMEM)] * len(outs),
        scratch_shapes=scratch,
        compiler_params=pltpu.CompilerParams(vmem_limit_bytes=VMEM_LIMIT),
        cost_estimate=pl.CostEstimate(flops=0, bytes_accessed=cost, transcendentals=0),
        name=name,
    )


def local(pop_flow, pop_heat, flags, nozzle_id, jet_velocity, cot_flow, cot_heat, cot_plate):
    nxt, nyt, nzt = (rounds(lax.axis_size(a)) for a in AXES)
    _, depth, width, length = cot_flow.shape
    layers = cot_plate.shape[0]
    f32 = jnp.float32
    array = lambda *shape: jax.ShapeDtypeStruct(shape, f32)
    cots = (cot_flow, cot_heat, cot_plate)
    side = padded(len(XM) * depth + layers)

    first = pl.pallas_call(
        functools.partial(pack_first, nxt, nzt),
        out_shape=[pltpu.VMEM((side, length), f32)] * nxt
        + [pltpu.VMEM((len(ZM) * width, length), f32)] * nzt,
        in_specs=[pl.BlockSpec(memory_space=pltpu.HBM)] * 3,
        out_specs=[pl.BlockSpec(memory_space=pltpu.VMEM)] * (nxt + nzt),
        scratch_shapes=[
            pltpu.VMEM((side, length), f32),
            pltpu.VMEM((side, length), f32),
            pltpu.SemaphoreType.DMA((2, len(XM))),
            pltpu.SemaphoreType.DMA((2,)),
            pltpu.SemaphoreType.DMA((nzt, len(ZM))),
        ],
        compiler_params=pltpu.CompilerParams(vmem_limit_bytes=VMEM_FIRST),
        cost_estimate=pl.CostEstimate(flops=0, bytes_accessed=2 << 20, transcendentals=0),
        name="first",
    )(*(pltpu.with_memory_space_constraint(c, pltpu.HBM) for c in cots))
    x_in = [swap(v, "gx", t) for t, v in enumerate(first[:nxt])]
    z_in = [swap(v, "gz", t) for t, v in enumerate(first[nxt:])]
    ue, ratio, end_values, end_kinds = kernel_call(
        prepare,
        [
            array(3, depth, width, length),
            array(depth, width, length),
            array(4, width, length),
            jax.ShapeDtypeStruct((width, length), jnp.int32),
        ],
        5 + nzt,
        "prepare",
        cost=2 << 20,
        smem=(4,),
    )(pop_flow, pop_heat, flags, nozzle_id, jet_velocity, *first[nxt:])
    rest = kernel_call(
        functools.partial(pack_rest, nxt, nzt, depth),
        [array(width + padded(len(XZM)), length)] * nzt,
        1 + nxt + 1,
        "rest",
        cost=1 << 17,
    )(cot_plate, *x_in, ratio)
    rest_in = [swap(v, "gz", t) for t, v in enumerate(rest)]
    columns = kernel_call(
        functools.partial(pack_columns, nxt, nyt, nzt),
        [array(width, length)] * nyt,
        3 + nxt + 2 * nzt,
        "columns",
        cost=1 << 18,
    )(*cots, *x_in, *z_in, *rest)
    y_in = [swap(v, "gy", t) for t, v in enumerate(columns)]
    main = kernel_call(
        functools.partial(interior, nxt, nzt),
        [array(*c.shape) for c in cots],
        6 + nxt + 2 * nzt + nyt,
        "interior",
        cost=2 << 20,
    )(flags, ue, ratio, *cots, *x_in, *z_in, *rest_in, *columns)
    return tuple(
        pl.pallas_call(
            functools.partial(finish, nyt, depth),
            out_shape=[array(*c.shape) for c in cots],
            in_specs=[pl.BlockSpec(memory_space=pltpu.VMEM)] * (5 + nyt),
            out_specs=[pl.BlockSpec(memory_space=pltpu.HBM)] * 3,
            scratch_shapes=[pltpu.VMEM(c.shape, f32) for c in cots]
            + [pltpu.SemaphoreType.DMA((FLOW + HEAT + 1,))],
            compiler_params=pltpu.CompilerParams(vmem_limit_bytes=VMEM_LIMIT),
            name="finish",
        )(end_values, end_kinds, *main, *y_in)
    )


def solution(mesh):
    return jax.shard_map(
        local,
        mesh=mesh,
        in_specs=(
            P(None, "gz", "gx", "gy"),
            P(None, "gz", "gx", "gy"),
            P("gz", "gx", "gy"),
            P("gx", "gy"),
            P(),
            P(None, "gz", "gx", "gy"),
            P(None, "gz", "gx", "gy"),
            P("gz", "gx", "gy"),
        ),
        out_specs=(P(None, "gz", "gx", "gy"), P(None, "gz", "gx", "gy"), P("gz", "gx", "gy")),
        check_vma=False,
    )
```

```python
import functools

import jax
import jax.numpy as jnp
from jax import lax
from jax.experimental import pallas as pl
from jax.experimental.pallas import tpu as pltpu
from jax.sharding import PartitionSpec as P

VELOCITY = (
    (0, 0, 0),
    (1, 0, 0),
    (-1, 0, 0),
    (0, 1, 0),
    (0, -1, 0),
    (0, 0, 1),
    (0, 0, -1),
    (1, 1, 0),
    (-1, -1, 0),
    (1, -1, 0),
    (-1, 1, 0),
    (1, 0, 1),
    (-1, 0, -1),
    (1, 0, -1),
    (-1, 0, 1),
    (0, 1, 1),
    (0, -1, -1),
    (0, 1, -1),
    (0, -1, 1),
)
OPPOSITE = tuple((VELOCITY.index((-a, -b, -c)) for a, b, c in VELOCITY))
WEIGHTS_FLOW = (1.0 / 3.0,) + (1.0 / 18.0,) * 6 + (1.0 / 36.0,) * 12
WEIGHTS_HEAT = (0.25,) + (0.125,) * 6
FLOW = 19
HEAT = 7
DIRECTIONS = VELOCITY + VELOCITY[:HEAT]
tau_flow = 0.8
tau_heat = 0.9
diffusion = 0.12
coupling = 0.3

AXES = ("gx", "gy", "gz")
COMPONENT = {"gx": 0, "gy": 1, "gz": 2}
VMEM_LIMIT = 8 << 20
EDGE_ROWS = 48


def moving(component, sign):
    return [k for k, c in enumerate(DIRECTIONS) if c[component] == sign]


XP, XM = moving(0, 1), moving(0, -1)
YP, YM = moving(1, 1), moving(1, -1)
ZP, ZM = moving(2, 1), moving(2, -1)


def rounds(size):
    return 1 if size == 2 else 2


def swap(value, **turns):
    sizes = [lax.axis_size(name) for name in AXES]
    flat = lambda p: (p[0] * sizes[1] + p[1]) * sizes[2] + p[2]
    pairs = []
    for a in range(sizes[0]):
        for b in range(sizes[1]):
            for c in range(sizes[2]):
                here = [a, b, c]
                there = [a, b, c]
                for axis, turn in turns.items():
                    at = AXES.index(axis)
                    i = here[at]
                    there[at] = i ^ 1 if turn == 0 else (i + 1 if i % 2 else i - 1)
                if not all(0 <= t < n for t, n in zip(there, sizes)):
                    there = [a, sizes[1] - 1 - b if "gy" in turns else b ^ 1, c]
                pairs.append((flat(here), flat(there)))
    return lax.ppermute(value, AXES, pairs)


def place(axis):
    i = lax.axis_index(axis)
    return lax.rem(i, 2) == 0, i < lax.axis_size(axis) - 1, i > 0


def outgoing(axis, turn, to_higher, to_lower):
    even, _, _ = place(axis)
    return jnp.where(even, to_higher, to_lower) if turn == 0 else jnp.where(even, to_lower, to_higher)


def incoming(axis, turns):
    even, higher, lower = place(axis)
    first, last = turns[0], turns[-1]
    zero = jnp.zeros_like(first)
    above = jnp.where(higher, jnp.where(even, first, last), zero)
    below = jnp.where(lower, jnp.where(even, last, first), zero)
    return above, below


def slab(cot_flow, cot_heat, k, z):
    return cot_flow[k, z] if k < FLOW else cot_heat[k - FLOW, z]


def row_of(cot_flow, cot_heat, k, z, x):
    return cot_flow[k, z, x : x + 1, :] if k < FLOW else cot_heat[k - FLOW, z, x : x + 1, :]


def padded(rows):
    return -(-rows // 8) * 8


def turned(plane, by):
    by %= plane.shape[1]
    return pltpu.roll(plane, by, 1) if by else plane


def column_lane(n, z, depth):
    return n * depth + z


def plate_lane(l, depth):
    return column_lane(len(YM), 0, depth) + l


def shift_lanes(plane, sign, halo, lane):
    y = lax.broadcasted_iota(jnp.int32, plane.shape, 1)
    edge = plane.shape[1] - 1 if sign == 1 else 0
    return jnp.where(y == edge, turned(halo, edge - lane), turned(plane, -sign))


def shift_rows(plane, sign):
    width = plane.shape[0]
    x = lax.broadcasted_iota(jnp.int32, plane.shape, 0)
    edge = width - 1 if sign == 1 else 0
    return jnp.where(x == edge, 0.0, pltpu.roll(plane, -sign % width, 0))


def pack_faces(nzt, cot_flow, cot_heat, cot_plate, *refs):
    outs, sems = refs[:nzt], refs[nzt]
    depth, width = cot_flow.shape[1], cot_flow.shape[2]
    layers = cot_plate.shape[0]
    even, _, _ = place("gz")
    copies = []
    for turn in range(nzt):
        up = even if turn == 0 else jnp.logical_not(even)
        z = jnp.where(up, depth - 1, 0)
        sources = []
        for hi, lo in zip(ZM, ZP):
            ref, skip = (cot_flow, 0) if hi < FLOW else (cot_heat, FLOW)
            sources.append(ref.at[jnp.where(up, hi - skip, lo - skip), z])
        sources.append(cot_plate.at[jnp.where(up, layers - 1, 0)])
        for n, source in enumerate(sources):
            target = outs[turn].at[n * width : (n + 1) * width, :]
            copies.append(pltpu.make_async_copy(source, target, sems.at[turn, n]))
            copies[-1].start()
    for copy in copies:
        copy.wait()


def pack_columns(nyt, cot_flow, cot_heat, cot_plate, *refs):
    outs = refs[-nyt:]
    depth, width, length = cot_flow.shape[1:]
    layers = cot_plate.shape[0]
    y = lax.broadcasted_iota(jnp.int32, (width, length), 1)

    def put(packed, plane, source, lane):
        return jnp.where(y == lane, turned(plane, lane - source), packed)

    packs = []
    for side, source in ((YM, length - 1), (YP, 0)):
        packed = jnp.zeros((width, length), jnp.float32)
        for n, k in enumerate(side):
            for z in range(depth):
                packed = put(
                    packed, slab(cot_flow, cot_heat, k, z), source, column_lane(n, z, depth)
                )
        for l in range(layers):
            packed = put(packed, cot_plate[l], source, plate_lane(l, depth))
        packs.append(packed)
    for turn in range(nyt):
        outs[turn][...] = outgoing("gy", turn, packs[0], packs[1])


def pack_edges(nyt, nzt, depth, *refs):
    y_in, outs = refs[:nyt], refs[-nzt:]
    above, below = incoming("gy", [r[...] for r in y_in])
    width, length = above.shape
    y = lax.broadcasted_iota(jnp.int32, above.shape, 1)

    def edge(cz, z):
        down = column_lane(YM.index(DIRECTIONS.index((0, -1, cz))), z, depth)
        up = column_lane(YP.index(DIRECTIONS.index((0, 1, cz))), z, depth)
        up_plane = jnp.where(y == length - 1, turned(above, length - 1 - up), 0.0)
        return jnp.where(y == 0, turned(below, -down), up_plane)

    to_higher, to_lower = edge(-1, depth - 1), edge(1, 0)
    for turn in range(nzt):
        outs[turn][:width, :] = outgoing("gz", turn, to_higher, to_lower)
        if outs[turn].shape[0] > width:
            outs[turn][width:, :] = jnp.zeros((outs[turn].shape[0] - width, length), jnp.float32)


def face_rows(z_in, k, rows):
    up = DIRECTIONS[k][2] == 1
    at = (ZP if up else ZM).index(k) * ((z_in[0].shape[0]) // (len(ZP) + 1))
    above, below = incoming("gz", [r[at + rows.start : at + rows.stop, :] for r in z_in])
    return above if up else below


def pack_rows(nxt, nyt, nzt, cot_flow, cot_heat, cot_plate, *refs):
    z_in, y_in, outs = refs[:nzt], refs[nzt : nzt + nyt], refs[-nxt:]
    depth, width, length = cot_flow.shape[1:]
    layers = cot_plate.shape[0]
    y_above, y_below = incoming("gy", [r[...] for r in y_in])

    def row(k, z, x):
        _, cy, cz = DIRECTIONS[k]
        if 0 <= z + cz < depth:
            value = row_of(cot_flow, cot_heat, k, z + cz, x)
        else:
            value = face_rows(z_in, k, slice(x, x + 1))
        if cy == 0:
            return value
        halo, n = (y_above, YP.index(k)) if cy == 1 else (y_below, YM.index(k))
        return shift_lanes(value, cy, halo[x : x + 1, :], column_lane(n, z, depth))

    used = len(XM) * depth + layers
    for turn in range(nxt):
        if used < outs[turn].shape[0]:
            outs[turn][used:, :] = jnp.zeros((outs[turn].shape[0] - used, length), jnp.float32)
    for n, (hi, lo) in enumerate(zip(XM, XP)):
        for z in range(depth):
            r = n * depth + z
            to_higher, to_lower = row(hi, z, width - 1), row(lo, z, 0)
            for turn in range(nxt):
                outs[turn][r : r + 1, :] = outgoing("gx", turn, to_higher, to_lower)
    for l in range(layers):
        r = len(XM) * depth + l
        for turn in range(nxt):
            outs[turn][r : r + 1, :] = outgoing(
                "gx", turn, cot_plate[l, width - 1 : width, :], cot_plate[l, 0:1, :]
            )


def prepare(pop_flow, pop_heat, flags, nozzle, jet_velocity, *refs):
    ue_out, ratio_out, rows_out, kinds_out = refs[-4:]
    depth, width = flags.shape[:2]
    jets = [jnp.zeros(nozzle.shape, jnp.float32)] * 3
    which = nozzle[...]
    for n in range(jet_velocity.shape[1]):
        hit = which == n
        jets = [jnp.where(hit, jet_velocity[c, n], jets[c]) for c in range(3)]
    for z in range(depth):
        inlet = flags[z] == 2
        pops = [pop_flow[q, z] for q in range(FLOW)]
        rho = sum(pops[1:], pops[0])
        inverse = 1.0 / rho
        values = []
        for c in range(3):
            plus = [pops[q] for q in range(FLOW) if VELOCITY[q][c] == 1]
            minus = [pops[q] for q in range(FLOW) if VELOCITY[q][c] == -1]
            total = sum(plus[1:], plus[0]) - sum(minus[1:], minus[0])
            values.append(jnp.where(inlet, jets[c], total * inverse))
            ue_out[c, z] = values[c]
        heat = [pop_heat[q, z] for q in range(HEAT)]
        values.append(sum(heat[1:], heat[0]) * inverse)
        ratio_out[z] = values[3]
        for side, x in enumerate((0, width - 1)):
            r = side * depth + z
            for c in range(4):
                rows_out[c, r : r + 1, :] = values[c][x : x + 1, :]
            kinds_out[r : r + 1, :] = flags[z, x : x + 1, :]


def collide_back(s, t, ue, ratio, wall, inlet):
    add = lambda a, b: b if a is None else a + b
    zero_moment = WEIGHTS_FLOW[0] * s[0]
    first = [None] * 3
    second = {}
    for group, weight in ((range(1, 7), WEIGHTS_FLOW[1]), (range(7, 19), WEIGHTS_FLOW[7])):
        odd = [None] * 3
        even = {}
        total = None
        for q in group:
            o = OPPOSITE[q]
            if o < q:
                continue
            c = VELOCITY[q]
            plus, minus = s[q] + s[o], s[q] - s[o]
            total = add(total, plus)
            for i in range(3):
                if c[i]:
                    odd[i] = add(odd[i], minus if c[i] == 1 else -minus)
                for j in range(i, 3):
                    if c[i] * c[j]:
                        even[i, j] = add(even.get((i, j)), plus if c[i] * c[j] == 1 else -plus)
        zero_moment = zero_moment + weight * total
        for i in range(3):
            first[i] = add(first[i], weight * odd[i])
        for key, value in even.items():
            second[key] = add(second.get(key), weight * value)
    heat_first = [WEIGHTS_HEAT[1] * (t[2 * c + 1] - t[2 * c + 2]) for c in range(3)]
    heat_zero = WEIGHTS_HEAT[0] * t[0] + WEIGHTS_HEAT[1] * (
        (t[1] + t[2]) + (t[3] + t[4]) + (t[5] + t[6])
    )
    dot = lambda a, b: a[0] * b[0] + a[1] * b[1] + a[2] * b[2]
    bent = [sum(second[min(i, j), max(i, j)] * ue[j] for j in range(3)) for i in range(3)]
    gain = zero_moment * (1.0 - 1.5 * dot(ue, ue)) + 3.0 * dot(first, ue) + 4.5 * dot(bent, ue)
    pull = [
        (3.0 / tau_flow) * (first[i] + 3.0 * bent[i] - ue[i] * zero_moment)
        + (4.0 / tau_heat) * ratio * heat_first[i]
        for i in range(3)
    ]
    common = jnp.where(inlet, gain, (1.0 / tau_flow) * gain - dot(ue, pull))
    pull = [jnp.where(inlet, 0.0, p) for p in pull]
    keep = jnp.where(inlet, 0.0, 1.0 - 1.0 / tau_flow)
    flow = []
    for q in range(FLOW):
        value = keep * s[q] + common
        for i in range(3):
            if VELOCITY[q][i] == 1:
                value = value + pull[i]
            elif VELOCITY[q][i] == -1:
                value = value - pull[i]
        flow.append(jnp.where(wall, s[OPPOSITE[q]], value))
    heat_common = jnp.where(inlet, 0.0, (1.0 / tau_heat) * (heat_zero + 4.0 * dot(heat_first, ue)))
    heat_keep = jnp.where(inlet, 0.0, 1.0 - 1.0 / tau_heat)
    heat = [
        jnp.where(wall, t[OPPOSITE[q]], heat_keep * t[q] + heat_common) for q in range(HEAT)
    ]
    return flow, heat


def interior(nyt, nzt, flags, ue_in, ratio_in, cot_flow, cot_heat, cot_plate, *refs):
    z_in, y_in, yz_in = refs[:nzt], refs[nzt : nzt + nyt], refs[nzt + nyt : 2 * nzt + nyt]
    out_flow, out_heat, out_plate, rows_flow, rows_heat, rows_plate = refs[-10:-4]
    flow_buf, heat_buf, plate_buf, sems = refs[-4:]
    depth, width = cot_flow.shape[1], cot_flow.shape[2]
    layers = cot_plate.shape[0]
    base = lax.axis_index("gz") == 0
    y_above, y_below = incoming("gy", [r[...] for r in y_in])
    yz_above, yz_below = incoming("gz", [r[:width, :] for r in yz_in])
    copies = []

    def send(source, target):
        copies.append(pltpu.make_async_copy(source, target, sems.at[len(copies)]))
        copies[-1].start()

    z_above = z_below = None
    z_rows = slice(len(ZP) * width, (len(ZP) + 1) * width)
    z_above, z_below = incoming("gz", [r[z_rows, :] for r in z_in])
    for l in range(layers):
        own = cot_plate[l]
        up = cot_plate[l + 1] if l + 1 < layers else z_above
        down = cot_plate[l - 1] if l > 0 else z_below
        total = up + down + shift_rows(own, 1) + shift_rows(own, -1)
        total = total + shift_lanes(own, 1, y_above, plate_lane(l, depth))
        total = total + shift_lanes(own, -1, y_below, plate_lane(l, depth))
        value = own + diffusion * (total - 6.0 * own)
        if l == 0:
            value = value + jnp.where(base, 0.25 * cot_heat[5, 0] - coupling * own, 0.0)
        plate_buf[l] = value
        rows_plate[l : l + 1, :] = value[0:1, :]
        rows_plate[layers + l : layers + l + 1, :] = value[width - 1 : width, :]
    send(plate_buf, out_plate)

    for z in range(depth):
        star = []
        for k, (cx, cy, cz) in enumerate(DIRECTIONS):
            at = z + cz
            inside = 0 <= at < depth
            plane = slab(cot_flow, cot_heat, k, at) if inside else face_rows(z_in, k, slice(0, width))
            if cy:
                halo, n = (y_above, YP.index(k)) if cy == 1 else (y_below, YM.index(k))
                if inside:
                    plane = shift_lanes(plane, cy, halo, column_lane(n, at, depth))
                else:
                    lane = plane.shape[1] - 1 if cy == 1 else 0
                    plane = shift_lanes(plane, cy, yz_above if cz == 1 else yz_below, lane)
            if cx:
                plane = shift_rows(plane, cx)
            if cz == -1 and z == 0:
                if k < FLOW:
                    bounced = cot_flow[OPPOSITE[k], 0]
                else:
                    bounced = -cot_heat[OPPOSITE[k - FLOW], 0]
                plane = jnp.where(base, bounced, plane)
            star.append(plane)
        kind = flags[z]
        flow, heat = collide_back(
            star[:FLOW], star[FLOW:], [ue_in[c, z] for c in range(3)], ratio_in[z], kind == 1, kind == 2
        )
        if z == 0:
            source = jnp.where(base, coupling * cot_plate[0], 0.0)
            heat = [value + source for value in heat]
        for values, buf, rows in ((flow, flow_buf, rows_flow), (heat, heat_buf, rows_heat)):
            for q, value in enumerate(values):
                buf[q, z] = value
                rows[q, z : z + 1, :] = value[0:1, :]
                rows[q, depth + z : depth + z + 1, :] = value[width - 1 : width, :]
        send(flow_buf.at[:, z], out_flow.at[:, z])
        send(heat_buf.at[:, z], out_heat.at[:, z])
    for copy in copies:
        copy.wait()


def finish(nxt, rows_in, kinds, rows_flow, rows_heat, rows_plate, *refs):
    x_in, refs = refs[:nxt], refs[nxt + 3 :]
    out_flow, out_heat, out_plate, above_buf, below_buf, star_buf, flow_buf, heat_buf, plate_buf, sems = refs
    depth, width = out_flow.shape[1], out_flow.shape[2]
    layers = out_plate.shape[0]
    above, below = incoming("gx", [r[...] for r in x_in])
    above_buf[...] = above
    below_buf[...] = below
    zero = jnp.zeros((2 * depth, above.shape[1]), jnp.float32)
    star = []
    for k, c in enumerate(DIRECTIONS):
        if c[0] == 0:
            star.append(zero)
            continue
        star_buf[k] = zero
        if c[0] == 1:
            n = XP.index(k) * depth
            star_buf[k, depth:, :] = above_buf[n : n + depth, :]
        else:
            n = XM.index(k) * depth
            star_buf[k, :depth, :] = below_buf[n : n + depth, :]
        star.append(star_buf[k])
    kind = kinds[...]
    flow, heat = collide_back(
        star[:FLOW], star[FLOW:], [rows_in[c] for c in range(3)], rows_in[3], kind == 1, kind == 2
    )
    copies = []
    for values, rows, buf, out in (
        (flow, rows_flow, flow_buf, out_flow),
        (heat, rows_heat, heat_buf, out_heat),
    ):
        for q, value in enumerate(values):
            buf[q] = rows[q] + value
        for side, x in enumerate((0, width - 1)):
            source = buf.at[:, side * depth : (side + 1) * depth, :]
            copies.append(pltpu.make_async_copy(source, out.at[:, :, x, :], sems.at[len(copies)]))
            copies[-1].start()
    n = len(XP) * depth
    for side, (x, beside) in enumerate(((0, below_buf), (width - 1, above_buf))):
        rows = slice(side * layers, (side + 1) * layers)
        plate_buf[side] = rows_plate[rows, :] + diffusion * beside[n : n + layers, :]
        copies.append(pltpu.make_async_copy(plate_buf.at[side], out_plate.at[:, x, :], sems.at[len(copies)]))
        copies[-1].start()
    for copy in copies:
        copy.wait()


def kernel_call(body, outs, spaces, name, cost, out_spaces=None, scratch=(), aliases=None):
    return pl.pallas_call(
        body,
        out_shape=outs,
        in_specs=[pl.BlockSpec(memory_space=space) for space in spaces],
        out_specs=[
            pl.BlockSpec(memory_space=space) for space in (out_spaces or [pltpu.VMEM] * len(outs))
        ],
        scratch_shapes=scratch,
        input_output_aliases=aliases or {},
        compiler_params=pltpu.CompilerParams(vmem_limit_bytes=VMEM_LIMIT),
        cost_estimate=pl.CostEstimate(flops=0, bytes_accessed=cost, transcendentals=0),
        name=name,
    )


def local(pop_flow, pop_heat, flags, nozzle_id, jet_velocity, cot_flow, cot_heat, cot_plate):
    nxt, nyt, nzt = (rounds(lax.axis_size(a)) for a in AXES)
    _, depth, width, length = cot_flow.shape
    layers = cot_plate.shape[0]
    f32 = jnp.float32
    array = lambda *shape: jax.ShapeDtypeStruct(shape, f32)
    vmem, hbm = pltpu.VMEM, pltpu.HBM
    cots = (cot_flow, cot_heat, cot_plate)
    side = padded(len(XM) * depth + layers)

    faces = kernel_call(
        functools.partial(pack_faces, nzt),
        [array((len(ZM) + 1) * width, length)] * nzt,
        [hbm] * 3,
        "faces",
        1 << 20,
        scratch=[pltpu.SemaphoreType.DMA((nzt, len(ZM) + 1))],
    )(*(pltpu.with_memory_space_constraint(c, hbm) for c in cots))
    z_in = [swap(v, gz=t) for t, v in enumerate(faces)]
    columns = kernel_call(
        functools.partial(pack_columns, nyt),
        [array(width, length)] * nyt,
        [vmem] * (3 + nzt),
        "columns",
        1 << 18,
    )(*cots, *faces)
    y_in = [swap(v, gy=t) for t, v in enumerate(columns)]
    edges = kernel_call(
        functools.partial(pack_edges, nyt, nzt, depth),
        [array(EDGE_ROWS, length)] * nzt,
        [vmem] * nyt,
        "edges",
        1 << 16,
    )(*y_in)
    yz_in = [swap(v, gz=t) for t, v in enumerate(edges)]
    rows = kernel_call(
        functools.partial(pack_rows, nxt, nyt, nzt),
        [array(side, length)] * nxt,
        [vmem] * (3 + 2 * nzt + nyt),
        "rows",
        1 << 18,
    )(*cots, *z_in, *y_in, *edges)
    x_in = [swap(v, gx=t) for t, v in enumerate(rows)]
    ue, ratio, row_values, row_kinds = kernel_call(
        prepare,
        [
            array(3, depth, width, length),
            array(depth, width, length),
            array(4, 2 * depth, length),
            jax.ShapeDtypeStruct((2 * depth, length), jnp.int32),
        ],
        [vmem] * 4 + [pltpu.SMEM] + [vmem] * nxt,
        "prepare",
        2 << 20,
    )(pop_flow, pop_heat, flags, nozzle_id, jet_velocity, *rows)
    *grads, rows_flow, rows_heat, rows_plate = kernel_call(
        functools.partial(interior, nyt, nzt),
        [array(*c.shape) for c in cots]
        + [array(FLOW, 2 * depth, length), array(HEAT, 2 * depth, length), array(2 * layers, length)],
        [vmem] * (6 + 2 * nzt + nyt),
        "interior",
        4 << 20,
        out_spaces=[hbm] * 3 + [vmem] * 3,
        scratch=[pltpu.VMEM(c.shape, f32) for c in cots] + [pltpu.SemaphoreType.DMA((2 * depth + 1,))],
    )(flags, ue, ratio, *cots, *z_in, *y_in, *yz_in)
    return tuple(
        kernel_call(
            functools.partial(finish, nxt),
            [array(*c.shape) for c in cots],
            [vmem] * (5 + nxt) + [hbm] * 3,
            "finish",
            1 << 20,
            out_spaces=[hbm] * 3,
            scratch=[
                pltpu.VMEM((side, length), f32),
                pltpu.VMEM((side, length), f32),
                pltpu.VMEM((FLOW + HEAT, 2 * depth, length), f32),
                pltpu.VMEM((FLOW, 2 * depth, length), f32),
                pltpu.VMEM((HEAT, 2 * depth, length), f32),
                pltpu.VMEM((2, layers, length), f32),
                pltpu.SemaphoreType.DMA((6,)),
            ],
            aliases={5 + nxt + i: i for i in range(3)},
        )(row_values, row_kinds, rows_flow, rows_heat, rows_plate, *x_in, *grads)
    )


def solution(mesh):
    return jax.shard_map(
        local,
        mesh=mesh,
        in_specs=(
            P(None, "gz", "gx", "gy"),
            P(None, "gz", "gx", "gy"),
            P("gz", "gx", "gy"),
            P("gx", "gy"),
            P(),
            P(None, "gz", "gx", "gy"),
            P(None, "gz", "gx", "gy"),
            P("gz", "gx", "gy"),
        ),
        out_specs=(P(None, "gz", "gx", "gy"), P(None, "gz", "gx", "gy"), P("gz", "gx", "gy")),
        check_vma=False,
    )
```

```python
import functools

import jax
import jax.numpy as jnp
from jax import lax
from jax.experimental import pallas as pl
from jax.experimental.pallas import tpu as pltpu
from jax.sharding import PartitionSpec as P

VELOCITY = (
    (0, 0, 0),
    (1, 0, 0),
    (-1, 0, 0),
    (0, 1, 0),
    (0, -1, 0),
    (0, 0, 1),
    (0, 0, -1),
    (1, 1, 0),
    (-1, -1, 0),
    (1, -1, 0),
    (-1, 1, 0),
    (1, 0, 1),
    (-1, 0, -1),
    (1, 0, -1),
    (-1, 0, 1),
    (0, 1, 1),
    (0, -1, -1),
    (0, 1, -1),
    (0, -1, 1),
)
OPPOSITE = tuple((VELOCITY.index((-a, -b, -c)) for a, b, c in VELOCITY))
WEIGHTS_FLOW = (1.0 / 3.0,) + (1.0 / 18.0,) * 6 + (1.0 / 36.0,) * 12
WEIGHTS_HEAT = (0.25,) + (0.125,) * 6
FLOW = 19
HEAT = 7
DIRECTIONS = VELOCITY + VELOCITY[:HEAT]
tau_flow = 0.8
tau_heat = 0.9
diffusion = 0.12
coupling = 0.3

AXES = ("gx", "gy", "gz")
COMPONENT = {"gx": 0, "gy": 1, "gz": 2}
VMEM_LIMIT = 8 << 20
EDGE_ROWS = 48
YPAD = (0, 0)
XPAD = (0, 0)


def moving(component, sign):
    return [k for k, c in enumerate(DIRECTIONS) if c[component] == sign]


XP, XM = moving(0, 1), moving(0, -1)
YP, YM = moving(1, 1), moving(1, -1)
ZP, ZM = moving(2, 1), moving(2, -1)


def rounds(size):
    return 1 if size == 2 else 2


def swap(value, **turns):
    sizes = [lax.axis_size(name) for name in AXES]
    flat = lambda p: (p[0] * sizes[1] + p[1]) * sizes[2] + p[2]
    pairs = []
    for a in range(sizes[0]):
        for b in range(sizes[1]):
            for c in range(sizes[2]):
                here = [a, b, c]
                there = [a, b, c]
                for axis, turn in turns.items():
                    at = AXES.index(axis)
                    i = here[at]
                    there[at] = i ^ 1 if turn == 0 else (i + 1 if i % 2 else i - 1)
                if not all(0 <= t < n for t, n in zip(there, sizes)):
                    there = [a, sizes[1] - 1 - b if "gy" in turns else b ^ 1, c]
                pairs.append((flat(here), flat(there)))
    return lax.ppermute(value, AXES, pairs)


def place(axis):
    i = lax.axis_index(axis)
    return lax.rem(i, 2) == 0, i < lax.axis_size(axis) - 1, i > 0


def outgoing(axis, turn, to_higher, to_lower):
    even, _, _ = place(axis)
    return jnp.where(even, to_higher, to_lower) if turn == 0 else jnp.where(even, to_lower, to_higher)


def incoming(axis, turns):
    even, higher, lower = place(axis)
    first, last = turns[0], turns[-1]
    zero = jnp.zeros_like(first)
    above = jnp.where(higher, jnp.where(even, first, last), zero)
    below = jnp.where(lower, jnp.where(even, last, first), zero)
    return above, below


def slab(cot_flow, cot_heat, k, z):
    return cot_flow[k, z] if k < FLOW else cot_heat[k - FLOW, z]


def row_of(cot_flow, cot_heat, k, z, x):
    return cot_flow[k, z, x : x + 1, :] if k < FLOW else cot_heat[k - FLOW, z, x : x + 1, :]


def padded(rows):
    return -(-rows // 8) * 8


def turned(plane, by):
    by %= plane.shape[1]
    return pltpu.roll(plane, by, 1) if by else plane


def column_lane(n, z, depth):
    return n * depth + z


def plate_lane(l, depth):
    return column_lane(len(YM), 0, depth) + l


def shift_lanes(plane, sign, halo, lane):
    y = lax.broadcasted_iota(jnp.int32, plane.shape, 1)
    edge = plane.shape[1] - 1 if sign == 1 else 0
    return jnp.where(y == edge, turned(halo, edge - lane), turned(plane, -sign))


def shift_rows(plane, sign):
    width = plane.shape[0]
    x = lax.broadcasted_iota(jnp.int32, plane.shape, 0)
    edge = width - 1 if sign == 1 else 0
    return jnp.where(x == edge, 0.0, pltpu.roll(plane, -sign % width, 0))


def pack_faces(nzt, cot_flow, cot_heat, cot_plate, *refs):
    outs, sems = refs[:nzt], refs[nzt]
    depth, width = cot_flow.shape[1], cot_flow.shape[2]
    layers = cot_plate.shape[0]
    even, _, _ = place("gz")
    copies = []
    for turn in range(nzt):
        up = even if turn == 0 else jnp.logical_not(even)
        z = jnp.where(up, depth - 1, 0)
        sources = []
        for hi, lo in zip(ZM, ZP):
            ref, skip = (cot_flow, 0) if hi < FLOW else (cot_heat, FLOW)
            sources.append(ref.at[jnp.where(up, hi - skip, lo - skip), z])
        sources.append(cot_plate.at[jnp.where(up, layers - 1, 0)])
        for n, source in enumerate(sources):
            target = outs[turn].at[n * width : (n + 1) * width, :]
            copies.append(pltpu.make_async_copy(source, target, sems.at[turn, n]))
            copies[-1].start()
    for copy in copies:
        copy.wait()


def pack_columns(nyt, cot_flow, cot_heat, cot_plate, *refs):
    outs = refs[-nyt:]
    depth, width, length = cot_flow.shape[1:]
    layers = cot_plate.shape[0]
    y = lax.broadcasted_iota(jnp.int32, (width, length), 1)

    def put(packed, plane, source, lane):
        return jnp.where(y == lane, turned(plane, lane - source), packed)

    packs = []
    for side, source in ((YM, length - 1), (YP, 0)):
        packed = jnp.zeros((width, length), jnp.float32)
        for n, k in enumerate(side):
            for z in range(depth):
                packed = put(
                    packed, slab(cot_flow, cot_heat, k, z), source, column_lane(n, z, depth)
                )
        for l in range(layers):
            packed = put(packed, cot_plate[l], source, plate_lane(l, depth))
        packs.append(packed)
    for turn in range(nyt):
        outs[turn][:width, :] = outgoing("gy", turn, packs[0], packs[1])
        if outs[turn].shape[0] > width:
            outs[turn][width:, :] = jnp.zeros((outs[turn].shape[0] - width, length), jnp.float32)


def pack_edges(nyt, nzt, depth, width, *refs):
    y_in, outs = refs[:nyt], refs[-nzt:]
    above, below = incoming("gy", [r[:width, :] for r in y_in])
    length = above.shape[1]
    y = lax.broadcasted_iota(jnp.int32, above.shape, 1)

    def edge(cz, z):
        down = column_lane(YM.index(DIRECTIONS.index((0, -1, cz))), z, depth)
        up = column_lane(YP.index(DIRECTIONS.index((0, 1, cz))), z, depth)
        up_plane = jnp.where(y == length - 1, turned(above, length - 1 - up), 0.0)
        return jnp.where(y == 0, turned(below, -down), up_plane)

    to_higher, to_lower = edge(-1, depth - 1), edge(1, 0)
    for turn in range(nzt):
        outs[turn][:width, :] = outgoing("gz", turn, to_higher, to_lower)
        if outs[turn].shape[0] > width:
            outs[turn][width:, :] = jnp.zeros((outs[turn].shape[0] - width, length), jnp.float32)


def face_rows(z_in, k, rows):
    up = DIRECTIONS[k][2] == 1
    at = (ZP if up else ZM).index(k) * ((z_in[0].shape[0]) // (len(ZP) + 1))
    above, below = incoming("gz", [r[at + rows.start : at + rows.stop, :] for r in z_in])
    return above if up else below


def pack_rows(nxt, nyt, nzt, cot_flow, cot_heat, cot_plate, *refs):
    z_in, y_in, outs = refs[:nzt], refs[nzt : nzt + nyt], refs[-nxt:]
    depth, width, length = cot_flow.shape[1:]
    layers = cot_plate.shape[0]
    y_above, y_below = incoming("gy", [r[:width, :] for r in y_in])

    def row(k, z, x):
        _, cy, cz = DIRECTIONS[k]
        if 0 <= z + cz < depth:
            value = row_of(cot_flow, cot_heat, k, z + cz, x)
        else:
            value = face_rows(z_in, k, slice(x, x + 1))
        if cy == 0:
            return value
        halo, n = (y_above, YP.index(k)) if cy == 1 else (y_below, YM.index(k))
        return shift_lanes(value, cy, halo[x : x + 1, :], column_lane(n, z, depth))

    used = len(XM) * depth + layers
    for turn in range(nxt):
        if used < outs[turn].shape[0]:
            outs[turn][used:, :] = jnp.zeros((outs[turn].shape[0] - used, length), jnp.float32)
    for n, (hi, lo) in enumerate(zip(XM, XP)):
        for z in range(depth):
            r = n * depth + z
            to_higher, to_lower = row(hi, z, width - 1), row(lo, z, 0)
            for turn in range(nxt):
                outs[turn][r : r + 1, :] = outgoing("gx", turn, to_higher, to_lower)
    for l in range(layers):
        r = len(XM) * depth + l
        for turn in range(nxt):
            outs[turn][r : r + 1, :] = outgoing(
                "gx", turn, cot_plate[l, width - 1 : width, :], cot_plate[l, 0:1, :]
            )


def prepare(pop_flow, pop_heat, flags, nozzle, jet_velocity, *refs):
    ue_out, ratio_out, rows_out, kinds_out = refs[-4:]
    depth, width = flags.shape[:2]
    jets = [jnp.zeros(nozzle.shape, jnp.float32)] * 3
    which = nozzle[...]
    for n in range(jet_velocity.shape[1]):
        hit = which == n
        jets = [jnp.where(hit, jet_velocity[c, n], jets[c]) for c in range(3)]
    for z in range(depth):
        inlet = flags[z] == 2
        pops = [pop_flow[q, z] for q in range(FLOW)]
        rho = sum(pops[1:], pops[0])
        inverse = 1.0 / rho
        values = []
        for c in range(3):
            plus = [pops[q] for q in range(FLOW) if VELOCITY[q][c] == 1]
            minus = [pops[q] for q in range(FLOW) if VELOCITY[q][c] == -1]
            total = sum(plus[1:], plus[0]) - sum(minus[1:], minus[0])
            values.append(jnp.where(inlet, jets[c], total * inverse))
            ue_out[c, z] = values[c]
        heat = [pop_heat[q, z] for q in range(HEAT)]
        values.append(sum(heat[1:], heat[0]) * inverse)
        ratio_out[z] = values[3]
        for side, x in enumerate((0, width - 1)):
            r = side * depth + z
            for c in range(4):
                rows_out[c, r : r + 1, :] = values[c][x : x + 1, :]
            kinds_out[r : r + 1, :] = flags[z, x : x + 1, :]


def collide_back(s, t, ue, ratio, wall, inlet):
    add = lambda a, b: b if a is None else a + b
    zero_moment = WEIGHTS_FLOW[0] * s[0]
    first = [None] * 3
    second = {}
    for group, weight in ((range(1, 7), WEIGHTS_FLOW[1]), (range(7, 19), WEIGHTS_FLOW[7])):
        odd = [None] * 3
        even = {}
        total = None
        for q in group:
            o = OPPOSITE[q]
            if o < q:
                continue
            c = VELOCITY[q]
            plus, minus = s[q] + s[o], s[q] - s[o]
            total = add(total, plus)
            for i in range(3):
                if c[i]:
                    odd[i] = add(odd[i], minus if c[i] == 1 else -minus)
                for j in range(i, 3):
                    if c[i] * c[j]:
                        even[i, j] = add(even.get((i, j)), plus if c[i] * c[j] == 1 else -plus)
        zero_moment = zero_moment + weight * total
        for i in range(3):
            first[i] = add(first[i], weight * odd[i])
        for key, value in even.items():
            second[key] = add(second.get(key), weight * value)
    heat_first = [WEIGHTS_HEAT[1] * (t[2 * c + 1] - t[2 * c + 2]) for c in range(3)]
    heat_zero = WEIGHTS_HEAT[0] * t[0] + WEIGHTS_HEAT[1] * (
        (t[1] + t[2]) + (t[3] + t[4]) + (t[5] + t[6])
    )
    dot = lambda a, b: a[0] * b[0] + a[1] * b[1] + a[2] * b[2]
    bent = [sum(second[min(i, j), max(i, j)] * ue[j] for j in range(3)) for i in range(3)]
    gain = zero_moment * (1.0 - 1.5 * dot(ue, ue)) + 3.0 * dot(first, ue) + 4.5 * dot(bent, ue)
    pull = [
        (3.0 / tau_flow) * (first[i] + 3.0 * bent[i] - ue[i] * zero_moment)
        + (4.0 / tau_heat) * ratio * heat_first[i]
        for i in range(3)
    ]
    common = jnp.where(inlet, gain, (1.0 / tau_flow) * gain - dot(ue, pull))
    pull = [jnp.where(inlet, 0.0, p) for p in pull]
    keep = jnp.where(inlet, 0.0, 1.0 - 1.0 / tau_flow)
    flow = []
    for q in range(FLOW):
        value = keep * s[q] + common
        for i in range(3):
            if VELOCITY[q][i] == 1:
                value = value + pull[i]
            elif VELOCITY[q][i] == -1:
                value = value - pull[i]
        flow.append(jnp.where(wall, s[OPPOSITE[q]], value))
    heat_common = jnp.where(inlet, 0.0, (1.0 / tau_heat) * (heat_zero + 4.0 * dot(heat_first, ue)))
    heat_keep = jnp.where(inlet, 0.0, 1.0 - 1.0 / tau_heat)
    heat = [
        jnp.where(wall, t[OPPOSITE[q]], heat_keep * t[q] + heat_common) for q in range(HEAT)
    ]
    return flow, heat


def interior(outer, nyt, nzt, flags, ue_in, ratio_in, cot_flow, cot_heat, cot_plate, *refs):
    z_in, y_in, refs = refs[:nzt], refs[nzt : nzt + nyt], refs[nzt + nyt :]
    depth, width = cot_flow.shape[1], cot_flow.shape[2]
    layers = cot_plate.shape[0]
    base = lax.axis_index("gz") == 0
    y_above, y_below = incoming("gy", [r[:width, :] for r in y_in])
    copies = []
    if outer:
        yz_above, yz_below = incoming("gz", [r[:width, :] for r in refs[:nzt]])
        out_flow, out_heat, rows_flow, rows_heat, flow_buf, heat_buf, sems = refs[-7:]
        zs = (0, depth - 1)
    else:
        out_flow, out_heat, out_plate, rows_flow, rows_heat, rows_plate = refs[-10:-4]
        flow_buf, heat_buf, plate_buf, sems = refs[-4:]
        zs = range(1, depth - 1)

    def send(source, target):
        copies.append(pltpu.make_async_copy(source, target, sems.at[len(copies)]))
        copies[-1].start()

    def plate():
        z_rows = slice(len(ZP) * width, (len(ZP) + 1) * width)
        z_above, z_below = incoming("gz", [r[z_rows, :] for r in z_in])
        for l in range(layers):
            own = cot_plate[l]
            up = cot_plate[l + 1] if l + 1 < layers else z_above
            down = cot_plate[l - 1] if l > 0 else z_below
            total = up + down + shift_rows(own, 1) + shift_rows(own, -1)
            total = total + shift_lanes(own, 1, y_above, plate_lane(l, depth))
            total = total + shift_lanes(own, -1, y_below, plate_lane(l, depth))
            value = own + diffusion * (total - 6.0 * own)
            if l == 0:
                value = value + jnp.where(base, 0.25 * cot_heat[5, 0] - coupling * own, 0.0)
            plate_buf[l] = value
            rows_plate[l : l + 1, :] = value[0:1, :]
            rows_plate[layers + l : layers + l + 1, :] = value[width - 1 : width, :]
        send(plate_buf, out_plate)

    if not outer:
        plate()
    rows_flow[...] = jnp.zeros_like(rows_flow)
    rows_heat[...] = jnp.zeros_like(rows_heat)
    for slot, z in enumerate(zs):
        star = []
        for k, (cx, cy, cz) in enumerate(DIRECTIONS):
            at = z + cz
            inside = 0 <= at < depth
            plane = slab(cot_flow, cot_heat, k, at) if inside else face_rows(z_in, k, slice(0, width))
            if cy:
                halo, n = (y_above, YP.index(k)) if cy == 1 else (y_below, YM.index(k))
                if inside:
                    plane = shift_lanes(plane, cy, halo, column_lane(n, at, depth))
                else:
                    lane = plane.shape[1] - 1 if cy == 1 else 0
                    plane = shift_lanes(plane, cy, yz_above if cz == 1 else yz_below, lane)
            if cx:
                plane = shift_rows(plane, cx)
            if cz == -1 and z == 0:
                if k < FLOW:
                    bounced = cot_flow[OPPOSITE[k], 0]
                else:
                    bounced = -cot_heat[OPPOSITE[k - FLOW], 0]
                plane = jnp.where(base, bounced, plane)
            star.append(plane)
        kind = flags[z]
        flow, heat = collide_back(
            star[:FLOW], star[FLOW:], [ue_in[c, z] for c in range(3)], ratio_in[z], kind == 1, kind == 2
        )
        if z == 0:
            source = jnp.where(base, coupling * cot_plate[0], 0.0)
            heat = [value + source for value in heat]
        for values, buf, rows in ((flow, flow_buf, rows_flow), (heat, heat_buf, rows_heat)):
            for q, value in enumerate(values):
                buf[q, slot] = value
                rows[q, z : z + 1, :] = value[0:1, :]
                rows[q, depth + z : depth + z + 1, :] = value[width - 1 : width, :]
        send(flow_buf.at[:, slot], out_flow.at[:, z])
        send(heat_buf.at[:, slot], out_heat.at[:, z])
    for copy in copies:
        copy.wait()


def finish(nxt, rows_in, kinds, rows_flow, rows_heat, rows_plate, outer_flow, outer_heat, *refs):
    x_in, refs = refs[:nxt], refs[nxt + 3 :]
    out_flow, out_heat, out_plate, above_buf, below_buf, star_buf, flow_buf, heat_buf, plate_buf, sems = refs
    depth, width = out_flow.shape[1], out_flow.shape[2]
    layers = out_plate.shape[0]
    used = above_buf.shape[0]
    above, below = incoming("gx", [r[:used, :] for r in x_in])
    above_buf[...] = above
    below_buf[...] = below
    zero = jnp.zeros((2 * depth, above.shape[1]), jnp.float32)
    star = []
    for k, c in enumerate(DIRECTIONS):
        if c[0] == 0:
            star.append(zero)
            continue
        star_buf[k] = zero
        if c[0] == 1:
            n = XP.index(k) * depth
            star_buf[k, depth:, :] = above_buf[n : n + depth, :]
        else:
            n = XM.index(k) * depth
            star_buf[k, :depth, :] = below_buf[n : n + depth, :]
        star.append(star_buf[k])
    kind = kinds[...]
    flow, heat = collide_back(
        star[:FLOW], star[FLOW:], [rows_in[c] for c in range(3)], rows_in[3], kind == 1, kind == 2
    )
    copies = []
    for values, rows, outer_rows, buf, out in (
        (flow, rows_flow, outer_flow, flow_buf, out_flow),
        (heat, rows_heat, outer_heat, heat_buf, out_heat),
    ):
        for q, value in enumerate(values):
            buf[q] = rows[q] + outer_rows[q] + value
        for side, x in enumerate((0, width - 1)):
            source = buf.at[:, side * depth : (side + 1) * depth, :]
            copies.append(pltpu.make_async_copy(source, out.at[:, :, x, :], sems.at[len(copies)]))
            copies[-1].start()
    n = len(XP) * depth
    for side, (x, beside) in enumerate(((0, below_buf), (width - 1, above_buf))):
        rows = slice(side * layers, (side + 1) * layers)
        plate_buf[side] = rows_plate[rows, :] + diffusion * beside[n : n + layers, :]
        copies.append(pltpu.make_async_copy(plate_buf.at[side], out_plate.at[:, x, :], sems.at[len(copies)]))
        copies[-1].start()
    for copy in copies:
        copy.wait()


def kernel_call(body, outs, spaces, name, cost, out_spaces=None, scratch=(), aliases=None):
    return pl.pallas_call(
        body,
        out_shape=outs,
        in_specs=[pl.BlockSpec(memory_space=space) for space in spaces],
        out_specs=[
            pl.BlockSpec(memory_space=space) for space in (out_spaces or [pltpu.VMEM] * len(outs))
        ],
        scratch_shapes=scratch,
        input_output_aliases=aliases or {},
        compiler_params=pltpu.CompilerParams(vmem_limit_bytes=VMEM_LIMIT),
        cost_estimate=pl.CostEstimate(flops=0, bytes_accessed=cost, transcendentals=0),
        name=name,
    )


def local(pop_flow, pop_heat, flags, nozzle_id, jet_velocity, cot_flow, cot_heat, cot_plate):
    nxt, nyt, nzt = (rounds(lax.axis_size(a)) for a in AXES)
    _, depth, width, length = cot_flow.shape
    layers = cot_plate.shape[0]
    f32 = jnp.float32
    array = lambda *shape: jax.ShapeDtypeStruct(shape, f32)
    vmem, hbm = pltpu.VMEM, pltpu.HBM
    cots = (cot_flow, cot_heat, cot_plate)
    side = padded(len(XM) * depth + layers)

    faces = kernel_call(
        functools.partial(pack_faces, nzt),
        [array((len(ZM) + 1) * width, length)] * nzt,
        [hbm] * 3,
        "faces",
        1 << 20,
        scratch=[pltpu.SemaphoreType.DMA((nzt, len(ZM) + 1))],
    )(*(pltpu.with_memory_space_constraint(c, hbm) for c in cots))
    z_in = [swap(v, gz=t) for t, v in enumerate(faces)]
    columns = kernel_call(
        functools.partial(pack_columns, nyt),
        [array(width + YPAD[t], length) for t in range(nyt)],
        [vmem] * (3 + nzt),
        "columns",
        1 << 18,
    )(*cots, *faces)
    y_in = [swap(v, gy=t) for t, v in enumerate(columns)]
    ue, ratio, row_values, row_kinds = kernel_call(
        prepare,
        [
            array(3, depth, width, length),
            array(depth, width, length),
            array(4, 2 * depth, length),
            jax.ShapeDtypeStruct((2 * depth, length), jnp.int32),
        ],
        [vmem] * 4 + [pltpu.SMEM] + [vmem] * nyt,
        "prepare",
        2 << 20,
    )(pop_flow, pop_heat, flags, nozzle_id, jet_velocity, *columns)
    edges = kernel_call(
        functools.partial(pack_edges, nyt, nzt, depth, width),
        [array(EDGE_ROWS, length)] * nzt,
        [vmem] * (nyt + 1),
        "edges",
        1 << 16,
    )(*y_in, ratio)
    yz_in = [swap(v, gz=t) for t, v in enumerate(edges)]
    rows = kernel_call(
        functools.partial(pack_rows, nxt, nyt, nzt),
        [array(side + XPAD[t], length) for t in range(nxt)],
        [vmem] * (3 + 2 * nzt + nyt),
        "rows",
        1 << 18,
    )(*cots, *z_in, *y_in, *edges)
    x_in = [swap(v, gx=t) for t, v in enumerate(rows)]
    ends = [array(FLOW, 2 * depth, length), array(HEAT, 2 * depth, length)]
    inner = max(depth - 2, 1)
    *grads, rows_flow, rows_heat, rows_plate = kernel_call(
        functools.partial(interior, False, nyt, nzt),
        [array(*c.shape) for c in cots] + ends + [array(2 * layers, length)],
        [vmem] * (6 + nzt + nyt + nxt),
        "inner",
        2 << 20,
        out_spaces=[hbm] * 3 + [vmem] * 3,
        scratch=[
            pltpu.VMEM((FLOW, inner, width, length), f32),
            pltpu.VMEM((HEAT, inner, width, length), f32),
            pltpu.VMEM(cot_plate.shape, f32),
            pltpu.SemaphoreType.DMA((2 * depth + 1,)),
        ],
    )(flags, ue, ratio, *cots, *z_in, *y_in, *rows)
    given = 6 + 2 * nzt + nyt
    flow, heat, outer_flow, outer_heat = kernel_call(
        functools.partial(interior, True, nyt, nzt),
        [array(*c.shape) for c in cots[:2]] + ends,
        [vmem] * given + [hbm] * 2,
        "outer",
        2 << 20,
        out_spaces=[hbm] * 2 + [vmem] * 2,
        scratch=[
            pltpu.VMEM((FLOW, 2, width, length), f32),
            pltpu.VMEM((HEAT, 2, width, length), f32),
            pltpu.SemaphoreType.DMA((4,)),
        ],
        aliases={given: 0, given + 1: 1},
    )(flags, ue, ratio, *cots, *z_in, *y_in, *yz_in, *grads[:2])
    return tuple(
        kernel_call(
            functools.partial(finish, nxt),
            [array(*c.shape) for c in cots],
            [vmem] * (7 + nxt) + [hbm] * 3,
            "finish",
            1 << 20,
            out_spaces=[hbm] * 3,
            scratch=[
                pltpu.VMEM((side, length), f32),
                pltpu.VMEM((side, length), f32),
                pltpu.VMEM((FLOW + HEAT, 2 * depth, length), f32),
                pltpu.VMEM((FLOW, 2 * depth, length), f32),
                pltpu.VMEM((HEAT, 2 * depth, length), f32),
                pltpu.VMEM((2, layers, length), f32),
                pltpu.SemaphoreType.DMA((6,)),
            ],
            aliases={7 + nxt + i: i for i in range(3)},
        )(row_values, row_kinds, rows_flow, rows_heat, rows_plate, outer_flow, outer_heat, *x_in, flow, heat, grads[2])
    )


def solution(mesh):
    return jax.shard_map(
        local,
        mesh=mesh,
        in_specs=(
            P(None, "gz", "gx", "gy"),
            P(None, "gz", "gx", "gy"),
            P("gz", "gx", "gy"),
            P("gx", "gy"),
            P(),
            P(None, "gz", "gx", "gy"),
            P(None, "gz", "gx", "gy"),
            P("gz", "gx", "gy"),
        ),
        out_specs=(P(None, "gz", "gx", "gy"), P(None, "gz", "gx", "gy"), P("gz", "gx", "gy")),
        check_vma=False,
    )
```

```python
import functools

import jax
import jax.numpy as jnp
from jax import lax
from jax.experimental import pallas as pl
from jax.experimental.pallas import tpu as pltpu
from jax.sharding import PartitionSpec as P

VELOCITY = (
    (0, 0, 0),
    (1, 0, 0),
    (-1, 0, 0),
    (0, 1, 0),
    (0, -1, 0),
    (0, 0, 1),
    (0, 0, -1),
    (1, 1, 0),
    (-1, -1, 0),
    (1, -1, 0),
    (-1, 1, 0),
    (1, 0, 1),
    (-1, 0, -1),
    (1, 0, -1),
    (-1, 0, 1),
    (0, 1, 1),
    (0, -1, -1),
    (0, 1, -1),
    (0, -1, 1),
)
OPPOSITE = tuple((VELOCITY.index((-a, -b, -c)) for a, b, c in VELOCITY))
WEIGHTS_FLOW = (1.0 / 3.0,) + (1.0 / 18.0,) * 6 + (1.0 / 36.0,) * 12
WEIGHTS_HEAT = (0.25,) + (0.125,) * 6
FLOW = 19
HEAT = 7
DIRECTIONS = VELOCITY + VELOCITY[:HEAT]
tau_flow = 0.8
tau_heat = 0.9
diffusion = 0.12
coupling = 0.3

AXES = ("gx", "gy", "gz")
COMPONENT = {"gx": 0, "gy": 1, "gz": 2}
VMEM_LIMIT = 8 << 20
YZ_ROWS = 48
YPAD = (0, 0)
XPAD = (0, 0)


def moving(component, sign):
    return [k for k, c in enumerate(DIRECTIONS) if c[component] == sign]


XP, XM = moving(0, 1), moving(0, -1)
YP, YM = moving(1, 1), moving(1, -1)
ZP, ZM = moving(2, 1), moving(2, -1)


def rounds(size):
    return 1 if size == 2 else 2


def swap(value, **turns):
    sizes = [lax.axis_size(name) for name in AXES]
    flat = lambda p: (p[0] * sizes[1] + p[1]) * sizes[2] + p[2]
    pairs = []
    for a in range(sizes[0]):
        for b in range(sizes[1]):
            for c in range(sizes[2]):
                here = [a, b, c]
                there = [a, b, c]
                for axis, turn in turns.items():
                    at = AXES.index(axis)
                    i = here[at]
                    there[at] = i ^ 1 if turn == 0 else (i + 1 if i % 2 else i - 1)
                if not all(0 <= t < n for t, n in zip(there, sizes)):
                    there = [a, sizes[1] - 1 - b if "gy" in turns else b ^ 1, c]
                pairs.append((flat(here), flat(there)))
    return lax.ppermute(value, AXES, pairs)


def place(axis):
    i = lax.axis_index(axis)
    return lax.rem(i, 2) == 0, i < lax.axis_size(axis) - 1, i > 0


def outgoing(axis, turn, to_higher, to_lower):
    even, _, _ = place(axis)
    return jnp.where(even, to_higher, to_lower) if turn == 0 else jnp.where(even, to_lower, to_higher)


def incoming(axis, turns):
    even, higher, lower = place(axis)
    first, last = turns[0], turns[-1]
    zero = jnp.zeros_like(first)
    above = jnp.where(higher, jnp.where(even, first, last), zero)
    below = jnp.where(lower, jnp.where(even, last, first), zero)
    return above, below


def slab(cot_flow, cot_heat, k, z):
    return cot_flow[k, z] if k < FLOW else cot_heat[k - FLOW, z]


def row_of(cot_flow, cot_heat, k, z, x):
    return cot_flow[k, z, x : x + 1, :] if k < FLOW else cot_heat[k - FLOW, z, x : x + 1, :]


def padded(rows):
    return -(-rows // 8) * 8


def turned(plane, by):
    by %= plane.shape[1]
    return pltpu.roll(plane, by, 1) if by else plane


def column_lane(n, z, depth):
    return n * depth + z


def plate_lane(l, depth):
    return column_lane(len(YM), 0, depth) + l


def shift_lanes(plane, sign, halo, lane):
    y = lax.broadcasted_iota(jnp.int32, plane.shape, 1)
    edge = plane.shape[1] - 1 if sign == 1 else 0
    return jnp.where(y == edge, turned(halo, edge - lane), turned(plane, -sign))


def shift_rows(plane, sign):
    width = plane.shape[0]
    x = lax.broadcasted_iota(jnp.int32, plane.shape, 0)
    edge = width - 1 if sign == 1 else 0
    return jnp.where(x == edge, 0.0, pltpu.roll(plane, -sign % width, 0))


def pack_faces(nzt, cot_flow, cot_heat, cot_plate, *refs):
    outs, sems = refs[:nzt], refs[nzt]
    depth, width = cot_flow.shape[1], cot_flow.shape[2]
    layers = cot_plate.shape[0]
    even, _, _ = place("gz")
    copies = []
    for turn in range(nzt):
        up = even if turn == 0 else jnp.logical_not(even)
        z = jnp.where(up, depth - 1, 0)
        sources = []
        for hi, lo in zip(ZM, ZP):
            ref, skip = (cot_flow, 0) if hi < FLOW else (cot_heat, FLOW)
            sources.append(ref.at[jnp.where(up, hi - skip, lo - skip), z])
        sources.append(cot_plate.at[jnp.where(up, layers - 1, 0)])
        for n, source in enumerate(sources):
            target = outs[turn].at[n * width : (n + 1) * width, :]
            copies.append(pltpu.make_async_copy(source, target, sems.at[turn, n]))
            copies[-1].start()
    for copy in copies:
        copy.wait()


def pack_columns(nyt, nzt, cot_flow, cot_heat, cot_plate, *refs):
    outs, yz_outs = refs[-nyt * (nzt + 1) : -nyt * nzt], refs[-nyt * nzt :]
    depth, width, length = cot_flow.shape[1:]
    layers = cot_plate.shape[0]
    y = lax.broadcasted_iota(jnp.int32, (width, length), 1)

    def put(packed, plane, source, lane):
        return jnp.where(y == lane, turned(plane, lane - source), packed)

    packs = []
    for side, source in ((YM, length - 1), (YP, 0)):
        packed = jnp.zeros((width, length), jnp.float32)
        for n, k in enumerate(side):
            for z in range(depth):
                packed = put(
                    packed, slab(cot_flow, cot_heat, k, z), source, column_lane(n, z, depth)
                )
        for l in range(layers):
            packed = put(packed, cot_plate[l], source, plate_lane(l, depth))
        packs.append(packed)
    for turn in range(nyt):
        outs[turn][:width, :] = outgoing("gy", turn, packs[0], packs[1])
        if outs[turn].shape[0] > width:
            outs[turn][width:, :] = jnp.zeros((outs[turn].shape[0] - width, length), jnp.float32)

    def plane(cy, cz):
        k = DIRECTIONS.index((0, cy, cz))
        return slab(cot_flow, cot_heat, k, depth - 1 if cz == -1 else 0)

    for ty in range(nyt):
        for tz in range(nzt):
            out = yz_outs[ty * nzt + tz]
            out[:width, :] = outgoing(
                "gy",
                ty,
                outgoing("gz", tz, plane(-1, -1), plane(-1, 1)),
                outgoing("gz", tz, plane(1, -1), plane(1, 1)),
            )
            if out.shape[0] > width:
                out[width:, :] = jnp.zeros((out.shape[0] - width, length), jnp.float32)


def face_rows(z_in, k, rows):
    up = DIRECTIONS[k][2] == 1
    at = (ZP if up else ZM).index(k) * ((z_in[0].shape[0]) // (len(ZP) + 1))
    above, below = incoming("gz", [r[at + rows.start : at + rows.stop, :] for r in z_in])
    return above if up else below


def pack_rows(nxt, nyt, nzt, cot_flow, cot_heat, cot_plate, *refs):
    z_in, y_in, outs = refs[:nzt], refs[nzt : nzt + nyt], refs[-nxt:]
    depth, width, length = cot_flow.shape[1:]
    layers = cot_plate.shape[0]
    y_above, y_below = incoming("gy", [r[:width, :] for r in y_in])

    def row(k, z, x):
        _, cy, cz = DIRECTIONS[k]
        if 0 <= z + cz < depth:
            value = row_of(cot_flow, cot_heat, k, z + cz, x)
        else:
            value = face_rows(z_in, k, slice(x, x + 1))
        if cy == 0:
            return value
        halo, n = (y_above, YP.index(k)) if cy == 1 else (y_below, YM.index(k))
        return shift_lanes(value, cy, halo[x : x + 1, :], column_lane(n, z, depth))

    used = len(XM) * depth + layers
    for turn in range(nxt):
        if used < outs[turn].shape[0]:
            outs[turn][used:, :] = jnp.zeros((outs[turn].shape[0] - used, length), jnp.float32)
    for n, (hi, lo) in enumerate(zip(XM, XP)):
        for z in range(depth):
            r = n * depth + z
            to_higher, to_lower = row(hi, z, width - 1), row(lo, z, 0)
            for turn in range(nxt):
                outs[turn][r : r + 1, :] = outgoing("gx", turn, to_higher, to_lower)
    for l in range(layers):
        r = len(XM) * depth + l
        for turn in range(nxt):
            outs[turn][r : r + 1, :] = outgoing(
                "gx", turn, cot_plate[l, width - 1 : width, :], cot_plate[l, 0:1, :]
            )


def prepare(pop_flow, pop_heat, flags, nozzle, jet_velocity, *refs):
    ue_out, ratio_out, rows_out, kinds_out = refs[-4:]
    depth, width = flags.shape[:2]
    jets = [jnp.zeros(nozzle.shape, jnp.float32)] * 3
    which = nozzle[...]
    for n in range(jet_velocity.shape[1]):
        hit = which == n
        jets = [jnp.where(hit, jet_velocity[c, n], jets[c]) for c in range(3)]
    for z in range(depth):
        inlet = flags[z] == 2
        pops = [pop_flow[q, z] for q in range(FLOW)]
        rho = sum(pops[1:], pops[0])
        inverse = 1.0 / rho
        values = []
        for c in range(3):
            plus = [pops[q] for q in range(FLOW) if VELOCITY[q][c] == 1]
            minus = [pops[q] for q in range(FLOW) if VELOCITY[q][c] == -1]
            total = sum(plus[1:], plus[0]) - sum(minus[1:], minus[0])
            values.append(jnp.where(inlet, jets[c], total * inverse))
            ue_out[c, z] = values[c]
        heat = [pop_heat[q, z] for q in range(HEAT)]
        values.append(sum(heat[1:], heat[0]) * inverse)
        ratio_out[z] = values[3]
        for side, x in enumerate((0, width - 1)):
            r = side * depth + z
            for c in range(4):
                rows_out[c, r : r + 1, :] = values[c][x : x + 1, :]
            kinds_out[r : r + 1, :] = flags[z, x : x + 1, :]


def collide_back(s, t, ue, ratio, wall, inlet):
    add = lambda a, b: b if a is None else a + b
    zero_moment = WEIGHTS_FLOW[0] * s[0]
    first = [None] * 3
    second = {}
    for group, weight in ((range(1, 7), WEIGHTS_FLOW[1]), (range(7, 19), WEIGHTS_FLOW[7])):
        odd = [None] * 3
        even = {}
        total = None
        for q in group:
            o = OPPOSITE[q]
            if o < q:
                continue
            c = VELOCITY[q]
            plus, minus = s[q] + s[o], s[q] - s[o]
            total = add(total, plus)
            for i in range(3):
                if c[i]:
                    odd[i] = add(odd[i], minus if c[i] == 1 else -minus)
                for j in range(i, 3):
                    if c[i] * c[j]:
                        even[i, j] = add(even.get((i, j)), plus if c[i] * c[j] == 1 else -plus)
        zero_moment = zero_moment + weight * total
        for i in range(3):
            first[i] = add(first[i], weight * odd[i])
        for key, value in even.items():
            second[key] = add(second.get(key), weight * value)
    heat_first = [WEIGHTS_HEAT[1] * (t[2 * c + 1] - t[2 * c + 2]) for c in range(3)]
    heat_zero = WEIGHTS_HEAT[0] * t[0] + WEIGHTS_HEAT[1] * (
        (t[1] + t[2]) + (t[3] + t[4]) + (t[5] + t[6])
    )
    dot = lambda a, b: a[0] * b[0] + a[1] * b[1] + a[2] * b[2]
    bent = [sum(second[min(i, j), max(i, j)] * ue[j] for j in range(3)) for i in range(3)]
    gain = zero_moment * (1.0 - 1.5 * dot(ue, ue)) + 3.0 * dot(first, ue) + 4.5 * dot(bent, ue)
    pull = [
        (3.0 / tau_flow) * (first[i] + 3.0 * bent[i] - ue[i] * zero_moment)
        + (4.0 / tau_heat) * ratio * heat_first[i]
        for i in range(3)
    ]
    common = jnp.where(inlet, gain, (1.0 / tau_flow) * gain - dot(ue, pull))
    pull = [jnp.where(inlet, 0.0, p) for p in pull]
    keep = jnp.where(inlet, 0.0, 1.0 - 1.0 / tau_flow)
    flow = []
    for q in range(FLOW):
        value = keep * s[q] + common
        for i in range(3):
            if VELOCITY[q][i] == 1:
                value = value + pull[i]
            elif VELOCITY[q][i] == -1:
                value = value - pull[i]
        flow.append(jnp.where(wall, s[OPPOSITE[q]], value))
    heat_common = jnp.where(inlet, 0.0, (1.0 / tau_heat) * (heat_zero + 4.0 * dot(heat_first, ue)))
    heat_keep = jnp.where(inlet, 0.0, 1.0 - 1.0 / tau_heat)
    heat = [
        jnp.where(wall, t[OPPOSITE[q]], heat_keep * t[q] + heat_common) for q in range(HEAT)
    ]
    return flow, heat


def interior(nyt, nzt, flags, ue_in, ratio_in, cot_flow, cot_heat, cot_plate, *refs):
    z_in, y_in, yz_in = refs[:nzt], refs[nzt : nzt + nyt], refs[nzt + nyt : nzt + nyt + nyt * nzt]
    out_flow, out_heat, out_plate, rows_flow, rows_heat, rows_plate = refs[-10:-4]
    flow_buf, heat_buf, plate_buf, sems = refs[-4:]
    depth, width = cot_flow.shape[1], cot_flow.shape[2]
    layers = cot_plate.shape[0]
    base = lax.axis_index("gz") == 0
    y_above, y_below = incoming("gy", [r[:width, :] for r in y_in])
    sides = [incoming("gy", [r[:width, :] for r in yz_in[tz::nzt]]) for tz in range(nzt)]
    yz = {1: incoming("gz", [side[0] for side in sides]), -1: incoming("gz", [side[1] for side in sides])}
    copies = []

    def send(source, target):
        copies.append(pltpu.make_async_copy(source, target, sems.at[len(copies)]))
        copies[-1].start()

    z_above = z_below = None
    z_rows = slice(len(ZP) * width, (len(ZP) + 1) * width)
    z_above, z_below = incoming("gz", [r[z_rows, :] for r in z_in])
    for l in range(layers):
        own = cot_plate[l]
        up = cot_plate[l + 1] if l + 1 < layers else z_above
        down = cot_plate[l - 1] if l > 0 else z_below
        total = up + down + shift_rows(own, 1) + shift_rows(own, -1)
        total = total + shift_lanes(own, 1, y_above, plate_lane(l, depth))
        total = total + shift_lanes(own, -1, y_below, plate_lane(l, depth))
        value = own + diffusion * (total - 6.0 * own)
        if l == 0:
            value = value + jnp.where(base, 0.25 * cot_heat[5, 0] - coupling * own, 0.0)
        plate_buf[l] = value
        rows_plate[l : l + 1, :] = value[0:1, :]
        rows_plate[layers + l : layers + l + 1, :] = value[width - 1 : width, :]
    send(plate_buf, out_plate)

    for z in range(depth):
        star = []
        for k, (cx, cy, cz) in enumerate(DIRECTIONS):
            at = z + cz
            inside = 0 <= at < depth
            plane = slab(cot_flow, cot_heat, k, at) if inside else face_rows(z_in, k, slice(0, width))
            if cy:
                halo, n = (y_above, YP.index(k)) if cy == 1 else (y_below, YM.index(k))
                if inside:
                    plane = shift_lanes(plane, cy, halo, column_lane(n, at, depth))
                else:
                    lane = 0 if cy == 1 else plane.shape[1] - 1
                    plane = shift_lanes(plane, cy, yz[cy][0 if cz == 1 else 1], lane)
            if cx:
                plane = shift_rows(plane, cx)
            if cz == -1 and z == 0:
                if k < FLOW:
                    bounced = cot_flow[OPPOSITE[k], 0]
                else:
                    bounced = -cot_heat[OPPOSITE[k - FLOW], 0]
                plane = jnp.where(base, bounced, plane)
            star.append(plane)
        kind = flags[z]
        flow, heat = collide_back(
            star[:FLOW], star[FLOW:], [ue_in[c, z] for c in range(3)], ratio_in[z], kind == 1, kind == 2
        )
        if z == 0:
            source = jnp.where(base, coupling * cot_plate[0], 0.0)
            heat = [value + source for value in heat]
        for values, buf, rows in ((flow, flow_buf, rows_flow), (heat, heat_buf, rows_heat)):
            for q, value in enumerate(values):
                buf[q, z] = value
                rows[q, z : z + 1, :] = value[0:1, :]
                rows[q, depth + z : depth + z + 1, :] = value[width - 1 : width, :]
        send(flow_buf.at[:, z], out_flow.at[:, z])
        send(heat_buf.at[:, z], out_heat.at[:, z])
    for copy in copies:
        copy.wait()


def finish(nxt, rows_in, kinds, rows_flow, rows_heat, rows_plate, *refs):
    x_in, refs = refs[:nxt], refs[nxt + 3 :]
    out_flow, out_heat, out_plate, above_buf, below_buf, star_buf, flow_buf, heat_buf, plate_buf, sems = refs
    depth, width = out_flow.shape[1], out_flow.shape[2]
    layers = out_plate.shape[0]
    used = above_buf.shape[0]
    above, below = incoming("gx", [r[:used, :] for r in x_in])
    above_buf[...] = above
    below_buf[...] = below
    zero = jnp.zeros((2 * depth, above.shape[1]), jnp.float32)
    star = []
    for k, c in enumerate(DIRECTIONS):
        if c[0] == 0:
            star.append(zero)
            continue
        star_buf[k] = zero
        if c[0] == 1:
            n = XP.index(k) * depth
            star_buf[k, depth:, :] = above_buf[n : n + depth, :]
        else:
            n = XM.index(k) * depth
            star_buf[k, :depth, :] = below_buf[n : n + depth, :]
        star.append(star_buf[k])
    kind = kinds[...]
    flow, heat = collide_back(
        star[:FLOW], star[FLOW:], [rows_in[c] for c in range(3)], rows_in[3], kind == 1, kind == 2
    )
    copies = []
    for values, rows, buf, out in (
        (flow, rows_flow, flow_buf, out_flow),
        (heat, rows_heat, heat_buf, out_heat),
    ):
        for q, value in enumerate(values):
            buf[q] = rows[q] + value
        for side, x in enumerate((0, width - 1)):
            source = buf.at[:, side * depth : (side + 1) * depth, :]
            copies.append(pltpu.make_async_copy(source, out.at[:, :, x, :], sems.at[len(copies)]))
            copies[-1].start()
    n = len(XP) * depth
    for side, (x, beside) in enumerate(((0, below_buf), (width - 1, above_buf))):
        rows = slice(side * layers, (side + 1) * layers)
        plate_buf[side] = rows_plate[rows, :] + diffusion * beside[n : n + layers, :]
        copies.append(pltpu.make_async_copy(plate_buf.at[side], out_plate.at[:, x, :], sems.at[len(copies)]))
        copies[-1].start()
    for copy in copies:
        copy.wait()


def kernel_call(body, outs, spaces, name, cost, out_spaces=None, scratch=(), aliases=None):
    return pl.pallas_call(
        body,
        out_shape=outs,
        in_specs=[pl.BlockSpec(memory_space=space) for space in spaces],
        out_specs=[
            pl.BlockSpec(memory_space=space) for space in (out_spaces or [pltpu.VMEM] * len(outs))
        ],
        scratch_shapes=scratch,
        input_output_aliases=aliases or {},
        compiler_params=pltpu.CompilerParams(vmem_limit_bytes=VMEM_LIMIT),
        cost_estimate=pl.CostEstimate(flops=0, bytes_accessed=cost, transcendentals=0),
        name=name,
    )


def local(pop_flow, pop_heat, flags, nozzle_id, jet_velocity, cot_flow, cot_heat, cot_plate):
    nxt, nyt, nzt = (rounds(lax.axis_size(a)) for a in AXES)
    _, depth, width, length = cot_flow.shape
    layers = cot_plate.shape[0]
    f32 = jnp.float32
    array = lambda *shape: jax.ShapeDtypeStruct(shape, f32)
    vmem, hbm = pltpu.VMEM, pltpu.HBM
    cots = (cot_flow, cot_heat, cot_plate)
    side = padded(len(XM) * depth + layers)

    faces = kernel_call(
        functools.partial(pack_faces, nzt),
        [array((len(ZM) + 1) * width, length)] * nzt,
        [hbm] * 3,
        "faces",
        1 << 20,
        scratch=[pltpu.SemaphoreType.DMA((nzt, len(ZM) + 1))],
    )(*(pltpu.with_memory_space_constraint(c, hbm) for c in cots))
    z_in = [swap(v, gz=t) for t, v in enumerate(faces)]
    columns = kernel_call(
        functools.partial(pack_columns, nyt, nzt),
        [array(width + YPAD[t], length) for t in range(nyt)] + [array(YZ_ROWS, length)] * (nyt * nzt),
        [vmem] * (3 + nzt),
        "columns",
        1 << 18,
    )(*cots, *faces)
    y_in = [swap(v, gy=t) for t, v in enumerate(columns[:nyt])]
    yz_in = [swap(columns[nyt + ty * nzt + tz], gy=ty, gz=tz) for ty in range(nyt) for tz in range(nzt)]
    rows = kernel_call(
        functools.partial(pack_rows, nxt, nyt, nzt),
        [array(side + XPAD[t], length) for t in range(nxt)],
        [vmem] * (3 + nzt + nyt),
        "rows",
        1 << 18,
    )(*cots, *z_in, *y_in)
    x_in = [swap(v, gx=t) for t, v in enumerate(rows)]
    ue, ratio, row_values, row_kinds = kernel_call(
        prepare,
        [
            array(3, depth, width, length),
            array(depth, width, length),
            array(4, 2 * depth, length),
            jax.ShapeDtypeStruct((2 * depth, length), jnp.int32),
        ],
        [vmem] * 4 + [pltpu.SMEM] + [vmem] * nxt,
        "prepare",
        2 << 20,
    )(pop_flow, pop_heat, flags, nozzle_id, jet_velocity, *rows)
    *grads, rows_flow, rows_heat, rows_plate = kernel_call(
        functools.partial(interior, nyt, nzt),
        [array(*c.shape) for c in cots]
        + [array(FLOW, 2 * depth, length), array(HEAT, 2 * depth, length), array(2 * layers, length)],
        [vmem] * (6 + nzt + nyt + nyt * nzt),
        "interior",
        4 << 20,
        out_spaces=[hbm] * 3 + [vmem] * 3,
        scratch=[pltpu.VMEM(c.shape, f32) for c in cots] + [pltpu.SemaphoreType.DMA((2 * depth + 1,))],
    )(flags, ue, ratio, *cots, *z_in, *y_in, *yz_in)
    return tuple(
        kernel_call(
            functools.partial(finish, nxt),
            [array(*c.shape) for c in cots],
            [vmem] * (5 + nxt) + [hbm] * 3,
            "finish",
            1 << 20,
            out_spaces=[hbm] * 3,
            scratch=[
                pltpu.VMEM((side, length), f32),
                pltpu.VMEM((side, length), f32),
                pltpu.VMEM((FLOW + HEAT, 2 * depth, length), f32),
                pltpu.VMEM((FLOW, 2 * depth, length), f32),
                pltpu.VMEM((HEAT, 2 * depth, length), f32),
                pltpu.VMEM((2, layers, length), f32),
                pltpu.SemaphoreType.DMA((6,)),
            ],
            aliases={5 + nxt + i: i for i in range(3)},
        )(row_values, row_kinds, rows_flow, rows_heat, rows_plate, *x_in, *grads)
    )


def solution(mesh):
    return jax.shard_map(
        local,
        mesh=mesh,
        in_specs=(
            P(None, "gz", "gx", "gy"),
            P(None, "gz", "gx", "gy"),
            P("gz", "gx", "gy"),
            P("gx", "gy"),
            P(),
            P(None, "gz", "gx", "gy"),
            P(None, "gz", "gx", "gy"),
            P("gz", "gx", "gy"),
        ),
        out_specs=(P(None, "gz", "gx", "gy"), P(None, "gz", "gx", "gy"), P("gz", "gx", "gy")),
        check_vma=False,
    )
```

```python
import functools

import jax
import jax.numpy as jnp
from jax import lax
from jax.experimental import pallas as pl
from jax.experimental.pallas import tpu as pltpu
from jax.sharding import PartitionSpec as P

VELOCITY = (
    (0, 0, 0),
    (1, 0, 0),
    (-1, 0, 0),
    (0, 1, 0),
    (0, -1, 0),
    (0, 0, 1),
    (0, 0, -1),
    (1, 1, 0),
    (-1, -1, 0),
    (1, -1, 0),
    (-1, 1, 0),
    (1, 0, 1),
    (-1, 0, -1),
    (1, 0, -1),
    (-1, 0, 1),
    (0, 1, 1),
    (0, -1, -1),
    (0, 1, -1),
    (0, -1, 1),
)
OPPOSITE = tuple((VELOCITY.index((-a, -b, -c)) for a, b, c in VELOCITY))
WEIGHTS_FLOW = (1.0 / 3.0,) + (1.0 / 18.0,) * 6 + (1.0 / 36.0,) * 12
WEIGHTS_HEAT = (0.25,) + (0.125,) * 6
FLOW = 19
HEAT = 7
DIRECTIONS = VELOCITY + VELOCITY[:HEAT]
tau_flow = 0.8
tau_heat = 0.9
diffusion = 0.12
coupling = 0.3

AXES = ("gx", "gy", "gz")
COMPONENT = {"gx": 0, "gy": 1, "gz": 2}
VMEM_LIMIT = 8 << 20
YZ_ROWS = 48
YPAD = (0, 8)


def moving(component, sign):
    return [k for k, c in enumerate(DIRECTIONS) if c[component] == sign]


XP, XM = moving(0, 1), moving(0, -1)
YP, YM = moving(1, 1), moving(1, -1)
ZP, ZM = moving(2, 1), moving(2, -1)


def rounds(size):
    return 1 if size == 2 else 2


def swap(value, **turns):
    sizes = [lax.axis_size(name) for name in AXES]
    flat = lambda p: (p[0] * sizes[1] + p[1]) * sizes[2] + p[2]
    pairs = []
    for a in range(sizes[0]):
        for b in range(sizes[1]):
            for c in range(sizes[2]):
                here = [a, b, c]
                there = [a, b, c]
                for axis, turn in turns.items():
                    at = AXES.index(axis)
                    i = here[at]
                    there[at] = i ^ 1 if turn == 0 else (i + 1 if i % 2 else i - 1)
                if not all(0 <= t < n for t, n in zip(there, sizes)):
                    there = [a, sizes[1] - 1 - b if "gy" in turns else b ^ 1, c]
                pairs.append((flat(here), flat(there)))
    return lax.ppermute(value, AXES, pairs)


def place(axis):
    i = lax.axis_index(axis)
    return lax.rem(i, 2) == 0, i < lax.axis_size(axis) - 1, i > 0


def outgoing(axis, turn, to_higher, to_lower):
    even, _, _ = place(axis)
    return jnp.where(even, to_higher, to_lower) if turn == 0 else jnp.where(even, to_lower, to_higher)


def incoming(axis, turns):
    even, higher, lower = place(axis)
    first, last = turns[0], turns[-1]
    zero = jnp.zeros_like(first)
    above = jnp.where(higher, jnp.where(even, first, last), zero)
    below = jnp.where(lower, jnp.where(even, last, first), zero)
    return above, below


def slab(cot_flow, cot_heat, k, z):
    return cot_flow[k, z] if k < FLOW else cot_heat[k - FLOW, z]


def row_of(cot_flow, cot_heat, k, z, x):
    return cot_flow[k, z, x : x + 1, :] if k < FLOW else cot_heat[k - FLOW, z, x : x + 1, :]


def padded(rows):
    return -(-rows // 8) * 8


def turned(plane, by):
    by %= plane.shape[1]
    return pltpu.roll(plane, by, 1) if by else plane


def column_lane(n, z, depth):
    return n * depth + z


def plate_lane(l, depth):
    return column_lane(len(YM), 0, depth) + l


def shift_lanes(plane, sign, halo, lane):
    y = lax.broadcasted_iota(jnp.int32, plane.shape, 1)
    edge = plane.shape[1] - 1 if sign == 1 else 0
    return jnp.where(y == edge, turned(halo, edge - lane), turned(plane, -sign))


def shift_rows(plane, sign):
    width = plane.shape[0]
    x = lax.broadcasted_iota(jnp.int32, plane.shape, 0)
    edge = width - 1 if sign == 1 else 0
    return jnp.where(x == edge, 0.0, pltpu.roll(plane, -sign % width, 0))


def pack_faces(nzt, cot_flow, cot_heat, cot_plate, *refs):
    outs, sems = refs[:nzt], refs[nzt]
    depth, width = cot_flow.shape[1], cot_flow.shape[2]
    layers = cot_plate.shape[0]
    even, _, _ = place("gz")
    copies = []
    for turn in range(nzt):
        up = even if turn == 0 else jnp.logical_not(even)
        z = jnp.where(up, depth - 1, 0)
        sources = []
        for hi, lo in zip(ZM, ZP):
            ref, skip = (cot_flow, 0) if hi < FLOW else (cot_heat, FLOW)
            sources.append(ref.at[jnp.where(up, hi - skip, lo - skip), z])
        sources.append(cot_plate.at[jnp.where(up, layers - 1, 0)])
        for n, source in enumerate(sources):
            target = outs[turn].at[n * width : (n + 1) * width, :]
            copies.append(pltpu.make_async_copy(source, target, sems.at[turn, n]))
            copies[-1].start()
    for copy in copies:
        copy.wait()


def pack_columns(nyt, nzt, cot_flow, cot_heat, cot_plate, *refs):
    outs, yz_outs = refs[-nyt * (nzt + 1) : -nyt * nzt], refs[-nyt * nzt :]
    depth, width, length = cot_flow.shape[1:]
    layers = cot_plate.shape[0]
    y = lax.broadcasted_iota(jnp.int32, (width, length), 1)

    def put(packed, plane, source, lane):
        return jnp.where(y == lane, turned(plane, lane - source), packed)

    packs = []
    for side, source in ((YM, length - 1), (YP, 0)):
        packed = jnp.zeros((width, length), jnp.float32)
        for n, k in enumerate(side):
            for z in range(depth):
                packed = put(
                    packed, slab(cot_flow, cot_heat, k, z), source, column_lane(n, z, depth)
                )
        for l in range(layers):
            packed = put(packed, cot_plate[l], source, plate_lane(l, depth))
        packs.append(packed)
    for turn in range(nyt):
        outs[turn][:width, :] = outgoing("gy", turn, packs[0], packs[1])
        if outs[turn].shape[0] > width:
            outs[turn][width:, :] = jnp.zeros((outs[turn].shape[0] - width, length), jnp.float32)

    def plane(cy, cz):
        k = DIRECTIONS.index((0, cy, cz))
        return slab(cot_flow, cot_heat, k, depth - 1 if cz == -1 else 0)

    for ty in range(nyt):
        for tz in range(nzt):
            out = yz_outs[ty * nzt + tz]
            out[:width, :] = outgoing(
                "gy",
                ty,
                outgoing("gz", tz, plane(-1, -1), plane(-1, 1)),
                outgoing("gz", tz, plane(1, -1), plane(1, 1)),
            )
            if out.shape[0] > width:
                out[width:, :] = jnp.zeros((out.shape[0] - width, length), jnp.float32)


def face_rows(z_in, k, rows):
    up = DIRECTIONS[k][2] == 1
    at = (ZP if up else ZM).index(k) * ((z_in[0].shape[0]) // (len(ZP) + 1))
    above, below = incoming("gz", [r[at + rows.start : at + rows.stop, :] for r in z_in])
    return above if up else below


def pack_rows(nxt, nyt, nzt, cot_flow, cot_heat, cot_plate, *refs):
    z_in, y_in, outs = refs[:nzt], refs[nzt : nzt + nyt], refs[-nxt:]
    depth, width, length = cot_flow.shape[1:]
    layers = cot_plate.shape[0]
    y_above, y_below = incoming("gy", [r[:width, :] for r in y_in])

    def row(k, z, x):
        _, cy, cz = DIRECTIONS[k]
        if 0 <= z + cz < depth:
            value = row_of(cot_flow, cot_heat, k, z + cz, x)
        else:
            value = face_rows(z_in, k, slice(x, x + 1))
        if cy == 0:
            return value
        halo, n = (y_above, YP.index(k)) if cy == 1 else (y_below, YM.index(k))
        return shift_lanes(value, cy, halo[x : x + 1, :], column_lane(n, z, depth))

    used = len(XM) * depth + layers
    for turn in range(nxt):
        if used < outs[turn].shape[0]:
            outs[turn][used:, :] = jnp.zeros((outs[turn].shape[0] - used, length), jnp.float32)
    for n, (hi, lo) in enumerate(zip(XM, XP)):
        for z in range(depth):
            r = n * depth + z
            to_higher, to_lower = row(hi, z, width - 1), row(lo, z, 0)
            for turn in range(nxt):
                outs[turn][r : r + 1, :] = outgoing("gx", turn, to_higher, to_lower)
    for l in range(layers):
        r = len(XM) * depth + l
        for turn in range(nxt):
            outs[turn][r : r + 1, :] = outgoing(
                "gx", turn, cot_plate[l, width - 1 : width, :], cot_plate[l, 0:1, :]
            )


def prepare(pop_flow, pop_heat, flags, nozzle, jet_velocity, *refs):
    ue_out, ratio_out, rows_out, kinds_out = refs[-4:]
    depth, width = flags.shape[:2]
    which = nozzle[...]
    table = jet_velocity[...]
    fill = jnp.zeros((3, which.shape[1] - table.shape[1]), jnp.float32)
    table = jnp.concatenate([table, fill], axis=1)
    jets = [
        jnp.concatenate(
            [
                jnp.take_along_axis(
                    jnp.broadcast_to(table[c : c + 1, :], (8, which.shape[1])), which[x : x + 8, :], axis=1
                )
                for x in range(0, width, 8)
            ],
            axis=0,
        )
        for c in range(3)
    ]
    for z in range(depth):
        inlet = flags[z] == 2
        pops = [pop_flow[q, z] for q in range(FLOW)]
        rho = sum(pops[1:], pops[0])
        inverse = 1.0 / rho
        values = []
        for c in range(3):
            plus = [pops[q] for q in range(FLOW) if VELOCITY[q][c] == 1]
            minus = [pops[q] for q in range(FLOW) if VELOCITY[q][c] == -1]
            total = sum(plus[1:], plus[0]) - sum(minus[1:], minus[0])
            values.append(jnp.where(inlet, jets[c], total * inverse))
            ue_out[c, z] = values[c]
        heat = [pop_heat[q, z] for q in range(HEAT)]
        values.append(sum(heat[1:], heat[0]) * inverse)
        ratio_out[z] = values[3]
        for side, x in enumerate((0, width - 1)):
            r = side * depth + z
            for c in range(4):
                rows_out[c, r : r + 1, :] = values[c][x : x + 1, :]
            kinds_out[r : r + 1, :] = flags[z, x : x + 1, :]


def collide_back(s, t, ue, ratio, wall, inlet):
    add = lambda a, b: b if a is None else a + b
    zero_moment = WEIGHTS_FLOW[0] * s[0]
    first = [None] * 3
    second = {}
    for group, weight in ((range(1, 7), WEIGHTS_FLOW[1]), (range(7, 19), WEIGHTS_FLOW[7])):
        odd = [None] * 3
        even = {}
        total = None
        for q in group:
            o = OPPOSITE[q]
            if o < q:
                continue
            c = VELOCITY[q]
            plus, minus = s[q] + s[o], s[q] - s[o]
            total = add(total, plus)
            for i in range(3):
                if c[i]:
                    odd[i] = add(odd[i], minus if c[i] == 1 else -minus)
                for j in range(i, 3):
                    if c[i] * c[j]:
                        even[i, j] = add(even.get((i, j)), plus if c[i] * c[j] == 1 else -plus)
        zero_moment = zero_moment + weight * total
        for i in range(3):
            first[i] = add(first[i], weight * odd[i])
        for key, value in even.items():
            second[key] = add(second.get(key), weight * value)
    heat_first = [WEIGHTS_HEAT[1] * (t[2 * c + 1] - t[2 * c + 2]) for c in range(3)]
    heat_zero = WEIGHTS_HEAT[0] * t[0] + WEIGHTS_HEAT[1] * (
        (t[1] + t[2]) + (t[3] + t[4]) + (t[5] + t[6])
    )
    dot = lambda a, b: a[0] * b[0] + a[1] * b[1] + a[2] * b[2]
    bent = [sum(second[min(i, j), max(i, j)] * ue[j] for j in range(3)) for i in range(3)]
    gain = zero_moment * (1.0 - 1.5 * dot(ue, ue)) + 3.0 * dot(first, ue) + 4.5 * dot(bent, ue)
    pull = [
        (3.0 / tau_flow) * (first[i] + 3.0 * bent[i] - ue[i] * zero_moment)
        + (4.0 / tau_heat) * ratio * heat_first[i]
        for i in range(3)
    ]
    common = jnp.where(inlet, gain, (1.0 / tau_flow) * gain - dot(ue, pull))
    pull = [jnp.where(inlet, 0.0, p) for p in pull]
    keep = jnp.where(inlet, 0.0, 1.0 - 1.0 / tau_flow)
    flow = []
    for q in range(FLOW):
        value = keep * s[q] + common
        for i in range(3):
            if VELOCITY[q][i] == 1:
                value = value + pull[i]
            elif VELOCITY[q][i] == -1:
                value = value - pull[i]
        flow.append(jnp.where(wall, s[OPPOSITE[q]], value))
    heat_common = jnp.where(inlet, 0.0, (1.0 / tau_heat) * (heat_zero + 4.0 * dot(heat_first, ue)))
    heat_keep = jnp.where(inlet, 0.0, 1.0 - 1.0 / tau_heat)
    heat = [
        jnp.where(wall, t[OPPOSITE[q]], heat_keep * t[q] + heat_common) for q in range(HEAT)
    ]
    return flow, heat


def interior(nyt, nzt, flags, ue_in, ratio_in, cot_flow, cot_heat, cot_plate, *refs):
    z_in, y_in, yz_in = refs[:nzt], refs[nzt : nzt + nyt], refs[nzt + nyt : nzt + nyt + nyt * nzt]
    out_flow, out_heat, out_plate, rows_flow, rows_heat, rows_plate = refs[-10:-4]
    flow_buf, heat_buf, plate_buf, sems = refs[-4:]
    depth, width = cot_flow.shape[1], cot_flow.shape[2]
    layers = cot_plate.shape[0]
    base = lax.axis_index("gz") == 0
    y_above, y_below = incoming("gy", [r[:width, :] for r in y_in])
    sides = [incoming("gy", [r[:width, :] for r in yz_in[tz::nzt]]) for tz in range(nzt)]
    yz = {1: incoming("gz", [side[0] for side in sides]), -1: incoming("gz", [side[1] for side in sides])}
    copies = []

    def send(source, target):
        copies.append(pltpu.make_async_copy(source, target, sems.at[len(copies)]))
        copies[-1].start()

    z_above = z_below = None
    z_rows = slice(len(ZP) * width, (len(ZP) + 1) * width)
    z_above, z_below = incoming("gz", [r[z_rows, :] for r in z_in])
    for l in range(layers):
        own = cot_plate[l]
        up = cot_plate[l + 1] if l + 1 < layers else z_above
        down = cot_plate[l - 1] if l > 0 else z_below
        total = up + down + shift_rows(own, 1) + shift_rows(own, -1)
        total = total + shift_lanes(own, 1, y_above, plate_lane(l, depth))
        total = total + shift_lanes(own, -1, y_below, plate_lane(l, depth))
        value = own + diffusion * (total - 6.0 * own)
        if l == 0:
            value = value + jnp.where(base, 0.25 * cot_heat[5, 0] - coupling * own, 0.0)
        plate_buf[l] = value
        rows_plate[l : l + 1, :] = value[0:1, :]
        rows_plate[layers + l : layers + l + 1, :] = value[width - 1 : width, :]
    send(plate_buf, out_plate)

    for z in range(depth):
        star = []
        for k, (cx, cy, cz) in enumerate(DIRECTIONS):
            at = z + cz
            inside = 0 <= at < depth
            plane = slab(cot_flow, cot_heat, k, at) if inside else face_rows(z_in, k, slice(0, width))
            if cy:
                halo, n = (y_above, YP.index(k)) if cy == 1 else (y_below, YM.index(k))
                if inside:
                    plane = shift_lanes(plane, cy, halo, column_lane(n, at, depth))
                else:
                    lane = 0 if cy == 1 else plane.shape[1] - 1
                    plane = shift_lanes(plane, cy, yz[cy][0 if cz == 1 else 1], lane)
            if cx:
                plane = shift_rows(plane, cx)
            if cz == -1 and z == 0:
                if k < FLOW:
                    bounced = cot_flow[OPPOSITE[k], 0]
                else:
                    bounced = -cot_heat[OPPOSITE[k - FLOW], 0]
                plane = jnp.where(base, bounced, plane)
            star.append(plane)
        kind = flags[z]
        flow, heat = collide_back(
            star[:FLOW], star[FLOW:], [ue_in[c, z] for c in range(3)], ratio_in[z], kind == 1, kind == 2
        )
        if z == 0:
            source = jnp.where(base, coupling * cot_plate[0], 0.0)
            heat = [value + source for value in heat]
        for values, buf, rows in ((flow, flow_buf, rows_flow), (heat, heat_buf, rows_heat)):
            for q, value in enumerate(values):
                buf[q, z] = value
                rows[q, z : z + 1, :] = value[0:1, :]
                rows[q, depth + z : depth + z + 1, :] = value[width - 1 : width, :]
        send(flow_buf.at[:, z], out_flow.at[:, z])
        send(heat_buf.at[:, z], out_heat.at[:, z])
    for copy in copies:
        copy.wait()


def finish(nxt, rows_in, kinds, rows_flow, rows_heat, rows_plate, *refs):
    x_in, refs = refs[:nxt], refs[nxt + 3 :]
    out_flow, out_heat, out_plate, above_buf, below_buf, star_buf, flow_buf, heat_buf, plate_buf, sems = refs
    depth, width = out_flow.shape[1], out_flow.shape[2]
    layers = out_plate.shape[0]
    used = above_buf.shape[0]
    above, below = incoming("gx", [r[:used, :] for r in x_in])
    above_buf[...] = above
    below_buf[...] = below
    zero = jnp.zeros((2 * depth, above.shape[1]), jnp.float32)
    star = []
    for k, c in enumerate(DIRECTIONS):
        if c[0] == 0:
            star.append(zero)
            continue
        star_buf[k] = zero
        if c[0] == 1:
            n = XP.index(k) * depth
            star_buf[k, depth:, :] = above_buf[n : n + depth, :]
        else:
            n = XM.index(k) * depth
            star_buf[k, :depth, :] = below_buf[n : n + depth, :]
        star.append(star_buf[k])
    kind = kinds[...]
    flow, heat = collide_back(
        star[:FLOW], star[FLOW:], [rows_in[c] for c in range(3)], rows_in[3], kind == 1, kind == 2
    )
    copies = []
    for values, rows, buf, out in (
        (flow, rows_flow, flow_buf, out_flow),
        (heat, rows_heat, heat_buf, out_heat),
    ):
        for q, value in enumerate(values):
            buf[q] = rows[q] + value
        for side, x in enumerate((0, width - 1)):
            source = buf.at[:, side * depth : (side + 1) * depth, :]
            copies.append(pltpu.make_async_copy(source, out.at[:, :, x, :], sems.at[len(copies)]))
            copies[-1].start()
    n = len(XP) * depth
    for side, (x, beside) in enumerate(((0, below_buf), (width - 1, above_buf))):
        rows = slice(side * layers, (side + 1) * layers)
        plate_buf[side] = rows_plate[rows, :] + diffusion * beside[n : n + layers, :]
        copies.append(pltpu.make_async_copy(plate_buf.at[side], out_plate.at[:, x, :], sems.at[len(copies)]))
        copies[-1].start()
    for copy in copies:
        copy.wait()


def kernel_call(body, outs, spaces, name, cost, out_spaces=None, scratch=(), aliases=None):
    return pl.pallas_call(
        body,
        out_shape=outs,
        in_specs=[pl.BlockSpec(memory_space=space) for space in spaces],
        out_specs=[
            pl.BlockSpec(memory_space=space) for space in (out_spaces or [pltpu.VMEM] * len(outs))
        ],
        scratch_shapes=scratch,
        input_output_aliases=aliases or {},
        compiler_params=pltpu.CompilerParams(vmem_limit_bytes=VMEM_LIMIT),
        cost_estimate=pl.CostEstimate(flops=0, bytes_accessed=cost, transcendentals=0),
        name=name,
    )


def local(pop_flow, pop_heat, flags, nozzle_id, jet_velocity, cot_flow, cot_heat, cot_plate):
    nxt, nyt, nzt = (rounds(lax.axis_size(a)) for a in AXES)
    _, depth, width, length = cot_flow.shape
    layers = cot_plate.shape[0]
    f32 = jnp.float32
    array = lambda *shape: jax.ShapeDtypeStruct(shape, f32)
    vmem, hbm = pltpu.VMEM, pltpu.HBM
    cots = (cot_flow, cot_heat, cot_plate)
    side = padded(len(XM) * depth + layers)

    faces = kernel_call(
        functools.partial(pack_faces, nzt),
        [array((len(ZM) + 1) * width, length)] * nzt,
        [hbm] * 3,
        "faces",
        1 << 20,
        scratch=[pltpu.SemaphoreType.DMA((nzt, len(ZM) + 1))],
    )(*(pltpu.with_memory_space_constraint(c, hbm) for c in cots))
    z_in = [swap(v, gz=t) for t, v in enumerate(faces)]
    columns = kernel_call(
        functools.partial(pack_columns, nyt, nzt),
        [array(width + YPAD[t], length) for t in range(nyt)] + [array(YZ_ROWS, length)] * (nyt * nzt),
        [vmem] * (3 + nzt),
        "columns",
        1 << 18,
    )(*cots, *faces)
    y_in = [swap(v, gy=t) for t, v in enumerate(columns[:nyt])]
    yz_in = [swap(columns[nyt + ty * nzt + tz], gy=ty, gz=tz) for ty in range(nyt) for tz in range(nzt)]
    rows = kernel_call(
        functools.partial(pack_rows, nxt, nyt, nzt),
        [array(side, length)] * nxt,
        [vmem] * (3 + nzt + nyt),
        "rows",
        1 << 18,
    )(*cots, *z_in, *y_in)
    x_in = [swap(v, gx=t) for t, v in enumerate(rows)]
    ue, ratio, row_values, row_kinds = kernel_call(
        prepare,
        [
            array(3, depth, width, length),
            array(depth, width, length),
            array(4, 2 * depth, length),
            jax.ShapeDtypeStruct((2 * depth, length), jnp.int32),
        ],
        [vmem] * (5 + nxt),
        "prepare",
        2 << 20,
    )(pop_flow, pop_heat, flags, nozzle_id, jet_velocity, *rows)
    *grads, rows_flow, rows_heat, rows_plate = kernel_call(
        functools.partial(interior, nyt, nzt),
        [array(*c.shape) for c in cots]
        + [array(FLOW, 2 * depth, length), array(HEAT, 2 * depth, length), array(2 * layers, length)],
        [vmem] * (6 + nzt + nyt + nyt * nzt),
        "interior",
        4 << 20,
        out_spaces=[hbm] * 3 + [vmem] * 3,
        scratch=[pltpu.VMEM(c.shape, f32) for c in cots] + [pltpu.SemaphoreType.DMA((2 * depth + 1,))],
    )(flags, ue, ratio, *cots, *z_in, *y_in, *yz_in)
    return tuple(
        kernel_call(
            functools.partial(finish, nxt),
            [array(*c.shape) for c in cots],
            [vmem] * (5 + nxt) + [hbm] * 3,
            "finish",
            1 << 20,
            out_spaces=[hbm] * 3,
            scratch=[
                pltpu.VMEM((side, length), f32),
                pltpu.VMEM((side, length), f32),
                pltpu.VMEM((FLOW + HEAT, 2 * depth, length), f32),
                pltpu.VMEM((FLOW, 2 * depth, length), f32),
                pltpu.VMEM((HEAT, 2 * depth, length), f32),
                pltpu.VMEM((2, layers, length), f32),
                pltpu.SemaphoreType.DMA((6,)),
            ],
            aliases={5 + nxt + i: i for i in range(3)},
        )(row_values, row_kinds, rows_flow, rows_heat, rows_plate, *x_in, *grads)
    )


def solution(mesh):
    return jax.shard_map(
        local,
        mesh=mesh,
        in_specs=(
            P(None, "gz", "gx", "gy"),
            P(None, "gz", "gx", "gy"),
            P("gz", "gx", "gy"),
            P("gx", "gy"),
            P(),
            P(None, "gz", "gx", "gy"),
            P(None, "gz", "gx", "gy"),
            P("gz", "gx", "gy"),
        ),
        out_specs=(P(None, "gz", "gx", "gy"), P(None, "gz", "gx", "gy"), P("gz", "gx", "gy")),
        check_vma=False,
    )
```

```python
import functools

import jax
import jax.numpy as jnp
from jax import lax
from jax.experimental import pallas as pl
from jax.experimental.pallas import tpu as pltpu
from jax.sharding import PartitionSpec as P

VELOCITY = (
    (0, 0, 0),
    (1, 0, 0),
    (-1, 0, 0),
    (0, 1, 0),
    (0, -1, 0),
    (0, 0, 1),
    (0, 0, -1),
    (1, 1, 0),
    (-1, -1, 0),
    (1, -1, 0),
    (-1, 1, 0),
    (1, 0, 1),
    (-1, 0, -1),
    (1, 0, -1),
    (-1, 0, 1),
    (0, 1, 1),
    (0, -1, -1),
    (0, 1, -1),
    (0, -1, 1),
)
OPPOSITE = tuple((VELOCITY.index((-a, -b, -c)) for a, b, c in VELOCITY))
WEIGHTS_FLOW = (1.0 / 3.0,) + (1.0 / 18.0,) * 6 + (1.0 / 36.0,) * 12
WEIGHTS_HEAT = (0.25,) + (0.125,) * 6
FLOW = 19
HEAT = 7
DIRECTIONS = VELOCITY + VELOCITY[:HEAT]
tau_flow = 0.8
tau_heat = 0.9
diffusion = 0.12
coupling = 0.3

AXES = ("gx", "gy", "gz")
COMPONENT = {"gx": 0, "gy": 1, "gz": 2}
VMEM_LIMIT = 8 << 20
YZ_ROWS = 48
YPAD = (0, 0)


def moving(component, sign):
    return [k for k, c in enumerate(DIRECTIONS) if c[component] == sign]


XP, XM = moving(0, 1), moving(0, -1)
YP, YM = moving(1, 1), moving(1, -1)
ZP, ZM = moving(2, 1), moving(2, -1)


def rounds(axis):
    if lax.axis_size(axis) == 2:
        return 1
    return 3 if axis == "gx" else 2


def partner(axis, i, turn):
    period = 3 if axis == "gx" else 2
    if i % period == turn:
        return i + 1
    return i - 1 if (i - 1) % period == turn else -1


def swap(value, **turns):
    sizes = [lax.axis_size(name) for name in AXES]
    flat = lambda p: (p[0] * sizes[1] + p[1]) * sizes[2] + p[2]
    pairs = []
    for a in range(sizes[0]):
        for b in range(sizes[1]):
            for c in range(sizes[2]):
                here = [a, b, c]
                there = [a, b, c]
                for axis, turn in turns.items():
                    at = AXES.index(axis)
                    i = here[at]
                    there[at] = partner(axis, i, turn)
                if not all(0 <= t < n for t, n in zip(there, sizes)):
                    there = [a, sizes[1] - 1 - b if "gy" in turns else b ^ 1, c]
                pairs.append((flat(here), flat(there)))
    return lax.ppermute(value, AXES, pairs)


def place(axis):
    i = lax.axis_index(axis)
    period = 3 if axis == "gx" else 2
    return lax.rem(i, period), lax.rem(i + period - 1, period), i < lax.axis_size(axis) - 1, i > 0


def outgoing(axis, turn, to_higher, to_lower):
    return jnp.where(place(axis)[0] == turn, to_higher, to_lower)


def incoming(axis, turns):
    first, second, higher, lower = place(axis)

    def pick(turn, there):
        value = turns[0]
        for t in range(1, len(turns)):
            value = jnp.where(turn == t, turns[t], value)
        return jnp.where(there, value, jnp.zeros_like(value))

    return pick(first, higher), pick(second, lower)


def slab(cot_flow, cot_heat, k, z):
    return cot_flow[k, z] if k < FLOW else cot_heat[k - FLOW, z]


def row_of(cot_flow, cot_heat, k, z, x):
    return cot_flow[k, z, x : x + 1, :] if k < FLOW else cot_heat[k - FLOW, z, x : x + 1, :]


def padded(rows):
    return -(-rows // 8) * 8


def turned(plane, by):
    by %= plane.shape[1]
    return pltpu.roll(plane, by, 1) if by else plane


def column_lane(n, z, depth):
    return n * depth + z


def plate_lane(l, depth):
    return column_lane(len(YM), 0, depth) + l


def shift_lanes(plane, sign, halo, lane):
    y = lax.broadcasted_iota(jnp.int32, plane.shape, 1)
    edge = plane.shape[1] - 1 if sign == 1 else 0
    return jnp.where(y == edge, turned(halo, edge - lane), turned(plane, -sign))


def shift_rows(plane, sign):
    width = plane.shape[0]
    x = lax.broadcasted_iota(jnp.int32, plane.shape, 0)
    edge = width - 1 if sign == 1 else 0
    return jnp.where(x == edge, 0.0, pltpu.roll(plane, -sign % width, 0))


def pack_faces(nzt, cot_flow, cot_heat, cot_plate, *refs):
    outs, sems = refs[:nzt], refs[nzt]
    depth, width = cot_flow.shape[1], cot_flow.shape[2]
    layers = cot_plate.shape[0]
    copies = []
    for turn in range(nzt):
        up = place("gz")[0] == turn
        z = jnp.where(up, depth - 1, 0)
        sources = []
        for hi, lo in zip(ZM, ZP):
            ref, skip = (cot_flow, 0) if hi < FLOW else (cot_heat, FLOW)
            sources.append(ref.at[jnp.where(up, hi - skip, lo - skip), z])
        sources.append(cot_plate.at[jnp.where(up, layers - 1, 0)])
        for n, source in enumerate(sources):
            target = outs[turn].at[n * width : (n + 1) * width, :]
            copies.append(pltpu.make_async_copy(source, target, sems.at[turn, n]))
            copies[-1].start()
    for copy in copies:
        copy.wait()


def pack_columns(nyt, nzt, cot_flow, cot_heat, cot_plate, *refs):
    outs, yz_outs = refs[-nyt * (nzt + 1) : -nyt * nzt], refs[-nyt * nzt :]
    depth, width, length = cot_flow.shape[1:]
    layers = cot_plate.shape[0]
    y = lax.broadcasted_iota(jnp.int32, (width, length), 1)

    def put(packed, plane, source, lane):
        return jnp.where(y == lane, turned(plane, lane - source), packed)

    packs = []
    for side, source in ((YM, length - 1), (YP, 0)):
        packed = jnp.zeros((width, length), jnp.float32)
        for n, k in enumerate(side):
            for z in range(depth):
                packed = put(
                    packed, slab(cot_flow, cot_heat, k, z), source, column_lane(n, z, depth)
                )
        for l in range(layers):
            packed = put(packed, cot_plate[l], source, plate_lane(l, depth))
        packs.append(packed)
    for turn in range(nyt):
        outs[turn][:width, :] = outgoing("gy", turn, packs[0], packs[1])
        if outs[turn].shape[0] > width:
            outs[turn][width:, :] = jnp.zeros((outs[turn].shape[0] - width, length), jnp.float32)

    def plane(cy, cz):
        k = DIRECTIONS.index((0, cy, cz))
        return slab(cot_flow, cot_heat, k, depth - 1 if cz == -1 else 0)

    for ty in range(nyt):
        for tz in range(nzt):
            out = yz_outs[ty * nzt + tz]
            out[:width, :] = outgoing(
                "gy",
                ty,
                outgoing("gz", tz, plane(-1, -1), plane(-1, 1)),
                outgoing("gz", tz, plane(1, -1), plane(1, 1)),
            )
            if out.shape[0] > width:
                out[width:, :] = jnp.zeros((out.shape[0] - width, length), jnp.float32)


def face_rows(z_in, k, rows):
    up = DIRECTIONS[k][2] == 1
    at = (ZP if up else ZM).index(k) * ((z_in[0].shape[0]) // (len(ZP) + 1))
    above, below = incoming("gz", [r[at + rows.start : at + rows.stop, :] for r in z_in])
    return above if up else below


def pack_rows(nxt, nyt, nzt, cot_flow, cot_heat, cot_plate, *refs):
    z_in, y_in, outs = refs[:nzt], refs[nzt : nzt + nyt], refs[-nxt:]
    depth, width, length = cot_flow.shape[1:]
    layers = cot_plate.shape[0]
    y_above, y_below = incoming("gy", [r[:width, :] for r in y_in])

    def row(k, z, x):
        _, cy, cz = DIRECTIONS[k]
        if 0 <= z + cz < depth:
            value = row_of(cot_flow, cot_heat, k, z + cz, x)
        else:
            value = face_rows(z_in, k, slice(x, x + 1))
        if cy == 0:
            return value
        halo, n = (y_above, YP.index(k)) if cy == 1 else (y_below, YM.index(k))
        return shift_lanes(value, cy, halo[x : x + 1, :], column_lane(n, z, depth))

    used = len(XM) * depth + layers
    for turn in range(nxt):
        if used < outs[turn].shape[0]:
            outs[turn][used:, :] = jnp.zeros((outs[turn].shape[0] - used, length), jnp.float32)
    for n, (hi, lo) in enumerate(zip(XM, XP)):
        for z in range(depth):
            r = n * depth + z
            to_higher, to_lower = row(hi, z, width - 1), row(lo, z, 0)
            for turn in range(nxt):
                outs[turn][r : r + 1, :] = outgoing("gx", turn, to_higher, to_lower)
    for l in range(layers):
        r = len(XM) * depth + l
        for turn in range(nxt):
            outs[turn][r : r + 1, :] = outgoing(
                "gx", turn, cot_plate[l, width - 1 : width, :], cot_plate[l, 0:1, :]
            )


def prepare(pop_flow, pop_heat, flags, nozzle, jet_velocity, *refs):
    ue_out, ratio_out, rows_out, kinds_out = refs[-4:]
    depth, width = flags.shape[:2]
    which = nozzle[...]
    table = jet_velocity[...]
    fill = jnp.zeros((3, which.shape[1] - table.shape[1]), jnp.float32)
    table = jnp.concatenate([table, fill], axis=1)
    jets = [
        jnp.concatenate(
            [
                jnp.take_along_axis(
                    jnp.broadcast_to(table[c : c + 1, :], (8, which.shape[1])), which[x : x + 8, :], axis=1
                )
                for x in range(0, width, 8)
            ],
            axis=0,
        )
        for c in range(3)
    ]
    for z in range(depth):
        inlet = flags[z] == 2
        pops = [pop_flow[q, z] for q in range(FLOW)]
        rho = sum(pops[1:], pops[0])
        inverse = 1.0 / rho
        values = []
        for c in range(3):
            plus = [pops[q] for q in range(FLOW) if VELOCITY[q][c] == 1]
            minus = [pops[q] for q in range(FLOW) if VELOCITY[q][c] == -1]
            total = sum(plus[1:], plus[0]) - sum(minus[1:], minus[0])
            values.append(jnp.where(inlet, jets[c], total * inverse))
            ue_out[c, z] = values[c]
        heat = [pop_heat[q, z] for q in range(HEAT)]
        values.append(sum(heat[1:], heat[0]) * inverse)
        ratio_out[z] = values[3]
        for side, x in enumerate((0, width - 1)):
            r = side * depth + z
            for c in range(4):
                rows_out[c, r : r + 1, :] = values[c][x : x + 1, :]
            kinds_out[r : r + 1, :] = flags[z, x : x + 1, :]


def collide_back(s, t, ue, ratio, wall, inlet):
    add = lambda a, b: b if a is None else a + b
    zero_moment = WEIGHTS_FLOW[0] * s[0]
    first = [None] * 3
    second = {}
    for group, weight in ((range(1, 7), WEIGHTS_FLOW[1]), (range(7, 19), WEIGHTS_FLOW[7])):
        odd = [None] * 3
        even = {}
        total = None
        for q in group:
            o = OPPOSITE[q]
            if o < q:
                continue
            c = VELOCITY[q]
            plus, minus = s[q] + s[o], s[q] - s[o]
            total = add(total, plus)
            for i in range(3):
                if c[i]:
                    odd[i] = add(odd[i], minus if c[i] == 1 else -minus)
                for j in range(i, 3):
                    if c[i] * c[j]:
                        even[i, j] = add(even.get((i, j)), plus if c[i] * c[j] == 1 else -plus)
        zero_moment = zero_moment + weight * total
        for i in range(3):
            first[i] = add(first[i], weight * odd[i])
        for key, value in even.items():
            second[key] = add(second.get(key), weight * value)
    heat_first = [WEIGHTS_HEAT[1] * (t[2 * c + 1] - t[2 * c + 2]) for c in range(3)]
    heat_zero = WEIGHTS_HEAT[0] * t[0] + WEIGHTS_HEAT[1] * (
        (t[1] + t[2]) + (t[3] + t[4]) + (t[5] + t[6])
    )
    dot = lambda a, b: a[0] * b[0] + a[1] * b[1] + a[2] * b[2]
    bent = [sum(second[min(i, j), max(i, j)] * ue[j] for j in range(3)) for i in range(3)]
    gain = zero_moment * (1.0 - 1.5 * dot(ue, ue)) + 3.0 * dot(first, ue) + 4.5 * dot(bent, ue)
    pull = [
        (3.0 / tau_flow) * (first[i] + 3.0 * bent[i] - ue[i] * zero_moment)
        + (4.0 / tau_heat) * ratio * heat_first[i]
        for i in range(3)
    ]
    common = jnp.where(inlet, gain, (1.0 / tau_flow) * gain - dot(ue, pull))
    pull = [jnp.where(inlet, 0.0, p) for p in pull]
    keep = jnp.where(inlet, 0.0, 1.0 - 1.0 / tau_flow)
    flow = []
    for q in range(FLOW):
        value = keep * s[q] + common
        for i in range(3):
            if VELOCITY[q][i] == 1:
                value = value + pull[i]
            elif VELOCITY[q][i] == -1:
                value = value - pull[i]
        flow.append(jnp.where(wall, s[OPPOSITE[q]], value))
    heat_common = jnp.where(inlet, 0.0, (1.0 / tau_heat) * (heat_zero + 4.0 * dot(heat_first, ue)))
    heat_keep = jnp.where(inlet, 0.0, 1.0 - 1.0 / tau_heat)
    heat = [
        jnp.where(wall, t[OPPOSITE[q]], heat_keep * t[q] + heat_common) for q in range(HEAT)
    ]
    return flow, heat


def interior(nyt, nzt, flags, ue_in, ratio_in, cot_flow, cot_heat, cot_plate, *refs):
    z_in, y_in, yz_in = refs[:nzt], refs[nzt : nzt + nyt], refs[nzt + nyt : nzt + nyt + nyt * nzt]
    out_flow, out_heat, out_plate, rows_flow, rows_heat, rows_plate = refs[-10:-4]
    flow_buf, heat_buf, plate_buf, sems = refs[-4:]
    depth, width = cot_flow.shape[1], cot_flow.shape[2]
    layers = cot_plate.shape[0]
    base = lax.axis_index("gz") == 0
    y_above, y_below = incoming("gy", [r[:width, :] for r in y_in])
    sides = [incoming("gy", [r[:width, :] for r in yz_in[tz::nzt]]) for tz in range(nzt)]
    yz = {1: incoming("gz", [side[0] for side in sides]), -1: incoming("gz", [side[1] for side in sides])}
    copies = []

    def send(source, target):
        copies.append(pltpu.make_async_copy(source, target, sems.at[len(copies)]))
        copies[-1].start()

    z_above = z_below = None
    z_rows = slice(len(ZP) * width, (len(ZP) + 1) * width)
    z_above, z_below = incoming("gz", [r[z_rows, :] for r in z_in])
    for l in range(layers):
        own = cot_plate[l]
        up = cot_plate[l + 1] if l + 1 < layers else z_above
        down = cot_plate[l - 1] if l > 0 else z_below
        total = up + down + shift_rows(own, 1) + shift_rows(own, -1)
        total = total + shift_lanes(own, 1, y_above, plate_lane(l, depth))
        total = total + shift_lanes(own, -1, y_below, plate_lane(l, depth))
        value = own + diffusion * (total - 6.0 * own)
        if l == 0:
            value = value + jnp.where(base, 0.25 * cot_heat[5, 0] - coupling * own, 0.0)
        plate_buf[l] = value
        rows_plate[l : l + 1, :] = value[0:1, :]
        rows_plate[layers + l : layers + l + 1, :] = value[width - 1 : width, :]
    send(plate_buf, out_plate)

    for z in range(depth):
        star = []
        for k, (cx, cy, cz) in enumerate(DIRECTIONS):
            at = z + cz
            inside = 0 <= at < depth
            plane = slab(cot_flow, cot_heat, k, at) if inside else face_rows(z_in, k, slice(0, width))
            if cy:
                halo, n = (y_above, YP.index(k)) if cy == 1 else (y_below, YM.index(k))
                if inside:
                    plane = shift_lanes(plane, cy, halo, column_lane(n, at, depth))
                else:
                    lane = 0 if cy == 1 else plane.shape[1] - 1
                    plane = shift_lanes(plane, cy, yz[cy][0 if cz == 1 else 1], lane)
            if cx:
                plane = shift_rows(plane, cx)
            if cz == -1 and z == 0:
                if k < FLOW:
                    bounced = cot_flow[OPPOSITE[k], 0]
                else:
                    bounced = -cot_heat[OPPOSITE[k - FLOW], 0]
                plane = jnp.where(base, bounced, plane)
            star.append(plane)
        kind = flags[z]
        flow, heat = collide_back(
            star[:FLOW], star[FLOW:], [ue_in[c, z] for c in range(3)], ratio_in[z], kind == 1, kind == 2
        )
        if z == 0:
            source = jnp.where(base, coupling * cot_plate[0], 0.0)
            heat = [value + source for value in heat]
        for values, buf, rows in ((flow, flow_buf, rows_flow), (heat, heat_buf, rows_heat)):
            for q, value in enumerate(values):
                buf[q, z] = value
                rows[q, z : z + 1, :] = value[0:1, :]
                rows[q, depth + z : depth + z + 1, :] = value[width - 1 : width, :]
        send(flow_buf.at[:, z], out_flow.at[:, z])
        send(heat_buf.at[:, z], out_heat.at[:, z])
    for copy in copies:
        copy.wait()


def finish(nxt, rows_in, kinds, rows_flow, rows_heat, rows_plate, *refs):
    x_in, refs = refs[:nxt], refs[nxt + 3 :]
    out_flow, out_heat, out_plate, above_buf, below_buf, star_buf, flow_buf, heat_buf, plate_buf, sems = refs
    depth, width = out_flow.shape[1], out_flow.shape[2]
    layers = out_plate.shape[0]
    used = above_buf.shape[0]
    above, below = incoming("gx", [r[:used, :] for r in x_in])
    above_buf[...] = above
    below_buf[...] = below
    zero = jnp.zeros((2 * depth, above.shape[1]), jnp.float32)
    star = []
    for k, c in enumerate(DIRECTIONS):
        if c[0] == 0:
            star.append(zero)
            continue
        star_buf[k] = zero
        if c[0] == 1:
            n = XP.index(k) * depth
            star_buf[k, depth:, :] = above_buf[n : n + depth, :]
        else:
            n = XM.index(k) * depth
            star_buf[k, :depth, :] = below_buf[n : n + depth, :]
        star.append(star_buf[k])
    kind = kinds[...]
    flow, heat = collide_back(
        star[:FLOW], star[FLOW:], [rows_in[c] for c in range(3)], rows_in[3], kind == 1, kind == 2
    )
    copies = []
    for values, rows, buf, out in (
        (flow, rows_flow, flow_buf, out_flow),
        (heat, rows_heat, heat_buf, out_heat),
    ):
        for q, value in enumerate(values):
            buf[q] = rows[q] + value
        for side, x in enumerate((0, width - 1)):
            source = buf.at[:, side * depth : (side + 1) * depth, :]
            copies.append(pltpu.make_async_copy(source, out.at[:, :, x, :], sems.at[len(copies)]))
            copies[-1].start()
    n = len(XP) * depth
    for side, (x, beside) in enumerate(((0, below_buf), (width - 1, above_buf))):
        rows = slice(side * layers, (side + 1) * layers)
        plate_buf[side] = rows_plate[rows, :] + diffusion * beside[n : n + layers, :]
        copies.append(pltpu.make_async_copy(plate_buf.at[side], out_plate.at[:, x, :], sems.at[len(copies)]))
        copies[-1].start()
    for copy in copies:
        copy.wait()


def kernel_call(body, outs, spaces, name, cost, out_spaces=None, scratch=(), aliases=None):
    return pl.pallas_call(
        body,
        out_shape=outs,
        in_specs=[pl.BlockSpec(memory_space=space) for space in spaces],
        out_specs=[
            pl.BlockSpec(memory_space=space) for space in (out_spaces or [pltpu.VMEM] * len(outs))
        ],
        scratch_shapes=scratch,
        input_output_aliases=aliases or {},
        compiler_params=pltpu.CompilerParams(vmem_limit_bytes=VMEM_LIMIT),
        cost_estimate=pl.CostEstimate(flops=0, bytes_accessed=cost, transcendentals=0),
        name=name,
    )


def local(pop_flow, pop_heat, flags, nozzle_id, jet_velocity, cot_flow, cot_heat, cot_plate):
    nxt, nyt, nzt = (rounds(a) for a in AXES)
    _, depth, width, length = cot_flow.shape
    layers = cot_plate.shape[0]
    f32 = jnp.float32
    array = lambda *shape: jax.ShapeDtypeStruct(shape, f32)
    vmem, hbm = pltpu.VMEM, pltpu.HBM
    cots = (cot_flow, cot_heat, cot_plate)
    side = padded(len(XM) * depth + layers)

    faces = kernel_call(
        functools.partial(pack_faces, nzt),
        [array((len(ZM) + 1) * width, length)] * nzt,
        [hbm] * 3,
        "faces",
        1 << 20,
        scratch=[pltpu.SemaphoreType.DMA((nzt, len(ZM) + 1))],
    )(*(pltpu.with_memory_space_constraint(c, hbm) for c in cots))
    z_in = [swap(v, gz=t) for t, v in enumerate(faces)]
    columns = kernel_call(
        functools.partial(pack_columns, nyt, nzt),
        [array(width + YPAD[t], length) for t in range(nyt)] + [array(YZ_ROWS, length)] * (nyt * nzt),
        [vmem] * (3 + nzt),
        "columns",
        1 << 18,
    )(*cots, *faces)
    y_in = [swap(v, gy=t) for t, v in enumerate(columns[:nyt])]
    yz_in = [swap(columns[nyt + ty * nzt + tz], gy=ty, gz=tz) for ty in range(nyt) for tz in range(nzt)]
    rows = kernel_call(
        functools.partial(pack_rows, nxt, nyt, nzt),
        [array(side, length)] * nxt,
        [vmem] * (3 + nzt + nyt),
        "rows",
        1 << 18,
    )(*cots, *z_in, *y_in)
    x_in = [swap(v, gx=t) for t, v in enumerate(rows)]
    ue, ratio, row_values, row_kinds = kernel_call(
        prepare,
        [
            array(3, depth, width, length),
            array(depth, width, length),
            array(4, 2 * depth, length),
            jax.ShapeDtypeStruct((2 * depth, length), jnp.int32),
        ],
        [vmem] * (5 + nxt),
        "prepare",
        2 << 20,
    )(pop_flow, pop_heat, flags, nozzle_id, jet_velocity, *rows)
    *grads, rows_flow, rows_heat, rows_plate = kernel_call(
        functools.partial(interior, nyt, nzt),
        [array(*c.shape) for c in cots]
        + [array(FLOW, 2 * depth, length), array(HEAT, 2 * depth, length), array(2 * layers, length)],
        [vmem] * (6 + nzt + nyt + nyt * nzt),
        "interior",
        4 << 20,
        out_spaces=[hbm] * 3 + [vmem] * 3,
        scratch=[pltpu.VMEM(c.shape, f32) for c in cots] + [pltpu.SemaphoreType.DMA((2 * depth + 1,))],
    )(flags, ue, ratio, *cots, *z_in, *y_in, *yz_in)
    return tuple(
        kernel_call(
            functools.partial(finish, nxt),
            [array(*c.shape) for c in cots],
            [vmem] * (5 + nxt) + [hbm] * 3,
            "finish",
            1 << 20,
            out_spaces=[hbm] * 3,
            scratch=[
                pltpu.VMEM((side, length), f32),
                pltpu.VMEM((side, length), f32),
                pltpu.VMEM((FLOW + HEAT, 2 * depth, length), f32),
                pltpu.VMEM((FLOW, 2 * depth, length), f32),
                pltpu.VMEM((HEAT, 2 * depth, length), f32),
                pltpu.VMEM((2, layers, length), f32),
                pltpu.SemaphoreType.DMA((6,)),
            ],
            aliases={5 + nxt + i: i for i in range(3)},
        )(row_values, row_kinds, rows_flow, rows_heat, rows_plate, *x_in, *grads)
    )


def solution(mesh):
    return jax.shard_map(
        local,
        mesh=mesh,
        in_specs=(
            P(None, "gz", "gx", "gy"),
            P(None, "gz", "gx", "gy"),
            P("gz", "gx", "gy"),
            P("gx", "gy"),
            P(),
            P(None, "gz", "gx", "gy"),
            P(None, "gz", "gx", "gy"),
            P("gz", "gx", "gy"),
        ),
        out_specs=(P(None, "gz", "gx", "gy"), P(None, "gz", "gx", "gy"), P("gz", "gx", "gy")),
        check_vma=False,
    )
```

```python
import functools

import jax
import jax.numpy as jnp
from jax import lax
from jax.experimental import pallas as pl
from jax.experimental.pallas import tpu as pltpu
from jax.sharding import PartitionSpec as P

VELOCITY = (
    (0, 0, 0),
    (1, 0, 0),
    (-1, 0, 0),
    (0, 1, 0),
    (0, -1, 0),
    (0, 0, 1),
    (0, 0, -1),
    (1, 1, 0),
    (-1, -1, 0),
    (1, -1, 0),
    (-1, 1, 0),
    (1, 0, 1),
    (-1, 0, -1),
    (1, 0, -1),
    (-1, 0, 1),
    (0, 1, 1),
    (0, -1, -1),
    (0, 1, -1),
    (0, -1, 1),
)
OPPOSITE = tuple((VELOCITY.index((-a, -b, -c)) for a, b, c in VELOCITY))
WEIGHTS_FLOW = (1.0 / 3.0,) + (1.0 / 18.0,) * 6 + (1.0 / 36.0,) * 12
WEIGHTS_HEAT = (0.25,) + (0.125,) * 6
FLOW = 19
HEAT = 7
DIRECTIONS = VELOCITY + VELOCITY[:HEAT]
tau_flow = 0.8
tau_heat = 0.9
diffusion = 0.12
coupling = 0.3

AXES = ("gx", "gy", "gz")
COMPONENT = {"gx": 0, "gy": 1, "gz": 2}
VMEM_LIMIT = 8 << 20
YZ_ROWS = 48
YPAD = (0, 0)


def moving(component, sign):
    return [k for k, c in enumerate(DIRECTIONS) if c[component] == sign]


XP, XM = moving(0, 1), moving(0, -1)
YP, YM = moving(1, 1), moving(1, -1)
ZP, ZM = moving(2, 1), moving(2, -1)


def rounds(axis):
    if lax.axis_size(axis) == 2:
        return 1
    return 3 if axis == "gx" else 2


def partner(axis, i, turn):
    period = 3 if axis == "gx" else 2
    if i % period == turn:
        return i + 1
    return i - 1 if (i - 1) % period == turn else -1


def swap(value, **turns):
    sizes = [lax.axis_size(name) for name in AXES]
    flat = lambda p: (p[0] * sizes[1] + p[1]) * sizes[2] + p[2]
    pairs = []
    for a in range(sizes[0]):
        for b in range(sizes[1]):
            for c in range(sizes[2]):
                here = [a, b, c]
                there = [a, b, c]
                for axis, turn in turns.items():
                    at = AXES.index(axis)
                    i = here[at]
                    there[at] = partner(axis, i, turn)
                if not all(0 <= t < n for t, n in zip(there, sizes)):
                    there = [a, sizes[1] - 1 - b if "gy" in turns else b ^ 1, c]
                pairs.append((flat(here), flat(there)))
    return lax.ppermute(value, AXES, pairs)


def place(axis):
    i = lax.axis_index(axis)
    period = 3 if axis == "gx" else 2
    return lax.rem(i, period), lax.rem(i + period - 1, period), i < lax.axis_size(axis) - 1, i > 0


def outgoing(axis, turn, to_higher, to_lower):
    return jnp.where(place(axis)[0] == turn, to_higher, to_lower)


def incoming(axis, turns):
    first, second, higher, lower = place(axis)

    def pick(turn, there):
        value = turns[0]
        for t in range(1, len(turns)):
            value = jnp.where(turn == t, turns[t], value)
        return jnp.where(there, value, jnp.zeros_like(value))

    return pick(first, higher), pick(second, lower)


def slab(cot_flow, cot_heat, k, z):
    return cot_flow[k, z] if k < FLOW else cot_heat[k - FLOW, z]


def row_of(cot_flow, cot_heat, k, z, x):
    return cot_flow[k, z, x : x + 1, :] if k < FLOW else cot_heat[k - FLOW, z, x : x + 1, :]


def padded(rows):
    return -(-rows // 8) * 8


def turned(plane, by):
    by %= plane.shape[1]
    return pltpu.roll(plane, by, 1) if by else plane


def column_lane(n, z, depth):
    return n * depth + z


def plate_lane(l, depth):
    return column_lane(len(YM), 0, depth) + l


def shift_lanes(plane, sign, halo, lane):
    y = lax.broadcasted_iota(jnp.int32, plane.shape, 1)
    edge = plane.shape[1] - 1 if sign == 1 else 0
    return jnp.where(y == edge, turned(halo, edge - lane), turned(plane, -sign))


def shift_rows(plane, sign):
    width = plane.shape[0]
    x = lax.broadcasted_iota(jnp.int32, plane.shape, 0)
    edge = width - 1 if sign == 1 else 0
    return jnp.where(x == edge, 0.0, pltpu.roll(plane, -sign % width, 0))


def pack_faces(nzt, cot_flow, cot_heat, cot_plate, *refs):
    outs, sems = refs[:nzt], refs[nzt]
    depth, width = cot_flow.shape[1], cot_flow.shape[2]
    layers = cot_plate.shape[0]
    copies = []
    for turn in range(nzt):
        up = place("gz")[0] == turn
        z = jnp.where(up, depth - 1, 0)
        sources = []
        for hi, lo in zip(ZM, ZP):
            ref, skip = (cot_flow, 0) if hi < FLOW else (cot_heat, FLOW)
            sources.append(ref.at[jnp.where(up, hi - skip, lo - skip), z])
        sources.append(cot_plate.at[jnp.where(up, layers - 1, 0)])
        for n, source in enumerate(sources):
            target = outs[turn].at[n * width : (n + 1) * width, :]
            copies.append(pltpu.make_async_copy(source, target, sems.at[turn, n]))
            copies[-1].start()
    for copy in copies:
        copy.wait()


def pack_columns(nyt, nzt, cot_flow, cot_heat, cot_plate, *refs):
    outs, yz_outs = refs[-nyt * (nzt + 1) : -nyt * nzt], refs[-nyt * nzt :]
    depth, width, length = cot_flow.shape[1:]
    layers = cot_plate.shape[0]
    y = lax.broadcasted_iota(jnp.int32, (width, length), 1)

    def put(packed, plane, source, lane):
        return jnp.where(y == lane, turned(plane, lane - source), packed)

    packs = []
    for side, source in ((YM, length - 1), (YP, 0)):
        packed = jnp.zeros((width, length), jnp.float32)
        for n, k in enumerate(side):
            for z in range(depth):
                packed = put(
                    packed, slab(cot_flow, cot_heat, k, z), source, column_lane(n, z, depth)
                )
        for l in range(layers):
            packed = put(packed, cot_plate[l], source, plate_lane(l, depth))
        packs.append(packed)
    for turn in range(nyt):
        outs[turn][:width, :] = outgoing("gy", turn, packs[0], packs[1])
        if outs[turn].shape[0] > width:
            outs[turn][width:, :] = jnp.zeros((outs[turn].shape[0] - width, length), jnp.float32)

    def plane(cy, cz):
        k = DIRECTIONS.index((0, cy, cz))
        return slab(cot_flow, cot_heat, k, depth - 1 if cz == -1 else 0)

    for ty in range(nyt):
        for tz in range(nzt):
            out = yz_outs[ty * nzt + tz]
            out[:width, :] = outgoing(
                "gy",
                ty,
                outgoing("gz", tz, plane(-1, -1), plane(-1, 1)),
                outgoing("gz", tz, plane(1, -1), plane(1, 1)),
            )
            if out.shape[0] > width:
                out[width:, :] = jnp.zeros((out.shape[0] - width, length), jnp.float32)


def face_rows(z_in, k, rows):
    up = DIRECTIONS[k][2] == 1
    at = (ZP if up else ZM).index(k) * ((z_in[0].shape[0]) // (len(ZP) + 1))
    above, below = incoming("gz", [r[at + rows.start : at + rows.stop, :] for r in z_in])
    return above if up else below


def pack_rows(nxt, nyt, nzt, cot_flow, cot_heat, cot_plate, *refs):
    z_in, y_in, outs = refs[:nzt], refs[nzt : nzt + nyt], refs[-nxt:]
    depth, width, length = cot_flow.shape[1:]
    layers = cot_plate.shape[0]
    y_above, y_below = incoming("gy", [r[:width, :] for r in y_in])

    def row(k, z, x):
        _, cy, cz = DIRECTIONS[k]
        if 0 <= z + cz < depth:
            value = row_of(cot_flow, cot_heat, k, z + cz, x)
        else:
            value = face_rows(z_in, k, slice(x, x + 1))
        if cy == 0:
            return value
        halo, n = (y_above, YP.index(k)) if cy == 1 else (y_below, YM.index(k))
        return shift_lanes(value, cy, halo[x : x + 1, :], column_lane(n, z, depth))

    used = len(XM) * depth + layers
    for turn in range(nxt):
        if used < outs[turn].shape[0]:
            outs[turn][used:, :] = jnp.zeros((outs[turn].shape[0] - used, length), jnp.float32)
    for n, (hi, lo) in enumerate(zip(XM, XP)):
        for z in range(depth):
            r = n * depth + z
            to_higher, to_lower = row(hi, z, width - 1), row(lo, z, 0)
            for turn in range(nxt):
                outs[turn][r : r + 1, :] = outgoing("gx", turn, to_higher, to_lower)
    for l in range(layers):
        r = len(XM) * depth + l
        for turn in range(nxt):
            outs[turn][r : r + 1, :] = outgoing(
                "gx", turn, cot_plate[l, width - 1 : width, :], cot_plate[l, 0:1, :]
            )


def prepare(pop_flow, pop_heat, flags, nozzle, jet_velocity, *refs):
    ue_out, ratio_out, rows_out, kinds_out = refs[-4:]
    depth, width = flags.shape[:2]
    which = nozzle[...]
    table = jet_velocity[...]
    fill = jnp.zeros((3, which.shape[1] - table.shape[1]), jnp.float32)
    table = jnp.concatenate([table, fill], axis=1)
    jets = [
        jnp.concatenate(
            [
                jnp.take_along_axis(
                    jnp.broadcast_to(table[c : c + 1, :], (8, which.shape[1])), which[x : x + 8, :], axis=1
                )
                for x in range(0, width, 8)
            ],
            axis=0,
        )
        for c in range(3)
    ]
    for z in range(depth):
        inlet = flags[z] == 2
        pops = [pop_flow[q, z] for q in range(FLOW)]
        rho = sum(pops[1:], pops[0])
        inverse = 1.0 / rho
        values = []
        for c in range(3):
            plus = [pops[q] for q in range(FLOW) if VELOCITY[q][c] == 1]
            minus = [pops[q] for q in range(FLOW) if VELOCITY[q][c] == -1]
            total = sum(plus[1:], plus[0]) - sum(minus[1:], minus[0])
            values.append(jnp.where(inlet, jets[c], total * inverse))
            ue_out[c, z] = values[c]
        heat = [pop_heat[q, z] for q in range(HEAT)]
        values.append(sum(heat[1:], heat[0]) * inverse)
        ratio_out[z] = values[3]
        for side, x in enumerate((0, width - 1)):
            r = side * depth + z
            for c in range(4):
                rows_out[c, r : r + 1, :] = values[c][x : x + 1, :]
            kinds_out[r : r + 1, :] = flags[z, x : x + 1, :]


def collide_back(s, t, ue, ratio, wall, inlet):
    add = lambda a, b: b if a is None else a + b
    zero_moment = WEIGHTS_FLOW[0] * s[0]
    first = [None] * 3
    second = {}
    for group, weight in ((range(1, 7), WEIGHTS_FLOW[1]), (range(7, 19), WEIGHTS_FLOW[7])):
        odd = [None] * 3
        even = {}
        total = None
        for q in group:
            o = OPPOSITE[q]
            if o < q:
                continue
            c = VELOCITY[q]
            plus, minus = s[q] + s[o], s[q] - s[o]
            total = add(total, plus)
            for i in range(3):
                if c[i]:
                    odd[i] = add(odd[i], minus if c[i] == 1 else -minus)
                for j in range(i, 3):
                    if c[i] * c[j]:
                        even[i, j] = add(even.get((i, j)), plus if c[i] * c[j] == 1 else -plus)
        zero_moment = zero_moment + weight * total
        for i in range(3):
            first[i] = add(first[i], weight * odd[i])
        for key, value in even.items():
            second[key] = add(second.get(key), weight * value)
    heat_first = [WEIGHTS_HEAT[1] * (t[2 * c + 1] - t[2 * c + 2]) for c in range(3)]
    heat_zero = WEIGHTS_HEAT[0] * t[0] + WEIGHTS_HEAT[1] * (
        (t[1] + t[2]) + (t[3] + t[4]) + (t[5] + t[6])
    )
    dot = lambda a, b: a[0] * b[0] + a[1] * b[1] + a[2] * b[2]
    bent = [sum(second[min(i, j), max(i, j)] * ue[j] for j in range(3)) for i in range(3)]
    gain = zero_moment * (1.0 - 1.5 * dot(ue, ue)) + 3.0 * dot(first, ue) + 4.5 * dot(bent, ue)
    pull = [
        (3.0 / tau_flow) * (first[i] + 3.0 * bent[i] - ue[i] * zero_moment)
        + (4.0 / tau_heat) * ratio * heat_first[i]
        for i in range(3)
    ]
    common = jnp.where(inlet, gain, (1.0 / tau_flow) * gain - dot(ue, pull))
    pull = [jnp.where(inlet, 0.0, p) for p in pull]
    keep = jnp.where(inlet, 0.0, 1.0 - 1.0 / tau_flow)
    flow = []
    for q in range(FLOW):
        value = keep * s[q] + common
        for i in range(3):
            if VELOCITY[q][i] == 1:
                value = value + pull[i]
            elif VELOCITY[q][i] == -1:
                value = value - pull[i]
        flow.append(jnp.where(wall, s[OPPOSITE[q]], value))
    heat_common = jnp.where(inlet, 0.0, (1.0 / tau_heat) * (heat_zero + 4.0 * dot(heat_first, ue)))
    heat_keep = jnp.where(inlet, 0.0, 1.0 - 1.0 / tau_heat)
    heat = [
        jnp.where(wall, t[OPPOSITE[q]], heat_keep * t[q] + heat_common) for q in range(HEAT)
    ]
    return flow, heat


def interior(nyt, nzt, flags, ue_in, ratio_in, cot_flow, cot_heat, cot_plate, *refs):
    z_in, y_in, yz_in = refs[:nzt], refs[nzt : nzt + nyt], refs[nzt + nyt : nzt + nyt + nyt * nzt]
    out_flow, out_heat, out_plate, rows_flow, rows_heat, rows_plate = refs[-10:-4]
    flow_buf, heat_buf, plate_buf, sems = refs[-4:]
    depth, width = cot_flow.shape[1], cot_flow.shape[2]
    layers = cot_plate.shape[0]
    base = lax.axis_index("gz") == 0
    y_above, y_below = incoming("gy", [r[:width, :] for r in y_in])
    sides = [incoming("gy", [r[:width, :] for r in yz_in[tz::nzt]]) for tz in range(nzt)]
    yz = {1: incoming("gz", [side[0] for side in sides]), -1: incoming("gz", [side[1] for side in sides])}
    copies = []

    def send(source, target):
        copies.append(pltpu.make_async_copy(source, target, sems.at[len(copies)]))
        copies[-1].start()

    z_above = z_below = None
    z_rows = slice(len(ZP) * width, (len(ZP) + 1) * width)
    z_above, z_below = incoming("gz", [r[z_rows, :] for r in z_in])
    for l in range(layers):
        own = cot_plate[l]
        up = cot_plate[l + 1] if l + 1 < layers else z_above
        down = cot_plate[l - 1] if l > 0 else z_below
        total = up + down + shift_rows(own, 1) + shift_rows(own, -1)
        total = total + shift_lanes(own, 1, y_above, plate_lane(l, depth))
        total = total + shift_lanes(own, -1, y_below, plate_lane(l, depth))
        value = own + diffusion * (total - 6.0 * own)
        if l == 0:
            value = value + jnp.where(base, 0.25 * cot_heat[5, 0] - coupling * own, 0.0)
        plate_buf[l] = value
        rows_plate[l : l + 1, :] = value[0:1, :]
        rows_plate[layers + l : layers + l + 1, :] = value[width - 1 : width, :]
    send(plate_buf, out_plate)

    for z in range(depth):
        star = []
        for k, (cx, cy, cz) in enumerate(DIRECTIONS):
            at = z + cz
            inside = 0 <= at < depth
            plane = slab(cot_flow, cot_heat, k, at) if inside else face_rows(z_in, k, slice(0, width))
            if cy:
                halo, n = (y_above, YP.index(k)) if cy == 1 else (y_below, YM.index(k))
                if inside:
                    plane = shift_lanes(plane, cy, halo, column_lane(n, at, depth))
                else:
                    lane = 0 if cy == 1 else plane.shape[1] - 1
                    plane = shift_lanes(plane, cy, yz[cy][0 if cz == 1 else 1], lane)
            if cx:
                plane = shift_rows(plane, cx)
            if cz == -1 and z == 0:
                if k < FLOW:
                    bounced = cot_flow[OPPOSITE[k], 0]
                else:
                    bounced = -cot_heat[OPPOSITE[k - FLOW], 0]
                plane = jnp.where(base, bounced, plane)
            star.append(plane)
        kind = flags[z]
        flow, heat = collide_back(
            star[:FLOW], star[FLOW:], [ue_in[c, z] for c in range(3)], ratio_in[z], kind == 1, kind == 2
        )
        if z == 0:
            source = jnp.where(base, coupling * cot_plate[0], 0.0)
            heat = [value + source for value in heat]
        for values, buf, rows in ((flow, flow_buf, rows_flow), (heat, heat_buf, rows_heat)):
            for q, value in enumerate(values):
                buf[q, z] = value
                rows[q, z : z + 1, :] = value[0:1, :]
                rows[q, depth + z : depth + z + 1, :] = value[width - 1 : width, :]
        send(flow_buf.at[:, z], out_flow.at[:, z])
        send(heat_buf.at[:, z], out_heat.at[:, z])
    for copy in copies:
        copy.wait()


def finish(nxt, rows_in, kinds, rows_flow, rows_heat, rows_plate, *refs):
    x_in, refs = refs[:nxt], refs[nxt + 3 :]
    out_flow, out_heat, out_plate, above_buf, below_buf, star_buf, flow_buf, heat_buf, plate_buf, sems = refs
    depth, width = out_flow.shape[1], out_flow.shape[2]
    layers = out_plate.shape[0]
    used = above_buf.shape[0]
    above, below = incoming("gx", [r[:used, :] for r in x_in])
    above_buf[...] = above
    below_buf[...] = below
    zero = jnp.zeros((2 * depth, above.shape[1]), jnp.float32)
    star = []
    for k, c in enumerate(DIRECTIONS):
        if c[0] == 0:
            star.append(zero)
            continue
        star_buf[k] = zero
        if c[0] == 1:
            n = XP.index(k) * depth
            star_buf[k, depth:, :] = above_buf[n : n + depth, :]
        else:
            n = XM.index(k) * depth
            star_buf[k, :depth, :] = below_buf[n : n + depth, :]
        star.append(star_buf[k])
    kind = kinds[...]
    flow, heat = collide_back(
        star[:FLOW], star[FLOW:], [rows_in[c] for c in range(3)], rows_in[3], kind == 1, kind == 2
    )
    copies = []
    for values, rows, buf, out in (
        (flow, rows_flow, flow_buf, out_flow),
        (heat, rows_heat, heat_buf, out_heat),
    ):
        for q, value in enumerate(values):
            buf[q] = rows[q] + value
        for side, x in enumerate((0, width - 1)):
            source = buf.at[:, side * depth : (side + 1) * depth, :]
            copies.append(pltpu.make_async_copy(source, out.at[:, :, x, :], sems.at[len(copies)]))
            copies[-1].start()
    n = len(XP) * depth
    for side, (x, beside) in enumerate(((0, below_buf), (width - 1, above_buf))):
        rows = slice(side * layers, (side + 1) * layers)
        plate_buf[side] = rows_plate[rows, :] + diffusion * beside[n : n + layers, :]
        copies.append(pltpu.make_async_copy(plate_buf.at[side], out_plate.at[:, x, :], sems.at[len(copies)]))
        copies[-1].start()
    for copy in copies:
        copy.wait()


def kernel_call(body, outs, spaces, name, cost, out_spaces=None, scratch=(), aliases=None):
    return pl.pallas_call(
        body,
        out_shape=outs,
        in_specs=[pl.BlockSpec(memory_space=space) for space in spaces],
        out_specs=[
            pl.BlockSpec(memory_space=space) for space in (out_spaces or [pltpu.VMEM] * len(outs))
        ],
        scratch_shapes=scratch,
        input_output_aliases=aliases or {},
        compiler_params=pltpu.CompilerParams(vmem_limit_bytes=VMEM_LIMIT),
        cost_estimate=pl.CostEstimate(flops=0, bytes_accessed=cost, transcendentals=0),
        name=name,
    )


def local(pop_flow, pop_heat, flags, nozzle_id, jet_velocity, cot_flow, cot_heat, cot_plate):
    nxt, nyt, nzt = (rounds(a) for a in AXES)
    _, depth, width, length = cot_flow.shape
    layers = cot_plate.shape[0]
    f32 = jnp.float32
    array = lambda *shape: jax.ShapeDtypeStruct(shape, f32)
    vmem, hbm = pltpu.VMEM, pltpu.HBM
    cots = (cot_flow, cot_heat, cot_plate)
    side = padded(len(XM) * depth + layers)

    faces = kernel_call(
        functools.partial(pack_faces, nzt),
        [array((len(ZM) + 1) * width, length)] * nzt,
        [hbm] * 3,
        "faces",
        1 << 20,
        scratch=[pltpu.SemaphoreType.DMA((nzt, len(ZM) + 1))],
    )(*(pltpu.with_memory_space_constraint(c, hbm) for c in cots))
    z_in = [swap(v, gz=t) for t, v in enumerate(faces)]
    columns = kernel_call(
        functools.partial(pack_columns, nyt, nzt),
        [array(width + YPAD[t], length) for t in range(nyt)] + [array(YZ_ROWS + 8 * ty, length) for ty in range(nyt) for tz in range(nzt)],
        [vmem] * (3 + nzt),
        "columns",
        1 << 18,
    )(*cots, *faces)
    y_in = [swap(v, gy=t) for t, v in enumerate(columns[:nyt])]
    yz_in = [swap(columns[nyt + ty * nzt + tz], gy=ty, gz=tz) for ty in range(nyt) for tz in range(nzt)]
    rows = kernel_call(
        functools.partial(pack_rows, nxt, nyt, nzt),
        [array(side, length)] * nxt,
        [vmem] * (3 + nzt + nyt),
        "rows",
        1 << 18,
    )(*cots, *z_in, *y_in)
    x_in = [swap(v, gx=t) for t, v in enumerate(rows)]
    ue, ratio, row_values, row_kinds = kernel_call(
        prepare,
        [
            array(3, depth, width, length),
            array(depth, width, length),
            array(4, 2 * depth, length),
            jax.ShapeDtypeStruct((2 * depth, length), jnp.int32),
        ],
        [vmem] * (5 + nxt),
        "prepare",
        2 << 20,
    )(pop_flow, pop_heat, flags, nozzle_id, jet_velocity, *rows)
    *grads, rows_flow, rows_heat, rows_plate = kernel_call(
        functools.partial(interior, nyt, nzt),
        [array(*c.shape) for c in cots]
        + [array(FLOW, 2 * depth, length), array(HEAT, 2 * depth, length), array(2 * layers, length)],
        [vmem] * (6 + nzt + nyt + nyt * nzt),
        "interior",
        4 << 20,
        out_spaces=[hbm] * 3 + [vmem] * 3,
        scratch=[pltpu.VMEM(c.shape, f32) for c in cots] + [pltpu.SemaphoreType.DMA((2 * depth + 1,))],
    )(flags, ue, ratio, *cots, *z_in, *y_in, *yz_in)
    return tuple(
        kernel_call(
            functools.partial(finish, nxt),
            [array(*c.shape) for c in cots],
            [vmem] * (5 + nxt) + [hbm] * 3,
            "finish",
            1 << 20,
            out_spaces=[hbm] * 3,
            scratch=[
                pltpu.VMEM((side, length), f32),
                pltpu.VMEM((side, length), f32),
                pltpu.VMEM((FLOW + HEAT, 2 * depth, length), f32),
                pltpu.VMEM((FLOW, 2 * depth, length), f32),
                pltpu.VMEM((HEAT, 2 * depth, length), f32),
                pltpu.VMEM((2, layers, length), f32),
                pltpu.SemaphoreType.DMA((6,)),
            ],
            aliases={5 + nxt + i: i for i in range(3)},
        )(row_values, row_kinds, rows_flow, rows_heat, rows_plate, *x_in, *grads)
    )


def solution(mesh):
    return jax.shard_map(
        local,
        mesh=mesh,
        in_specs=(
            P(None, "gz", "gx", "gy"),
            P(None, "gz", "gx", "gy"),
            P("gz", "gx", "gy"),
            P("gx", "gy"),
            P(),
            P(None, "gz", "gx", "gy"),
            P(None, "gz", "gx", "gy"),
            P("gz", "gx", "gy"),
        ),
        out_specs=(P(None, "gz", "gx", "gy"), P(None, "gz", "gx", "gy"), P("gz", "gx", "gy")),
        check_vma=False,
    )
```

```python
import functools

import jax
import jax.numpy as jnp
from jax import lax
from jax.experimental import pallas as pl
from jax.experimental.pallas import tpu as pltpu
from jax.sharding import PartitionSpec as P

VELOCITY = (
    (0, 0, 0),
    (1, 0, 0),
    (-1, 0, 0),
    (0, 1, 0),
    (0, -1, 0),
    (0, 0, 1),
    (0, 0, -1),
    (1, 1, 0),
    (-1, -1, 0),
    (1, -1, 0),
    (-1, 1, 0),
    (1, 0, 1),
    (-1, 0, -1),
    (1, 0, -1),
    (-1, 0, 1),
    (0, 1, 1),
    (0, -1, -1),
    (0, 1, -1),
    (0, -1, 1),
)
OPPOSITE = tuple((VELOCITY.index((-a, -b, -c)) for a, b, c in VELOCITY))
WEIGHTS_FLOW = (1.0 / 3.0,) + (1.0 / 18.0,) * 6 + (1.0 / 36.0,) * 12
WEIGHTS_HEAT = (0.25,) + (0.125,) * 6
FLOW = 19
HEAT = 7
DIRECTIONS = VELOCITY + VELOCITY[:HEAT]
tau_flow = 0.8
tau_heat = 0.9
diffusion = 0.12
coupling = 0.3

AXES = ("gx", "gy", "gz")
COMPONENT = {"gx": 0, "gy": 1, "gz": 2}
VMEM_LIMIT = 8 << 20
YZ_ROWS = 48
YPAD = (0, 0)


def moving(component, sign):
    return [k for k, c in enumerate(DIRECTIONS) if c[component] == sign]


XP, XM = moving(0, 1), moving(0, -1)
YP, YM = moving(1, 1), moving(1, -1)
ZP, ZM = moving(2, 1), moving(2, -1)


def rounds(axis):
    if lax.axis_size(axis) == 2:
        return 1
    return 3 if axis == "gx" else 2


def partner(axis, i, turn):
    period = 3 if axis == "gx" else 2
    if i % period == turn:
        return i + 1
    return i - 1 if (i - 1) % period == turn else -1


def swap(value, **turns):
    sizes = [lax.axis_size(name) for name in AXES]
    flat = lambda p: (p[0] * sizes[1] + p[1]) * sizes[2] + p[2]
    pairs = []
    for a in range(sizes[0]):
        for b in range(sizes[1]):
            for c in range(sizes[2]):
                here = [a, b, c]
                there = [a, b, c]
                for axis, turn in turns.items():
                    at = AXES.index(axis)
                    i = here[at]
                    there[at] = partner(axis, i, turn)
                if not all(0 <= t < n for t, n in zip(there, sizes)):
                    there = [a, sizes[1] - 1 - b if "gy" in turns else b ^ 1, c]
                pairs.append((flat(here), flat(there)))
    return lax.ppermute(value, AXES, pairs)


def place(axis):
    i = lax.axis_index(axis)
    period = 3 if axis == "gx" else 2
    return lax.rem(i, period), lax.rem(i + period - 1, period), i < lax.axis_size(axis) - 1, i > 0


def outgoing(axis, turn, to_higher, to_lower):
    return jnp.where(place(axis)[0] == turn, to_higher, to_lower)


def incoming(axis, turns):
    first, second, higher, lower = place(axis)

    def pick(turn, there):
        value = turns[0]
        for t in range(1, len(turns)):
            value = jnp.where(turn == t, turns[t], value)
        return jnp.where(there, value, jnp.zeros_like(value))

    return pick(first, higher), pick(second, lower)


def slab(cot_flow, cot_heat, k, z):
    return cot_flow[k, z] if k < FLOW else cot_heat[k - FLOW, z]


def row_of(cot_flow, cot_heat, k, z, x):
    return cot_flow[k, z, x : x + 1, :] if k < FLOW else cot_heat[k - FLOW, z, x : x + 1, :]


def padded(rows):
    return -(-rows // 8) * 8


def turned(plane, by):
    by %= plane.shape[1]
    return pltpu.roll(plane, by, 1) if by else plane


def column_lane(n, z, depth):
    return n * depth + z


def plate_lane(l, depth):
    return column_lane(len(YM), 0, depth) + l


def shift_lanes(plane, sign, halo, lane):
    y = lax.broadcasted_iota(jnp.int32, plane.shape, 1)
    edge = plane.shape[1] - 1 if sign == 1 else 0
    return jnp.where(y == edge, turned(halo, edge - lane), turned(plane, -sign))


def shift_rows(plane, sign):
    width = plane.shape[0]
    x = lax.broadcasted_iota(jnp.int32, plane.shape, 0)
    edge = width - 1 if sign == 1 else 0
    return jnp.where(x == edge, 0.0, pltpu.roll(plane, -sign % width, 0))


def pack_faces(nzt, cot_flow, cot_heat, cot_plate, *refs):
    outs, sems = refs[:nzt], refs[nzt]
    depth, width = cot_flow.shape[1], cot_flow.shape[2]
    layers = cot_plate.shape[0]
    copies = []
    for turn in range(nzt):
        up = place("gz")[0] == turn
        z = jnp.where(up, depth - 1, 0)
        sources = []
        for hi, lo in zip(ZM, ZP):
            ref, skip = (cot_flow, 0) if hi < FLOW else (cot_heat, FLOW)
            sources.append(ref.at[jnp.where(up, hi - skip, lo - skip), z])
        sources.append(cot_plate.at[jnp.where(up, layers - 1, 0)])
        for n, source in enumerate(sources):
            target = outs[turn].at[n * width : (n + 1) * width, :]
            copies.append(pltpu.make_async_copy(source, target, sems.at[turn, n]))
            copies[-1].start()
    for copy in copies:
        copy.wait()


def pack_columns(nyt, nzt, cot_flow, cot_heat, cot_plate, *refs):
    outs, yz_outs = refs[-nyt * (nzt + 1) : -nyt * nzt], refs[-nyt * nzt :]
    depth, width, length = cot_flow.shape[1:]
    layers = cot_plate.shape[0]
    y = lax.broadcasted_iota(jnp.int32, (width, length), 1)

    def put(packed, plane, source, lane):
        return jnp.where(y == lane, turned(plane, lane - source), packed)

    packs = []
    for side, source in ((YM, length - 1), (YP, 0)):
        packed = jnp.zeros((width, length), jnp.float32)
        for n, k in enumerate(side):
            for z in range(depth):
                packed = put(
                    packed, slab(cot_flow, cot_heat, k, z), source, column_lane(n, z, depth)
                )
        for l in range(layers):
            packed = put(packed, cot_plate[l], source, plate_lane(l, depth))
        packs.append(packed)
    for turn in range(nyt):
        outs[turn][:width, :] = outgoing("gy", turn, packs[0], packs[1])
        if outs[turn].shape[0] > width:
            outs[turn][width:, :] = jnp.zeros((outs[turn].shape[0] - width, length), jnp.float32)

    def plane(cy, cz):
        k = DIRECTIONS.index((0, cy, cz))
        return slab(cot_flow, cot_heat, k, depth - 1 if cz == -1 else 0)

    for ty in range(nyt):
        for tz in range(nzt):
            out = yz_outs[ty * nzt + tz]
            out[:width, :] = outgoing(
                "gy",
                ty,
                outgoing("gz", tz, plane(-1, -1), plane(-1, 1)),
                outgoing("gz", tz, plane(1, -1), plane(1, 1)),
            )
            if out.shape[0] > width:
                out[width:, :] = jnp.zeros((out.shape[0] - width, length), jnp.float32)


def face_rows(z_in, k, rows):
    up = DIRECTIONS[k][2] == 1
    at = (ZP if up else ZM).index(k) * ((z_in[0].shape[0]) // (len(ZP) + 1))
    above, below = incoming("gz", [r[at + rows.start : at + rows.stop, :] for r in z_in])
    return above if up else below


def pack_rows(nxt, nyt, nzt, cot_flow, cot_heat, cot_plate, *refs):
    z_in, y_in, outs = refs[:nzt], refs[nzt : nzt + nyt], refs[-nxt:]
    depth, width, length = cot_flow.shape[1:]
    layers = cot_plate.shape[0]
    y_above, y_below = incoming("gy", [r[:width, :] for r in y_in])

    def row(k, z, x):
        _, cy, cz = DIRECTIONS[k]
        if 0 <= z + cz < depth:
            value = row_of(cot_flow, cot_heat, k, z + cz, x)
        else:
            value = face_rows(z_in, k, slice(x, x + 1))
        if cy == 0:
            return value
        halo, n = (y_above, YP.index(k)) if cy == 1 else (y_below, YM.index(k))
        return shift_lanes(value, cy, halo[x : x + 1, :], column_lane(n, z, depth))

    used = len(XM) * depth + layers
    for turn in range(nxt):
        if used < outs[turn].shape[0]:
            outs[turn][used:, :] = jnp.zeros((outs[turn].shape[0] - used, length), jnp.float32)
    for n, (hi, lo) in enumerate(zip(XM, XP)):
        for z in range(depth):
            r = n * depth + z
            to_higher, to_lower = row(hi, z, width - 1), row(lo, z, 0)
            for turn in range(nxt):
                outs[turn][r : r + 1, :] = outgoing("gx", turn, to_higher, to_lower)
    for l in range(layers):
        r = len(XM) * depth + l
        for turn in range(nxt):
            outs[turn][r : r + 1, :] = outgoing(
                "gx", turn, cot_plate[l, width - 1 : width, :], cot_plate[l, 0:1, :]
            )


def prepare(pop_flow, pop_heat, flags, nozzle, jet_velocity, *refs):
    ue_out, ratio_out, rows_out, kinds_out = refs[-4:]
    depth, width = flags.shape[:2]
    which = nozzle[...]
    table = jet_velocity[...]
    fill = jnp.zeros((3, which.shape[1] - table.shape[1]), jnp.float32)
    table = jnp.concatenate([table, fill], axis=1)
    jets = [
        jnp.concatenate(
            [
                jnp.take_along_axis(
                    jnp.broadcast_to(table[c : c + 1, :], (8, which.shape[1])), which[x : x + 8, :], axis=1
                )
                for x in range(0, width, 8)
            ],
            axis=0,
        )
        for c in range(3)
    ]
    for z in range(depth):
        inlet = flags[z] == 2
        pops = [pop_flow[q, z] for q in range(FLOW)]
        rho = sum(pops[1:], pops[0])
        inverse = 1.0 / rho
        values = []
        for c in range(3):
            plus = [pops[q] for q in range(FLOW) if VELOCITY[q][c] == 1]
            minus = [pops[q] for q in range(FLOW) if VELOCITY[q][c] == -1]
            total = sum(plus[1:], plus[0]) - sum(minus[1:], minus[0])
            values.append(jnp.where(inlet, jets[c], total * inverse))
            ue_out[c, z] = values[c]
        heat = [pop_heat[q, z] for q in range(HEAT)]
        values.append(sum(heat[1:], heat[0]) * inverse)
        ratio_out[z] = values[3]
        for side, x in enumerate((0, width - 1)):
            r = side * depth + z
            for c in range(4):
                rows_out[c, r : r + 1, :] = values[c][x : x + 1, :]
            kinds_out[r : r + 1, :] = flags[z, x : x + 1, :]


def collide_back(s, t, ue, ratio, wall, inlet):
    add = lambda a, b: b if a is None else a + b
    zero_moment = WEIGHTS_FLOW[0] * s[0]
    first = [None] * 3
    second = {}
    for group, weight in ((range(1, 7), WEIGHTS_FLOW[1]), (range(7, 19), WEIGHTS_FLOW[7])):
        odd = [None] * 3
        even = {}
        total = None
        for q in group:
            o = OPPOSITE[q]
            if o < q:
                continue
            c = VELOCITY[q]
            plus, minus = s[q] + s[o], s[q] - s[o]
            total = add(total, plus)
            for i in range(3):
                if c[i]:
                    odd[i] = add(odd[i], minus if c[i] == 1 else -minus)
                for j in range(i, 3):
                    if c[i] * c[j]:
                        even[i, j] = add(even.get((i, j)), plus if c[i] * c[j] == 1 else -plus)
        zero_moment = zero_moment + weight * total
        for i in range(3):
            first[i] = add(first[i], weight * odd[i])
        for key, value in even.items():
            second[key] = add(second.get(key), weight * value)
    heat_first = [WEIGHTS_HEAT[1] * (t[2 * c + 1] - t[2 * c + 2]) for c in range(3)]
    heat_zero = WEIGHTS_HEAT[0] * t[0] + WEIGHTS_HEAT[1] * (
        (t[1] + t[2]) + (t[3] + t[4]) + (t[5] + t[6])
    )
    dot = lambda a, b: a[0] * b[0] + a[1] * b[1] + a[2] * b[2]
    bent = [sum(second[min(i, j), max(i, j)] * ue[j] for j in range(3)) for i in range(3)]
    gain = zero_moment * (1.0 - 1.5 * dot(ue, ue)) + 3.0 * dot(first, ue) + 4.5 * dot(bent, ue)
    pull = [
        (3.0 / tau_flow) * (first[i] + 3.0 * bent[i] - ue[i] * zero_moment)
        + (4.0 / tau_heat) * ratio * heat_first[i]
        for i in range(3)
    ]
    common = jnp.where(inlet, gain, (1.0 / tau_flow) * gain - dot(ue, pull))
    pull = [jnp.where(inlet, 0.0, p) for p in pull]
    keep = jnp.where(inlet, 0.0, 1.0 - 1.0 / tau_flow)
    flow = []
    for q in range(FLOW):
        value = keep * s[q] + common
        for i in range(3):
            if VELOCITY[q][i] == 1:
                value = value + pull[i]
            elif VELOCITY[q][i] == -1:
                value = value - pull[i]
        flow.append(jnp.where(wall, s[OPPOSITE[q]], value))
    heat_common = jnp.where(inlet, 0.0, (1.0 / tau_heat) * (heat_zero + 4.0 * dot(heat_first, ue)))
    heat_keep = jnp.where(inlet, 0.0, 1.0 - 1.0 / tau_heat)
    heat = [
        jnp.where(wall, t[OPPOSITE[q]], heat_keep * t[q] + heat_common) for q in range(HEAT)
    ]
    return flow, heat


def interior(nyt, nzt, flags, ue_in, ratio_in, cot_flow, cot_heat, cot_plate, *refs):
    z_in, y_in, yz_in = refs[:nzt], refs[nzt : nzt + nyt], refs[nzt + nyt : nzt + nyt + nyt * nzt]
    out_flow, out_heat, out_plate, rows_flow, rows_heat, rows_plate = refs[-10:-4]
    flow_buf, heat_buf, plate_buf, sems = refs[-4:]
    depth, width = cot_flow.shape[1], cot_flow.shape[2]
    layers = cot_plate.shape[0]
    base = lax.axis_index("gz") == 0
    y_above, y_below = incoming("gy", [r[:width, :] for r in y_in])
    sides = [incoming("gy", [r[:width, :] for r in yz_in[tz::nzt]]) for tz in range(nzt)]
    yz = {1: incoming("gz", [side[0] for side in sides]), -1: incoming("gz", [side[1] for side in sides])}
    copies = []

    def send(source, target):
        copies.append(pltpu.make_async_copy(source, target, sems.at[len(copies)]))
        copies[-1].start()

    z_above = z_below = None
    z_rows = slice(len(ZP) * width, (len(ZP) + 1) * width)
    z_above, z_below = incoming("gz", [r[z_rows, :] for r in z_in])
    for l in range(layers):
        own = cot_plate[l]
        up = cot_plate[l + 1] if l + 1 < layers else z_above
        down = cot_plate[l - 1] if l > 0 else z_below
        total = up + down + shift_rows(own, 1) + shift_rows(own, -1)
        total = total + shift_lanes(own, 1, y_above, plate_lane(l, depth))
        total = total + shift_lanes(own, -1, y_below, plate_lane(l, depth))
        value = own + diffusion * (total - 6.0 * own)
        if l == 0:
            value = value + jnp.where(base, 0.25 * cot_heat[5, 0] - coupling * own, 0.0)
        plate_buf[l] = value
        rows_plate[l : l + 1, :] = value[0:1, :]
        rows_plate[layers + l : layers + l + 1, :] = value[width - 1 : width, :]
    send(plate_buf, out_plate)

    for z in range(depth):
        star = []
        for k, (cx, cy, cz) in enumerate(DIRECTIONS):
            at = z + cz
            inside = 0 <= at < depth
            plane = slab(cot_flow, cot_heat, k, at) if inside else face_rows(z_in, k, slice(0, width))
            if cy:
                halo, n = (y_above, YP.index(k)) if cy == 1 else (y_below, YM.index(k))
                if inside:
                    plane = shift_lanes(plane, cy, halo, column_lane(n, at, depth))
                else:
                    lane = 0 if cy == 1 else plane.shape[1] - 1
                    plane = shift_lanes(plane, cy, yz[cy][0 if cz == 1 else 1], lane)
            if cx:
                plane = shift_rows(plane, cx)
            if cz == -1 and z == 0:
                if k < FLOW:
                    bounced = cot_flow[OPPOSITE[k], 0]
                else:
                    bounced = -cot_heat[OPPOSITE[k - FLOW], 0]
                plane = jnp.where(base, bounced, plane)
            star.append(plane)
        kind = flags[z]
        flow, heat = collide_back(
            star[:FLOW], star[FLOW:], [ue_in[c, z] for c in range(3)], ratio_in[z], kind == 1, kind == 2
        )
        if z == 0:
            source = jnp.where(base, coupling * cot_plate[0], 0.0)
            heat = [value + source for value in heat]
        for values, buf, rows in ((flow, flow_buf, rows_flow), (heat, heat_buf, rows_heat)):
            for q, value in enumerate(values):
                buf[q, z] = value
                rows[q, z : z + 1, :] = value[0:1, :]
                rows[q, depth + z : depth + z + 1, :] = value[width - 1 : width, :]
        send(flow_buf.at[:, z], out_flow.at[:, z])
        send(heat_buf.at[:, z], out_heat.at[:, z])
    for copy in copies:
        copy.wait()


def finish(nxt, rows_in, kinds, rows_flow, rows_heat, rows_plate, *refs):
    x_in, refs = refs[:nxt], refs[nxt + 3 :]
    out_flow, out_heat, out_plate, above_buf, below_buf, star_buf, flow_buf, heat_buf, plate_buf, sems = refs
    depth, width = out_flow.shape[1], out_flow.shape[2]
    layers = out_plate.shape[0]
    used = above_buf.shape[0]
    above, below = incoming("gx", [r[:used, :] for r in x_in])
    above_buf[...] = above
    below_buf[...] = below
    copies = []
    n = len(XP) * depth
    for side, (x, beside) in enumerate(((0, below_buf), (width - 1, above_buf))):
        rows = slice(side * layers, (side + 1) * layers)
        plate_buf[side] = rows_plate[rows, :] + diffusion * beside[n : n + layers, :]
        copies.append(pltpu.make_async_copy(plate_buf.at[side], out_plate.at[:, x, :], sems.at[len(copies)]))
        copies[-1].start()
    zero = jnp.zeros((2 * depth, above.shape[1]), jnp.float32)
    star = []
    for k, c in enumerate(DIRECTIONS):
        if c[0] == 0:
            star.append(zero)
            continue
        star_buf[k] = zero
        if c[0] == 1:
            n = XP.index(k) * depth
            star_buf[k, depth:, :] = above_buf[n : n + depth, :]
        else:
            n = XM.index(k) * depth
            star_buf[k, :depth, :] = below_buf[n : n + depth, :]
        star.append(star_buf[k])
    kind = kinds[...]
    flow, heat = collide_back(
        star[:FLOW], star[FLOW:], [rows_in[c] for c in range(3)], rows_in[3], kind == 1, kind == 2
    )
    for values, rows, buf, out in (
        (flow, rows_flow, flow_buf, out_flow),
        (heat, rows_heat, heat_buf, out_heat),
    ):
        for q, value in enumerate(values):
            buf[q] = rows[q] + value
        for side, x in enumerate((0, width - 1)):
            source = buf.at[:, side * depth : (side + 1) * depth, :]
            copies.append(pltpu.make_async_copy(source, out.at[:, :, x, :], sems.at[len(copies)]))
            copies[-1].start()
    for copy in copies:
        copy.wait()


def kernel_call(body, outs, spaces, name, cost, out_spaces=None, scratch=(), aliases=None):
    return pl.pallas_call(
        body,
        out_shape=outs,
        in_specs=[pl.BlockSpec(memory_space=space) for space in spaces],
        out_specs=[
            pl.BlockSpec(memory_space=space) for space in (out_spaces or [pltpu.VMEM] * len(outs))
        ],
        scratch_shapes=scratch,
        input_output_aliases=aliases or {},
        compiler_params=pltpu.CompilerParams(vmem_limit_bytes=VMEM_LIMIT),
        cost_estimate=pl.CostEstimate(flops=0, bytes_accessed=cost, transcendentals=0),
        name=name,
    )


def local(pop_flow, pop_heat, flags, nozzle_id, jet_velocity, cot_flow, cot_heat, cot_plate):
    nxt, nyt, nzt = (rounds(a) for a in AXES)
    _, depth, width, length = cot_flow.shape
    layers = cot_plate.shape[0]
    f32 = jnp.float32
    array = lambda *shape: jax.ShapeDtypeStruct(shape, f32)
    vmem, hbm = pltpu.VMEM, pltpu.HBM
    cots = (cot_flow, cot_heat, cot_plate)
    side = padded(len(XM) * depth + layers)

    faces = kernel_call(
        functools.partial(pack_faces, nzt),
        [array((len(ZM) + 1) * width, length)] * nzt,
        [hbm] * 3,
        "faces",
        1 << 20,
        scratch=[pltpu.SemaphoreType.DMA((nzt, len(ZM) + 1))],
    )(*(pltpu.with_memory_space_constraint(c, hbm) for c in cots))
    z_in = [swap(v, gz=t) for t, v in enumerate(faces)]
    columns = kernel_call(
        functools.partial(pack_columns, nyt, nzt),
        [array(width + YPAD[t], length) for t in range(nyt)] + [array(YZ_ROWS + 8 * ty, length) for ty in range(nyt) for tz in range(nzt)],
        [vmem] * (3 + nzt),
        "columns",
        1 << 18,
    )(*cots, *faces)
    y_in = [swap(v, gy=t) for t, v in enumerate(columns[:nyt])]
    yz_in = [swap(columns[nyt + ty * nzt + tz], gy=ty, gz=tz) for ty in range(nyt) for tz in range(nzt)]
    rows = kernel_call(
        functools.partial(pack_rows, nxt, nyt, nzt),
        [array(side, length)] * nxt,
        [vmem] * (3 + nzt + nyt),
        "rows",
        1 << 18,
    )(*cots, *z_in, *y_in)
    x_in = [swap(v, gx=t) for t, v in enumerate(rows)]
    ue, ratio, row_values, row_kinds = kernel_call(
        prepare,
        [
            array(3, depth, width, length),
            array(depth, width, length),
            array(4, 2 * depth, length),
            jax.ShapeDtypeStruct((2 * depth, length), jnp.int32),
        ],
        [vmem] * (5 + nxt),
        "prepare",
        2 << 20,
    )(pop_flow, pop_heat, flags, nozzle_id, jet_velocity, *rows)
    *grads, rows_flow, rows_heat, rows_plate = kernel_call(
        functools.partial(interior, nyt, nzt),
        [array(*c.shape) for c in cots]
        + [array(FLOW, 2 * depth, length), array(HEAT, 2 * depth, length), array(2 * layers, length)],
        [vmem] * (6 + nzt + nyt + nyt * nzt),
        "interior",
        4 << 20,
        out_spaces=[hbm] * 3 + [vmem] * 3,
        scratch=[pltpu.VMEM(c.shape, f32) for c in cots] + [pltpu.SemaphoreType.DMA((2 * depth + 1,))],
    )(flags, ue, ratio, *cots, *z_in, *y_in, *yz_in)
    return tuple(
        kernel_call(
            functools.partial(finish, nxt),
            [array(*c.shape) for c in cots],
            [vmem] * (5 + nxt) + [hbm] * 3,
            "finish",
            1 << 20,
            out_spaces=[hbm] * 3,
            scratch=[
                pltpu.VMEM((side, length), f32),
                pltpu.VMEM((side, length), f32),
                pltpu.VMEM((FLOW + HEAT, 2 * depth, length), f32),
                pltpu.VMEM((FLOW, 2 * depth, length), f32),
                pltpu.VMEM((HEAT, 2 * depth, length), f32),
                pltpu.VMEM((2, layers, length), f32),
                pltpu.SemaphoreType.DMA((6,)),
            ],
            aliases={5 + nxt + i: i for i in range(3)},
        )(row_values, row_kinds, rows_flow, rows_heat, rows_plate, *x_in, *grads)
    )


def solution(mesh):
    return jax.shard_map(
        local,
        mesh=mesh,
        in_specs=(
            P(None, "gz", "gx", "gy"),
            P(None, "gz", "gx", "gy"),
            P("gz", "gx", "gy"),
            P("gx", "gy"),
            P(),
            P(None, "gz", "gx", "gy"),
            P(None, "gz", "gx", "gy"),
            P("gz", "gx", "gy"),
        ),
        out_specs=(P(None, "gz", "gx", "gy"), P(None, "gz", "gx", "gy"), P("gz", "gx", "gy")),
        check_vma=False,
    )
```
